32 devices in a mesh: dp: 32 (over z, y, x, core).
Axes of the slice: x: 2, y: 2, z: 4, core: 2. Of those that a mesh axis runs over, the one named last changes fastest.
Arguments:
- block_input: bfloat16 [4096, 1088], P('dp'), may hold values from -6 to 6
- out_cotangent: bfloat16 [4096, 1088], P('dp'), may hold values from -6 to 6
- seq_lengths: int32 [32, 4], P('dp'), may hold values from 1 to 64, 128 in all within a row
- w_qkv: bfloat16 [3551232], P('dp'), may hold values from -1 to 1
- w_out: bfloat16 [1183744], P('dp'), may hold values from -0.75 to 0.75
- w_up: bfloat16 [4734976], P('dp'), may hold values from -0.1875 to 0.1875
- w_down: bfloat16 [4734976], P('dp'), may hold values from -0.09375 to 0.09375
- vectors: bfloat16 [13056], P('dp'), may hold values from 0.099609375 to 1.8984375
Outputs:
- block_output: bfloat16 [4096, 1088], P('dp')
- input_grad: float32 [4096, 1088], P('dp')
- grad_qkv: float32 [3551232], P('dp')
- grad_out: float32 [1183744], P('dp')
- grad_up: float32 [4734976], P('dp')
- grad_down: float32 [4734976], P('dp')
- grad_vectors: float32 [13056], P('dp')
The draws below stay inside these ranges and needn't reach their ends.
Inputs may be any that keep to these rules, and one draw needn't show every extreme that they name: `seq_lengths`: in every row the lengths sum to 128; the longest sequence has 64 tokens.
All inputs are finite; a program needn't handle non-finite values.
Results may differ from the reference program's by a relative error of at most 0.012.
The reference program's roundings to bfloat16 on the way count: a program that leaves them out, or rounds other values in their place, can miss the bound.
Values may be sent and summed in bfloat16 or wider, within the bound.
A program may use at most 320 MiB of HBM per device.

```python
import math
import jax
import jax.numpy as jnp
import numpy as np
from jax import lax

HEADS = 17
HEAD_DIM = 64
D = 1088
FF = 4352
TOK_DEV = 128
SEQS = 4
MOST = 64
TOKENS = 4096
N_DP = 32


def draw_block_input(key, part):
    own = jax.random.fold_in(key, 31)
    values = jax.random.truncated_normal(own, -6.0, 6.0, (TOKENS, D), jnp.float32)
    return values.astype(jnp.bfloat16)


def draw_w_qkv(key, part):
    own = jax.random.fold_in(key, 47)
    spread = D ** (-0.5)
    base = jax.random.truncated_normal(own, -6.0, 6.0, (D, 3 * D), jnp.float32) * spread
    return base.reshape(3 * D * D).astype(jnp.bfloat16)


def steps_of(rng, dims, pieces, smallest, top_value):
    loudness, own = 1.0, jax.random.fold_in(rng, 6)
    for axis_at, parts in pieces:
        heights = jnp.exp(jax.random.uniform(jax.random.fold_in(own, axis_at), (parts,), jnp.float32, smallest / len(pieces), top_value / len(pieces)))
        loudness = loudness * jnp.repeat(heights, dims[axis_at] // parts).reshape([-1 if axis == axis_at else 1 for axis in range(len(dims))])
    return loudness


def split_up(amount, total, limit, lean):
    weights = [(1 << 20) // math.isqrt(grade ** lean) + 1 for grade in range(2, amount + 1)]
    spare, counts = total - limit - (amount - 1), [1] * (amount - 1)
    while spare > 0:
        free = [i for i in range(amount - 1) if counts[i] < limit]
        whole, remaining = sum([weights[i] for i in free]), spare
        for i in free:
            more = min(limit - counts[i], max(1, remaining * weights[i] // whole), spare)
            counts[i] = counts[i] + more
            spare = spare - more
    return np.array([limit] + counts)


def uneven_parts(own_key, number_of, total, most, slope):
    if number_of == 2:
        one = jax.random.randint(own_key, (), max(1, total - most), min(most, total - 1) + 1)
        return jnp.stack([one, total - one])
    tallies = jnp.asarray(split_up(number_of, total, most, slope), jnp.int32)
    couples = (number_of - 1) // 2
    donor, taker = tallies[1:1 + 2 * couples:2], tallies[2:2 + 2 * couples:2]
    slack = jnp.minimum(donor - 1, most - taker)
    shifted = jax.random.randint(jax.random.fold_in(own_key, 1), (couples,), 0, 1 << 20) % (slack + 1)
    tallies = tallies.at[1:1 + 2 * couples:2].set(donor - shifted).at[2:2 + 2 * couples:2].set(taker + shifted)
    return tallies[jax.random.permutation(jax.random.fold_in(own_key, 2), number_of)]


def scatter_about(stream_key, dims, scale, most, shards=(), kind=jnp.bfloat16):
    array = scale * jax.random.normal(stream_key, dims, jnp.float32)
    if shards:
        array = array * steps_of(stream_key, dims, shards, -0.22, 0.18)
    return jnp.clip(array, -most, most).astype(kind)


def setup_inputs(seed: int = 0) -> dict:
    streams_of = jax.random.split(jax.random.key(seed), 9)
    block_input = draw_block_input(jax.random.fold_in(streams_of[8], 71), 0)
    out_cotangent = scatter_about(streams_of[1], (TOKENS, D), 1.0, 6.0, ((0, 32),))
    seq_lengths = jax.vmap(lambda own: uneven_parts(own, SEQS, TOK_DEV, MOST, 2))(jax.random.split(streams_of[2], N_DP)).reshape((N_DP, SEQS)).astype(jnp.int32)
    w_qkv = draw_w_qkv(jax.random.fold_in(streams_of[8], 71), 0)
    w_out = scatter_about(streams_of[4], (D * D,), (D // 16) ** -0.5, 0.75, ((0, 32),))
    w_up = scatter_about(streams_of[5], (D * FF,), D ** -0.5, 0.1875, ((0, 32),))
    w_down = scatter_about(streams_of[6], (FF * D,), FF ** -0.5, 0.09375, ((0, 32),))
    vectors = jnp.clip(1.0 + 0.18 * jax.random.normal(streams_of[7], (8 * D + FF,), jnp.float32), 0.099609375, 1.8984375).astype(jnp.bfloat16)
    return {"block_input": block_input, "out_cotangent": out_cotangent, "seq_lengths": seq_lengths, "w_qkv": w_qkv, "w_out": w_out, "w_up": w_up, "w_down": w_down, "vectors": vectors}


EPS = 1e-05
ROOT_HALF = 0.7071067811865476
INV_ROOT_TAU = 0.3989422804014327

def layer_norm(rows, gain, shift):
    mean = lax.optimization_barrier(jnp.mean(rows, axis=1, keepdims=True))
    centered = rows - mean
    inverse = lax.rsqrt(lax.optimization_barrier(jnp.mean(centered * centered, axis=1, keepdims=True)) + EPS)
    normed = centered * inverse
    return (normed, inverse, normed * gain + shift)

def norm_back(grad_rows, normed, inverse, gain):
    scaled = grad_rows * gain
    inner = lax.optimization_barrier(jnp.mean(scaled * normed, axis=1, keepdims=True))
    return inverse * (scaled - lax.optimization_barrier(jnp.mean(scaled, axis=1, keepdims=True)) - normed * inner)

def gelu_exact(value):
    return 0.5 * value * (1.0 + lax.erf(value * ROOT_HALF))

def gelu_slope(value):
    return 0.5 * (1.0 + lax.erf(value * ROOT_HALF)) + value * jnp.exp(-0.5 * value * value) * INV_ROOT_TAU

def causal_mask(lengths, rows):
    ends = jnp.cumsum(lengths.astype(jnp.int32))
    position = jnp.arange(rows, dtype=jnp.int32)
    segment = lax.optimization_barrier(jnp.sum((position[:, None] >= ends[None, :]).astype(jnp.int32), axis=1))
    return (segment[:, None] == segment[None, :]) & (position[None, :] <= position[:, None])

def score_block(query, keys, mask):
    scores = jnp.einsum('qhe,khe->hqk', query.astype(jnp.float32), keys.astype(jnp.float32))
    return jnp.where(mask[None], scores, -1e+30)

def device_pass(block, cotangent, lengths, wqkv, wo, wup, wdn, vec):
    rows = block.shape[0]
    scale = HEAD_DIM ** (-0.5)
    mask = causal_mask(lengths, rows)
    inputs = block.astype(jnp.float32)
    normed1, inverse1, pre1 = layer_norm(inputs, vec[0:D], vec[D:2 * D])
    first = pre1.astype(jnp.bfloat16)
    qkv = jnp.dot(first, wqkv, preferred_element_type=jnp.float32)
    query = ((qkv[:, 0:D] + vec[2 * D:3 * D]) * scale).astype(jnp.bfloat16).reshape(rows, HEADS, HEAD_DIM)
    keys = qkv[:, D:2 * D].astype(jnp.bfloat16).reshape(rows, HEADS, HEAD_DIM)
    values = (qkv[:, 2 * D:3 * D] + vec[3 * D:4 * D]).astype(jnp.bfloat16).reshape(rows, HEADS, HEAD_DIM)
    scores = score_block(query, keys, mask)
    peak = lax.optimization_barrier(jnp.max(scores, axis=2, keepdims=True))
    logsum = peak + jnp.log(lax.optimization_barrier(jnp.sum(jnp.exp(scores - peak), axis=2, keepdims=True)))
    probs_low = jnp.exp(scores - logsum).astype(jnp.bfloat16)
    mixed = jnp.einsum('hqk,khe->qhe', probs_low.astype(jnp.float32), values.astype(jnp.float32))
    mixed = mixed.astype(jnp.bfloat16).reshape(rows, D)
    resid = inputs + jnp.dot(mixed, wo, preferred_element_type=jnp.float32) + vec[4 * D:5 * D]
    normed2, inverse2, pre2 = layer_norm(resid, vec[5 * D:6 * D], vec[6 * D:7 * D])
    second = pre2.astype(jnp.bfloat16)
    upper = jnp.dot(second, wup, preferred_element_type=jnp.float32) + vec[7 * D:7 * D + FF]
    active = gelu_exact(upper).astype(jnp.bfloat16)
    output = (resid + jnp.dot(active, wdn, preferred_element_type=jnp.float32) + vec[7 * D + FF:]).astype(jnp.bfloat16)
    grad_top = cotangent.astype(jnp.float32)
    grad_low = cotangent
    g_down = jnp.dot(active.T, grad_low, preferred_element_type=jnp.float32)
    d_upper = jnp.dot(grad_low, wdn.T, preferred_element_type=jnp.float32) * gelu_slope(upper)
    d_upper_low = d_upper.astype(jnp.bfloat16)
    g_up = jnp.dot(second.T, d_upper_low, preferred_element_type=jnp.float32)
    d_second = jnp.dot(d_upper_low, wup.T, preferred_element_type=jnp.float32)
    d_resid = grad_top + norm_back(d_second, normed2, inverse2, vec[5 * D:6 * D])
    d_resid_low = d_resid.astype(jnp.bfloat16)
    g_out = jnp.dot(mixed.T, d_resid_low, preferred_element_type=jnp.float32)
    d_mixed = jnp.dot(d_resid_low, wo.T, preferred_element_type=jnp.float32).astype(jnp.bfloat16)
    d_mixed = d_mixed.reshape(rows, HEADS, HEAD_DIM)
    probs = jnp.exp(score_block(query, keys, mask) - logsum)
    probs_low = probs.astype(jnp.bfloat16)
    d_values = jnp.einsum('hqk,qhe->khe', probs_low.astype(jnp.float32), d_mixed.astype(jnp.float32))
    d_probs = jnp.einsum('qhe,khe->hqk', d_mixed.astype(jnp.float32), values.astype(jnp.float32))
    delta = lax.optimization_barrier(jnp.sum(probs * d_probs, axis=2, keepdims=True))
    d_scores = (probs * (d_probs - delta)).astype(jnp.bfloat16).astype(jnp.float32)
    d_query = jnp.einsum('hqk,khe->qhe', d_scores, keys.astype(jnp.float32)).reshape(rows, D) * scale
    d_keys = jnp.einsum('hqk,qhe->khe', d_scores, query.astype(jnp.float32)).reshape(rows, D)
    d_values = d_values.reshape(rows, D)
    d_qkv = jnp.concatenate([d_query, d_keys, d_values], axis=1).astype(jnp.bfloat16)
    g_qkv = jnp.dot(first.T, d_qkv, preferred_element_type=jnp.float32)
    d_first = jnp.dot(d_qkv, wqkv.T, preferred_element_type=jnp.float32)
    d_input = d_resid + norm_back(d_first, normed1, inverse1, vec[0:D])
    g_vec = jnp.concatenate([lax.optimization_barrier(jnp.sum(d_first * normed1, axis=0)), lax.optimization_barrier(jnp.sum(d_first, axis=0)), lax.optimization_barrier(jnp.sum(d_query, axis=0)), lax.optimization_barrier(jnp.sum(d_values, axis=0)), lax.optimization_barrier(jnp.sum(d_resid, axis=0)), lax.optimization_barrier(jnp.sum(d_second * normed2, axis=0)), lax.optimization_barrier(jnp.sum(d_second, axis=0)), lax.optimization_barrier(jnp.sum(d_upper, axis=0)), lax.optimization_barrier(jnp.sum(grad_top, axis=0))])
    return (output, d_input, (g_qkv, g_out, g_up, g_down, g_vec))

def reference(block_input, out_cotangent, seq_lengths, w_qkv, w_out, w_up, w_down, vectors):
    wqkv = w_qkv.reshape(D, 3 * D)
    wo = w_out.reshape(D, D)
    wup = w_up.reshape(D, FF)
    wdn = w_down.reshape(FF, D)
    vec = vectors.astype(jnp.float32)
    inputs = block_input.reshape(N_DP, TOK_DEV, D)
    cotangents = out_cotangent.reshape(N_DP, TOK_DEV, D)

    def step(carry, item):
        block, cotangent, lengths = item
        output, d_input, grads = device_pass(block, cotangent, lengths, wqkv, wo, wup, wdn, vec)
        return (tuple((total + part for total, part in zip(carry, grads))), (output, d_input))
    start = (jnp.zeros((D, 3 * D), jnp.float32), jnp.zeros((D, D), jnp.float32), jnp.zeros((D, FF), jnp.float32), jnp.zeros((FF, D), jnp.float32), jnp.zeros((8 * D + FF,), jnp.float32))
    totals, (outputs, d_inputs) = lax.scan(step, start, (inputs, cotangents, seq_lengths))
    return (outputs.reshape(TOKENS, D), d_inputs.reshape(TOKENS, D), totals[0].reshape(-1), totals[1].reshape(-1), totals[2].reshape(-1), totals[3].reshape(-1), totals[4])
```

```python
import functools

import jax
import jax.numpy as jnp
from jax import lax
from jax.experimental import pallas as pl
from jax.experimental.pallas import tpu as pltpu
from jax.sharding import PartitionSpec as P

HEADS = 17
HEAD_DIM = 64


EPS = 1e-05
ROOT_HALF = 0.7071067811865476
INV_ROOT_TAU = 0.3989422804014327


def layer_norm(rows, gain, shift):
    mean = jnp.mean(rows, axis=1, keepdims=True)
    centered = rows - mean
    inverse = lax.rsqrt(jnp.mean(centered * centered, axis=1, keepdims=True) + EPS)
    normed = centered * inverse
    return (normed, inverse, normed * gain + shift)


def norm_back(grad_rows, normed, inverse, gain):
    scaled = grad_rows * gain
    inner = jnp.mean(scaled * normed, axis=1, keepdims=True)
    return inverse * (scaled - jnp.mean(scaled, axis=1, keepdims=True) - normed * inner)


def gelu_exact(value):
    return 0.5 * value * (1.0 + lax.erf(value * ROOT_HALF))


def gelu_slope(value):
    return (
        0.5 * (1.0 + lax.erf(value * ROOT_HALF))
        + value * jnp.exp(-0.5 * value * value) * INV_ROOT_TAU
    )


def causal_mask(lengths, rows):
    count = lengths.shape[0]
    order = jnp.arange(count, dtype=jnp.int32)
    ends = jnp.sum(jnp.where(order[:, None] <= order[None, :], lengths[:, None], 0), axis=0)
    position = jnp.arange(rows, dtype=jnp.int32)
    segment = jnp.sum((position[:, None] >= ends[None, :]).astype(jnp.int32), axis=1)
    return (segment[:, None] == segment[None, :]) & (position[None, :] <= position[:, None])


def score_block(query, keys, mask):
    scores = jnp.einsum("qhe,khe->hqk", query, keys, preferred_element_type=jnp.float32)
    return jnp.where(mask[None], scores, -1e30)


def shape_params(flat_parts, width):
    hidden = 4 * width
    return (
        flat_parts[0].reshape(width, 3 * width),
        flat_parts[1].reshape(width, width),
        flat_parts[2].reshape(width, hidden),
        flat_parts[3].reshape(hidden, width),
        flat_parts[4].astype(jnp.float32),
    )


def window_term(left_rows, right_rows, flat_start, flat_count):
    inner_len = left_rows.shape[1]
    columns = right_rows.shape[1]
    row_count = min(inner_len, flat_count // columns + 2)
    row_first = jnp.clip(flat_start // columns, 0, inner_len - row_count)
    product = lax.dot_general(
        left_rows, right_rows, (((0,), (0,)), ((), ())), preferred_element_type=jnp.float32
    ).reshape(-1)
    padded = jnp.concatenate([product, jnp.zeros((flat_count,), jnp.float32)])
    return lax.dynamic_slice_in_dim(padded, flat_start - row_first * columns, flat_count, 0)


def shard_terms(pairs, vector_grad, device_total):
    piece_lens = [
        left_rows.shape[1] * right_rows.shape[1] // device_total for left_rows, right_rows in pairs
    ]
    piece_lens = piece_lens + [vector_grad.shape[0] // device_total]
    shard_len = sum(piece_lens)

    def shard_term(start, count):
        dev_count = count // shard_len
        dev_first = start // shard_len
        pieces = []
        for (left_rows, right_rows), piece_len in zip(pairs, piece_lens):
            window = window_term(
                left_rows, right_rows, dev_first * piece_len, dev_count * piece_len
            )
            pieces.append(window.reshape(dev_count, piece_len))
        vec_len = piece_lens[-1]
        window = vector_grad
        pieces.append(window.reshape(dev_count, vec_len))
        return jnp.concatenate(pieces, axis=1).reshape(-1)

    return (shard_term, shard_len, piece_lens)


def split_shard(summed, piece_lens):
    outputs = []
    offset = 0
    for piece_len in piece_lens:
        outputs.append(summed[offset : offset + piece_len])
        offset = offset + piece_len
    return outputs


def fetch_flat(w_qkv, w_out, w_up, w_down, vectors, width):
    fetched = tuple(
        lax.all_gather(part, "dp", axis=0, tiled=True)
        for part in (w_qkv, w_out, w_up, w_down, vectors)
    )
    return shape_params(fetched, width)


def reduce_flat(pairs, g_vec, device_total):
    all_term, all_len, all_lens = shard_terms(pairs, g_vec, device_total)
    return split_shard(
        lax.psum_scatter(
            all_term(jnp.int32(0), all_len * device_total),
            "dp",
            scatter_dimension=0,
            tiled=True,
        ),
        all_lens,
    )


def body_flat(block_input, out_cotangent, seq_lengths, w_qkv, w_out, w_up, w_down, vectors):
    rows, width = block_input.shape
    hidden = 4 * width
    scale = HEAD_DIM ** (-0.5)
    device_total = lax.axis_size("dp")
    mask = causal_mask(seq_lengths[0], rows)
    wqkv, wo, wup, wdn, vec = fetch_flat(w_qkv, w_out, w_up, w_down, vectors, width)
    inputs = block_input.astype(jnp.float32)
    normed1, inverse1, pre1 = layer_norm(inputs, vec[0:width], vec[width : 2 * width])
    first = pre1.astype(jnp.bfloat16)
    qkv = jnp.dot(first, wqkv, preferred_element_type=jnp.float32)
    query = (
        ((qkv[:, 0:width] + vec[2 * width : 3 * width]) * scale)
        .astype(jnp.bfloat16)
        .reshape(rows, HEADS, HEAD_DIM)
    )
    keys = qkv[:, width : 2 * width].astype(jnp.bfloat16).reshape(rows, HEADS, HEAD_DIM)
    values = (
        (qkv[:, 2 * width : 3 * width] + vec[3 * width : 4 * width])
        .astype(jnp.bfloat16)
        .reshape(rows, HEADS, HEAD_DIM)
    )
    scores = score_block(query, keys, mask)
    peak = jnp.max(scores, axis=2, keepdims=True)
    logsum = peak + jnp.log(jnp.sum(jnp.exp(scores - peak), axis=2, keepdims=True))
    probs_low = jnp.exp(scores - logsum).astype(jnp.bfloat16)
    mixed = jnp.einsum("hqk,khe->qhe", probs_low, values, preferred_element_type=jnp.float32)
    mixed = mixed.astype(jnp.bfloat16).reshape(rows, width)
    resid = (
        inputs + jnp.dot(mixed, wo, preferred_element_type=jnp.float32) + vec[4 * width : 5 * width]
    )
    normed2, inverse2, pre2 = layer_norm(
        resid, vec[5 * width : 6 * width], vec[6 * width : 7 * width]
    )
    second = pre2.astype(jnp.bfloat16)
    upper = (
        jnp.dot(second, wup, preferred_element_type=jnp.float32)
        + vec[7 * width : 7 * width + hidden]
    )
    active = gelu_exact(upper).astype(jnp.bfloat16)
    output = (
        resid + jnp.dot(active, wdn, preferred_element_type=jnp.float32) + vec[7 * width + hidden :]
    )
    block_output = output.astype(jnp.bfloat16)
    back_w = (wqkv, wo, wup, wdn)
    bqkv, bwo, bwup, bwdn = back_w
    grad_top = out_cotangent.astype(jnp.float32)
    d_upper = jnp.dot(out_cotangent, bwdn.T, preferred_element_type=jnp.float32) * gelu_slope(upper)
    d_upper_low = d_upper.astype(jnp.bfloat16)
    d_second = jnp.dot(d_upper_low, bwup.T, preferred_element_type=jnp.float32)
    d_resid = grad_top + norm_back(d_second, normed2, inverse2, vec[5 * width : 6 * width])
    d_resid_low = d_resid.astype(jnp.bfloat16)
    d_mixed = jnp.dot(d_resid_low, bwo.T, preferred_element_type=jnp.float32).astype(jnp.bfloat16)
    d_mixed = d_mixed.reshape(rows, HEADS, HEAD_DIM)
    probs = jnp.exp(score_block(query, keys, mask) - logsum)
    probs_low = probs.astype(jnp.bfloat16)
    d_values = jnp.einsum("hqk,qhe->khe", probs_low, d_mixed, preferred_element_type=jnp.float32)
    d_probs = jnp.einsum("qhe,khe->hqk", d_mixed, values, preferred_element_type=jnp.float32)
    delta = jnp.sum(probs * d_probs, axis=2, keepdims=True)
    d_scores = (probs * (d_probs - delta)).astype(jnp.bfloat16)
    d_query = (
        jnp.einsum("hqk,khe->qhe", d_scores, keys, preferred_element_type=jnp.float32).reshape(
            rows, width
        )
        * scale
    )
    d_keys = jnp.einsum(
        "hqk,qhe->khe", d_scores, query, preferred_element_type=jnp.float32
    ).reshape(rows, width)
    d_values = d_values.reshape(rows, width)
    d_qkv = jnp.concatenate([d_query, d_keys, d_values], axis=1).astype(jnp.bfloat16)
    d_first = jnp.dot(d_qkv, bqkv.T, preferred_element_type=jnp.float32)
    input_grad = d_resid + norm_back(d_first, normed1, inverse1, vec[0:width])
    g_vec = jnp.concatenate(
        [
            jnp.sum(d_first * normed1, axis=0),
            jnp.sum(d_first, axis=0),
            jnp.sum(d_query, axis=0),
            jnp.sum(d_values, axis=0),
            jnp.sum(d_resid, axis=0),
            jnp.sum(d_second * normed2, axis=0),
            jnp.sum(d_second, axis=0),
            jnp.sum(d_upper, axis=0),
            jnp.sum(grad_top, axis=0),
        ]
    )
    pairs = [(first, d_qkv), (mixed, d_resid_low), (second, d_upper_low), (active, out_cotangent)]
    grad_qkv, grad_out, grad_up, grad_down, grad_vectors = reduce_flat(pairs, g_vec, device_total)
    return (block_output, input_grad, grad_qkv, grad_out, grad_up, grad_down, grad_vectors)


GROUP = 8
CHIPS = 4
ROWS = 16
LANES = 128
MESH = pl.DeviceIdType.MESH


def ceil_to(count, unit):
    return -(-count // unit) * unit


def gather_kernel(
    depth, s_in, t_in, u_in, d_in, c_in, s_all, t_all, u_all, d_all, c_all, *sems
):
    (
        local,
        z_send,
        z_recv,
        s_send,
        s_recv,
        half_send,
        half_recv,
        core_send,
        core_recv,
        t_send,
        t_recv,
        u_send,
        u_recv,
        c_send,
        c_recv,
    ) = sems
    me = lax.axis_index("dp")
    layer = me // GROUP
    chip = (me % GROUP) // 2
    core = me % 2
    east = chip % 2
    north = chip // 2
    chip_at = (
        chip,
        north * 2 + (1 - east),
        (1 - north) * 2 + east,
        (1 - north) * 2 + (1 - east),
    )
    mates = tuple(layer * GROUP + at * 2 + core for at in chip_at)
    twin = layer * GROUP + chip * 2 + (1 - core)
    above = me + GROUP
    below = me - GROUP
    has_above = layer < depth - 1
    has_below = layer > 0

    barrier = pltpu.get_barrier_semaphore()
    for device in mates[1:] + (twin,):
        pl.semaphore_signal(barrier, inc=1, device_id=(device,), device_id_type=MESH)

    @pl.when(has_above)
    def _():
        pl.semaphore_signal(barrier, inc=1, device_id=(above,), device_id_type=MESH)

    @pl.when(has_below)
    def _():
        pl.semaphore_signal(barrier, inc=1, device_id=(below,), device_id_type=MESH)

    ends = (layer + depth - 1) // depth + (2 * depth - 2 - layer) // depth
    pl.semaphore_wait(barrier, CHIPS + ends)

    def send(source, target, send_sem, recv_sem, device):
        return pltpu.make_async_remote_copy(
            src_ref=source,
            dst_ref=target,
            send_sem=send_sem,
            recv_sem=recv_sem,
            device_id=(device,),
            device_id_type=MESH,
        )

    def layer_of(slot):
        return lax.rem(layer + slot, depth)

    def s_at(slot):
        return s_in if slot == 0 else s_all.at[0, 0, slot]

    def t_at(slot):
        return t_in if slot == 0 else t_all.at[layer_of(slot), chip, core]

    def d_at(slot):
        return d_in if slot == 0 else d_all.at[layer_of(slot), core]

    def u_at(slot):
        return u_all.at[0, :, slot]

    def s_to(slot, source):
        return s_all.at[0, 0, slot]

    def t_to(slot, source):
        return t_all.at[layer_of(source), chip, core]

    def d_to(slot, source):
        return d_all.at[layer_of(source), core]

    def u_to(slot, source):
        return u_all.at[0, :, slot]

    places = {"t": (0, t_at, t_to), "s": (1, s_at, s_to), "d": (2, d_at, d_to), "u": (3, u_at, u_to)}

    def z_copy(name, slot, up):
        index, source, target = places[name]
        there = (slot - 1) % depth if up else (slot + 1) % depth
        return send(
            source(slot),
            target(there, slot),
            z_send.at[index, slot, 0 if up else 1],
            z_recv.at[index, there],
            above if up else below,
        )

    def z_arrival(name, slot):
        index, source, target = places[name]
        here = target(slot, slot)
        return send(here, here, z_send.at[index, slot, 0], z_recv.at[index, slot], above)

    def routes():
        found = [(0, True, has_above), (0, False, has_below)]
        for far in range(1, depth - 1):
            found.append((depth - far, True, (layer >= far) & has_above))
            found.append((far, False, (layer + far < depth) & has_below))
        return found

    def z_forward(name, step):
        for slot, up, allowed in routes()[2 * step : 2 * step + 2]:

            @pl.when(allowed)
            def _(slot=slot, up=up):
                z_copy(name, slot, up).start()

    def z_land(name, far, then=None):
        for slot, came in ((depth - far, layer >= far), (far, layer + far < depth)):

            @pl.when(came)
            def _(slot=slot):
                z_arrival(name, slot).wait_recv()
                if then is not None:
                    then(slot)

    def s_plane(slot, way):
        return send(
            s_at(slot), s_all.at[0, way, slot], s_send.at[way, slot], s_recv.at[way, slot], mates[way]
        )

    def s_half(slot, way):
        rows = s_in.shape[0] // 2
        part = pl.ds(0 if way == 1 else rows, rows)
        return send(
            s_all.at[0, way, slot, part],
            s_all.at[0, 3, slot, part],
            half_send.at[way, slot],
            half_recv.at[way, slot],
            mates[3 - way],
        )

    def s_core(slot, way):
        source = s_at(slot) if way == 0 else s_all.at[0, way, slot]
        return send(
            source, s_all.at[1, way, slot], core_send.at[way, slot], core_recv.at[way, slot], twin
        )

    def s_spread(slot):
        s_plane(slot, 1).start()
        s_plane(slot, 2).start()
        s_core(slot, 0).start()

    def s_pass(slot):
        for way in (1, 2):
            s_plane(slot, way).wait_recv()
            s_half(slot, way).start()
            s_core(slot, way).start()

    def s_close(slot):
        for way in (1, 2):
            s_half(slot, way).wait_recv()
        s_core(slot, 3).start()

    def by_distance(far, act):
        if far == 0:
            act(0)
            return
        for slot, came in ((depth - far, layer >= far), (far, layer + far < depth)):

            @pl.when(came)
            def _(slot=slot):
                act(slot)

    def d_core(slot):
        return send(
            d_at(slot), d_to(slot, slot), core_send.at[4, slot], core_recv.at[4, slot], twin
        )

    def u_core(slot):
        return send(
            u_at(slot), u_all.at[1, :, slot], core_send.at[5, slot], core_recv.at[5, slot], twin
        )

    def d_twin_arrival(slot):
        here = d_all.at[layer_of(slot), 1 - core]
        return send(here, here, core_send.at[4, slot], core_recv.at[4, slot], twin)

    t_mine = t_all.at[:, chip, core]

    def t_plane(way):
        return send(t_mine, t_mine, t_send.at[way], t_recv.at[way], mates[way])

    def t_plane_arrival(way):
        here = t_all.at[:, chip_at[way], core]
        return send(here, here, t_send.at[way], t_recv.at[way], mates[way])

    t_core_block = t_all.at[:, :, core]
    t_twin_block = t_all.at[:, :, 1 - core]
    t_core = send(t_core_block, t_core_block, t_send.at[0], t_recv.at[0], twin)
    t_core_arrival = send(t_twin_block, t_twin_block, t_send.at[0], t_recv.at[0], twin)

    def u_plane(way):
        return send(
            u_in.at[chip_at[way]], u_all.at[0, way, 0], u_send.at[way], u_recv.at[way], mates[way]
        )

    def c_plane(way):
        return send(c_in, c_all.at[way], c_send.at[way], c_recv.at[way], mates[way])

    stay = [
        pltpu.make_async_copy(t_in, t_all.at[layer, chip, core], local.at[0]),
        pltpu.make_async_copy(u_in.at[chip], u_all.at[0, 0, 0], local.at[1]),
        pltpu.make_async_copy(s_in, s_all.at[0, 0, 0], local.at[2]),
        pltpu.make_async_copy(d_in, d_all.at[layer, core], local.at[3]),
        pltpu.make_async_copy(c_in, c_all.at[0], local.at[4]),
    ]

    z_forward("t", 0)
    z_forward("s", 0)
    for copy in stay:
        copy.start()
    for way in (1, 2, 3):
        u_plane(way).start()
    s_spread(0)
    for far in range(1, depth):
        z_land("t", far)
        if far < depth - 1:
            z_forward("t", far)
        z_land("s", far)
        if far < depth - 1:
            z_forward("s", far)
        if far == 1:
            z_forward("d", 0)
        by_distance(far, s_spread)
        if far == depth - 1:
            stay[0].wait()
            for way in (1, 2, 3):
                t_plane(way).start()
        if far == min(2, depth - 1):
            for way in (1, 2, 3):
                u_plane(way).wait_recv()
            stay[1].wait()
            z_forward("u", 0)
            u_core(0).start()
            d_core(0).start()
        by_distance(far - 1, s_pass)
    for way in (1, 2, 3):
        c_plane(way).start()
    for far in range(1, depth):
        z_land("d", far)
        if far < depth - 1:
            z_forward("d", far)
        by_distance(far, lambda slot: d_core(slot).start())
        if far == 1:
            by_distance(depth - 1, s_pass)
            for way in (1, 2, 3):
                t_plane_arrival(way).wait_recv()
            t_core.start()
        z_land("u", far)
        if far < depth - 1:
            z_forward("u", far)
        by_distance(far, lambda slot: u_core(slot).start())
        if far == 1:
            for near in range(depth):
                by_distance(near, s_close)
    for slot in range(depth):
        for way in range(CHIPS):
            s_core(slot, way).wait()
        u_core(slot).wait()
        d_core(slot).wait_send()
        d_twin_arrival(slot).wait_recv()
        for way in (1, 2):
            s_plane(slot, way).wait_send()
            s_half(slot, way).wait_send()
    for way in (1, 2, 3):
        u_plane(way).wait_send()
        t_plane(way).wait_send()
        c_plane(way).wait()
    t_core.wait_send()
    t_core_arrival.wait_recv()
    for copy in stay[2:]:
        copy.wait()
    for slot, up, allowed in routes():

        @pl.when(allowed)
        def _(slot=slot, up=up):
            for name in places:
                z_copy(name, slot, up).wait_send()


def gather_all(s_own, t_own, u_own, d_own, c_own, depth):
    low = jnp.bfloat16
    return pl.pallas_call(
        functools.partial(gather_kernel, depth),
        out_shape=[
            jax.ShapeDtypeStruct((2, CHIPS, depth) + s_own.shape, low),
            jax.ShapeDtypeStruct((depth, CHIPS, 2) + t_own.shape, low),
            jax.ShapeDtypeStruct((2, CHIPS, depth) + u_own.shape[1:], low),
            jax.ShapeDtypeStruct((depth, 2) + d_own.shape, low),
            jax.ShapeDtypeStruct((CHIPS,) + c_own.shape, low),
        ],
        in_specs=[pl.BlockSpec(memory_space=pl.ANY)] * 5,
        out_specs=[pl.BlockSpec(memory_space=pl.ANY)] * 5,
        scratch_shapes=[
            pltpu.SemaphoreType.DMA((5,)),
            pltpu.SemaphoreType.DMA((4, depth, 2)),
            pltpu.SemaphoreType.DMA((4, depth)),
            pltpu.SemaphoreType.DMA((3, depth)),
            pltpu.SemaphoreType.DMA((3, depth)),
            pltpu.SemaphoreType.DMA((3, depth)),
            pltpu.SemaphoreType.DMA((3, depth)),
            pltpu.SemaphoreType.DMA((6, depth)),
            pltpu.SemaphoreType.DMA((6, depth)),
            pltpu.SemaphoreType.DMA((4,)),
            pltpu.SemaphoreType.DMA((4,)),
            pltpu.SemaphoreType.DMA((4,)),
            pltpu.SemaphoreType.DMA((4,)),
            pltpu.SemaphoreType.DMA((4,)),
            pltpu.SemaphoreType.DMA((4,)),
        ],
        compiler_params=pltpu.CompilerParams(collective_id=0, has_side_effects=True),
        name="gather_params",
    )(s_own, t_own, u_own, d_own, c_own)


def swap(value, offset):
    total = lax.axis_size("dp")
    return lax.ppermute(value, "dp", [(at, at ^ offset) for at in range(total)])


def shift(value, first, last, step):
    pairs = [
        (layer * GROUP + at, (layer + step) * GROUP + at)
        for layer in range(first, last)
        for at in range(GROUP)
    ]
    return lax.ppermute(value, "dp", pairs)


def lower(value):
    return value.astype(jnp.bfloat16)


def wide(value):
    return value.astype(jnp.float32)


def chain_sum(terms):
    depth = len(terms)
    terms = list(terms)
    for step in range(1, depth):
        up = shift(lower(terms[depth - step]), 0, step, 1)
        down = shift(lower(terms[step]), depth - step, depth, -1)
        terms[depth - step - 1] = wide(terms[depth - step - 1]) + wide(up)
        after = (step + 1) % depth
        terms[after] = wide(terms[after]) + wide(down)
    return wide(terms[0])


def contract_rows(left, right):
    return lax.dot_general(left, right, (((0,), (0,)), ((), ())), preferred_element_type=jnp.float32)


def contract_columns(left, right):
    return lax.dot_general(left, right, (((1,), (1,)), ((), ())), preferred_element_type=jnp.float32)


def multiply(left, right):
    return jnp.dot(left, right, preferred_element_type=jnp.float32)


def core_sum(left, right):
    half = left.shape[1] // 2
    other = swap(lower(contract_rows(left[:, half:], right)), 1)
    return contract_rows(left[:, :half], right) + wide(other)


def scatter_all(left, right, depth, rows):
    whole = lower(core_sum(left, right)).reshape(CHIPS, depth, rows, right.shape[1])
    cut = depth // 2
    first, second = whole[:, :cut], whole[:, cut:]
    first = wide(first[:2]) + wide(swap(first[2:], 4))
    first = wide(first[0]) + wide(swap(lower(first[1]), 2))
    second = wide(second[0::2]) + wide(swap(second[1::2], 2))
    second = wide(second[0]) + wide(swap(lower(second[1]), 4))
    terms = [first[at] for at in range(cut)] + [second[at] for at in range(depth - cut)]
    return chain_sum(terms)


def two_parts(value):
    high = lax.reduce_precision(value, 8, 7)
    return jnp.concatenate([lower(high), lower(value - high)], axis=0)


def body_group(block_input, out_cotangent, seq_lengths, w_qkv, w_out, w_up, w_down, vectors):
    rows, width = block_input.shape
    hidden = 4 * width
    scale = HEAD_DIM ** (-0.5)
    total = lax.axis_size("dp")
    depth = total // GROUP
    own = width // total
    main = own // ROWS * ROWS
    tail = own - main
    step = hidden // total
    wide_step = ceil_to(step, ROWS)
    part = total // CHIPS * wide_step
    count = vectors.shape[0]
    me = lax.axis_index("dp")
    layer = me // GROUP
    chip = (me // 2) % CHIPS
    core = me % 2
    mask = causal_mask(seq_lengths[0], rows)

    side = jnp.concatenate([w_qkv.reshape(own, 3 * width), w_out.reshape(own, width)], axis=1)
    upper_own = jnp.pad(
        w_up.reshape(own, depth, CHIPS, 2, step), ((0, 0),) * 4 + ((0, wide_step - step),)
    )
    upper_own = upper_own.transpose(2, 0, 1, 3, 4).reshape(CHIPS, own, part)
    down_own = jnp.pad(w_down.reshape(step, width), ((0, wide_step - step), (0, 0)))
    side_rows = tail * hidden // LANES
    up_rows = tail * CHIPS * part // LANES
    vec_rows = ceil_to(count, LANES) // LANES
    used = side_rows + up_rows + vec_rows
    tail_rows = ceil_to(used, ROWS)
    extra = jnp.concatenate(
        [
            side[main:].reshape(side_rows, LANES),
            upper_own[:, main:].reshape(up_rows, LANES),
            jnp.pad(vectors, (0, vec_rows * LANES - count)).reshape(vec_rows, LANES),
            jnp.zeros((tail_rows - used, LANES), jnp.bfloat16),
        ],
        axis=0,
    )
    s_all, t_all, u_all, d_all, c_all = gather_all(
        side[:main], extra, upper_own[:, :main], down_own, out_cotangent, depth
    )
    bulk = total * main
    w_side = s_all.reshape(bulk, hidden)
    w_upper = u_all.reshape(bulk, part)
    w_lower = d_all.reshape(part, width)
    cots = c_all.reshape(CHIPS * rows, width)
    t_all = t_all.reshape(total, tail_rows, LANES)
    side_tail = t_all[:, :side_rows].reshape(total * tail, hidden)
    up_tail = t_all[:, side_rows : side_rows + up_rows].reshape(total, CHIPS, tail, part)
    up_tail = lax.dynamic_index_in_dim(up_tail, chip, 1, keepdims=False)
    up_tail = up_tail.reshape(total * tail, part)
    vec = t_all[:, side_rows + up_rows : used].reshape(total, vec_rows * LANES)[:, :count]
    vec = wide(vec.reshape(-1))
    bias_up = vec[7 * width : 7 * width + hidden].reshape(depth, CHIPS, 2, step)
    bias_up = lax.dynamic_index_in_dim(bias_up, chip, 1, keepdims=False)
    bias_up = jnp.pad(bias_up, ((0, 0), (0, 0), (0, wide_step - step))).reshape(1, part)

    place = jnp.arange(width, dtype=jnp.int32)
    slot = place // main
    there = (layer + slot % depth) % depth * GROUP
    there = there + jnp.bitwise_xor(chip, slot // depth % CHIPS) * 2
    there = there + jnp.bitwise_xor(core, slot // (depth * CHIPS))
    late = place - bulk
    origin = jnp.where(
        place < bulk, there * own + place % main, late // tail * own + main + late % tail
    )
    onehot = lower(place[:, None] == origin[None, :])

    def permute(value):
        return lower(multiply(value, onehot))

    def restore(value):
        return lower(contract_columns(value, onehot))

    def restore_wide(value):
        both = contract_columns(two_parts(value), onehot)
        return both[:rows] + both[rows:]

    wq, wo = w_side[:, : 3 * width], w_side[:, 3 * width :]
    wq_tail, wo_tail = side_tail[:, : 3 * width], side_tail[:, 3 * width :]

    inputs = wide(block_input)
    normed1, inverse1, pre1 = layer_norm(inputs, vec[0:width], vec[width : 2 * width])
    first = permute(lower(pre1))
    qkv = multiply(first[:, :bulk], wq) + multiply(first[:, bulk:], wq_tail)
    query = lower((qkv[:, 0:width] + vec[2 * width : 3 * width]) * scale)
    query = query.reshape(rows, HEADS, HEAD_DIM)
    keys = lower(qkv[:, width : 2 * width]).reshape(rows, HEADS, HEAD_DIM)
    values = lower(qkv[:, 2 * width : 3 * width] + vec[3 * width : 4 * width])
    values = values.reshape(rows, HEADS, HEAD_DIM)
    scores = score_block(query, keys, mask)
    peak = jnp.max(scores, axis=2, keepdims=True)
    logsum = peak + jnp.log(jnp.sum(jnp.exp(scores - peak), axis=2, keepdims=True))
    probs_low = lower(jnp.exp(scores - logsum))
    mixed = jnp.einsum("hqk,khe->qhe", probs_low, values, preferred_element_type=jnp.float32)
    mixed = permute(lower(mixed).reshape(rows, width))
    resid = inputs + multiply(mixed[:, :bulk], wo) + multiply(mixed[:, bulk:], wo_tail)
    resid = resid + vec[4 * width : 5 * width]
    gain2 = vec[5 * width : 6 * width]
    normed2, inverse2, pre2 = layer_norm(resid, gain2, vec[6 * width : 7 * width])
    second = lower(pre2)
    second = jnp.concatenate([second] + [swap(second, 2 * way) for way in range(1, CHIPS)], axis=0)
    second = permute(second)

    upper = multiply(second[:, :bulk], w_upper) + multiply(second[:, bulk:], up_tail) + bias_up
    active = lower(gelu_exact(upper))
    d_upper = contract_columns(cots, w_lower) * gelu_slope(upper)
    d_upper_low = lower(d_upper)
    d_second = jnp.concatenate(
        [contract_columns(d_upper_low, w_upper), contract_columns(d_upper_low, up_tail)], axis=1
    )
    d_second = contract_columns(lower(d_second), onehot).reshape(CHIPS, rows, width)
    d_second_low = lower(d_second)
    d_second = d_second[0] + sum(
        wide(swap(d_second_low[way], 2 * way)) for way in range(1, CHIPS)
    )
    lifted = multiply(active, w_lower).reshape(CHIPS, rows, width)
    lifted_low = lower(lifted)
    lifted = lifted[0] + sum(wide(swap(lifted_low[way], 2 * way)) for way in range(1, CHIPS))
    block_output = lower(resid + lifted + vec[7 * width + hidden :])

    g_up_tail = lower(contract_rows(second[:, bulk:], d_upper_low)).reshape(total, 1, tail, part)
    g_up = lower(core_sum(second[:, :bulk], d_upper_low)).reshape(CHIPS, depth, main, part)
    g_up = chain_sum([g_up[:, at] for at in range(depth)])
    g_up_low = lower(g_up)
    g_up = [g_up[0]] + [wide(swap(g_up_low[way], 2 * way)) for way in range(1, CHIPS)]
    g_up = jnp.stack(g_up, axis=0)
    g_up = jnp.stack(
        [
            lax.dynamic_index_in_dim(g_up, jnp.bitwise_xor(chip, at), 0, keepdims=False)
            for at in range(CHIPS)
        ],
        axis=0,
    )
    g_down = lower(contract_rows(active, cots)).reshape(depth, 2, wide_step, width)
    g_other = lax.dynamic_index_in_dim(g_down, 1 - core, 1, keepdims=False)
    g_mine = lax.dynamic_index_in_dim(g_down, core, 1, keepdims=False)
    g_down = wide(g_mine) + wide(swap(g_other, 1))
    g_down = chain_sum(
        [
            lax.dynamic_index_in_dim(g_down, (layer + at) % depth, 0, keepdims=False)
            for at in range(depth)
        ]
    )

    grad_top = wide(out_cotangent)
    d_resid = grad_top + norm_back(d_second, normed2, inverse2, gain2)
    d_resid_low = lower(d_resid)
    g_out_tail = contract_rows(mixed[:, bulk:], d_resid_low)
    g_out = scatter_all(mixed[:, :bulk], d_resid_low, depth, main)
    d_mixed = jnp.concatenate(
        [contract_columns(d_resid_low, wo), contract_columns(d_resid_low, wo_tail)], axis=1
    )
    d_mixed = restore(lower(d_mixed)).reshape(rows, HEADS, HEAD_DIM)
    probs = jnp.exp(score_block(query, keys, mask) - logsum)
    probs_low = lower(probs)
    d_values = jnp.einsum("hqk,qhe->khe", probs_low, d_mixed, preferred_element_type=jnp.float32)
    d_probs = jnp.einsum("qhe,khe->hqk", d_mixed, values, preferred_element_type=jnp.float32)
    delta = jnp.sum(probs * d_probs, axis=2, keepdims=True)
    d_scores = lower(probs * (d_probs - delta))
    d_query = jnp.einsum("hqk,khe->qhe", d_scores, keys, preferred_element_type=jnp.float32)
    d_query = d_query.reshape(rows, width) * scale
    d_keys = jnp.einsum("hqk,qhe->khe", d_scores, query, preferred_element_type=jnp.float32)
    d_keys = d_keys.reshape(rows, width)
    d_values = d_values.reshape(rows, width)
    d_qkv = lower(jnp.concatenate([d_query, d_keys, d_values], axis=1))
    g_qkv_tail = contract_rows(first[:, bulk:], d_qkv)
    g_qkv = scatter_all(first[:, :bulk], d_qkv, depth, main)
    d_first = jnp.concatenate(
        [contract_columns(d_qkv, wq), contract_columns(d_qkv, wq_tail)], axis=1
    )
    d_first = restore_wide(d_first)
    input_grad = d_resid + norm_back(d_first, normed1, inverse1, vec[0:width])

    d_bias_up = jnp.sum(d_upper, axis=0).reshape(depth, 1, 2, wide_step)[..., :step]
    turn = jnp.arange(CHIPS, dtype=jnp.int32)
    d_bias_up = jnp.where(turn[None, :, None, None] == chip, d_bias_up, 0.0)
    g_vec = jnp.concatenate(
        [
            jnp.sum(d_first * normed1, axis=0),
            jnp.sum(d_first, axis=0),
            jnp.sum(d_query, axis=0),
            jnp.sum(d_values, axis=0),
            jnp.sum(d_resid, axis=0),
            jnp.sum(d_second * normed2, axis=0),
            jnp.sum(d_second, axis=0),
            d_bias_up.reshape(hidden),
            jnp.sum(grad_top, axis=0),
        ]
    )
    g_side_tail = lower(jnp.concatenate([g_qkv_tail, g_out_tail], axis=1))
    g_up_tail = jnp.where(turn[None, :, None, None] == chip, g_up_tail, jnp.bfloat16(0))
    g_vec = jnp.pad(lower(g_vec).reshape(total, count), ((0, 0), (0, vec_rows * LANES - count)))
    g_extra = jnp.concatenate(
        [
            g_side_tail.reshape(total, side_rows, LANES),
            g_up_tail.reshape(total, up_rows, LANES),
            g_vec.reshape(total, vec_rows, LANES),
        ],
        axis=1,
    )
    g_extra = wide(lax.psum_scatter(g_extra, "dp", scatter_dimension=0, tiled=False))
    g_side_tail = g_extra[:side_rows].reshape(tail, hidden)
    g_up_tail = g_extra[side_rows : side_rows + up_rows].reshape(CHIPS, tail, part)
    grad_vectors = g_extra[side_rows + up_rows :].reshape(-1)[:count]
    grad_qkv = jnp.concatenate([g_qkv, g_side_tail[:, : 3 * width]], axis=0).reshape(-1)
    grad_out = jnp.concatenate([g_out, g_side_tail[:, 3 * width :]], axis=0).reshape(-1)
    grad_up = jnp.concatenate([g_up, g_up_tail], axis=1)
    grad_up = grad_up.reshape(CHIPS, own, depth, 2, wide_step)[..., :step]
    grad_up = grad_up.transpose(1, 2, 0, 3, 4).reshape(-1)
    grad_down = g_down[:step].reshape(-1)
    return (block_output, input_grad, grad_qkv, grad_out, grad_up, grad_down, grad_vectors)


def solution(mesh):
    in_specs = (
        P("dp", None),
        P("dp", None),
        P("dp", None),
        P("dp"),
        P("dp"),
        P("dp"),
        P("dp"),
        P("dp"),
    )
    out_specs = (P("dp", None), P("dp", None), P("dp"), P("dp"), P("dp"), P("dp"), P("dp"))
    total = mesh.shape["dp"]

    def body(*blocks):
        width = blocks[0].shape[1]
        own = width // total
        small = own % ROWS * 4 * width
        tidy = total % GROUP == 0 and width % total == 0 and own >= ROWS
        if tidy and small > 0 and small % LANES == 0:
            return body_group(*blocks)
        return body_flat(*blocks)

    return jax.shard_map(body, mesh=mesh, in_specs=in_specs, out_specs=out_specs, check_vma=False)
```

```python
import functools

import jax
import jax.numpy as jnp
from jax import lax
from jax.experimental import pallas as pl
from jax.experimental.pallas import tpu as pltpu
from jax.sharding import PartitionSpec as P

HEADS = 17
HEAD_DIM = 64


EPS = 1e-05
ROOT_HALF = 0.7071067811865476
INV_ROOT_TAU = 0.3989422804014327


def layer_norm(rows, gain, shift):
    mean = jnp.mean(rows, axis=1, keepdims=True)
    centered = rows - mean
    inverse = lax.rsqrt(jnp.mean(centered * centered, axis=1, keepdims=True) + EPS)
    normed = centered * inverse
    return (normed, inverse, normed * gain + shift)


def norm_back(grad_rows, normed, inverse, gain):
    scaled = grad_rows * gain
    inner = jnp.mean(scaled * normed, axis=1, keepdims=True)
    return inverse * (scaled - jnp.mean(scaled, axis=1, keepdims=True) - normed * inner)


def gelu_exact(value):
    return 0.5 * value * (1.0 + lax.erf(value * ROOT_HALF))


def gelu_slope(value):
    return (
        0.5 * (1.0 + lax.erf(value * ROOT_HALF))
        + value * jnp.exp(-0.5 * value * value) * INV_ROOT_TAU
    )


def causal_mask(lengths, rows):
    count = lengths.shape[0]
    order = jnp.arange(count, dtype=jnp.int32)
    ends = jnp.sum(jnp.where(order[:, None] <= order[None, :], lengths[:, None], 0), axis=0)
    position = jnp.arange(rows, dtype=jnp.int32)
    segment = jnp.sum((position[:, None] >= ends[None, :]).astype(jnp.int32), axis=1)
    return (segment[:, None] == segment[None, :]) & (position[None, :] <= position[:, None])


def score_block(query, keys, mask):
    scores = jnp.einsum("qhe,khe->hqk", query, keys, preferred_element_type=jnp.float32)
    return jnp.where(mask[None], scores, -1e30)


def shape_params(flat_parts, width):
    hidden = 4 * width
    return (
        flat_parts[0].reshape(width, 3 * width),
        flat_parts[1].reshape(width, width),
        flat_parts[2].reshape(width, hidden),
        flat_parts[3].reshape(hidden, width),
        flat_parts[4].astype(jnp.float32),
    )


def window_term(left_rows, right_rows, flat_start, flat_count):
    inner_len = left_rows.shape[1]
    columns = right_rows.shape[1]
    row_count = min(inner_len, flat_count // columns + 2)
    row_first = jnp.clip(flat_start // columns, 0, inner_len - row_count)
    product = lax.dot_general(
        left_rows, right_rows, (((0,), (0,)), ((), ())), preferred_element_type=jnp.float32
    ).reshape(-1)
    padded = jnp.concatenate([product, jnp.zeros((flat_count,), jnp.float32)])
    return lax.dynamic_slice_in_dim(padded, flat_start - row_first * columns, flat_count, 0)


def shard_terms(pairs, vector_grad, device_total):
    piece_lens = [
        left_rows.shape[1] * right_rows.shape[1] // device_total for left_rows, right_rows in pairs
    ]
    piece_lens = piece_lens + [vector_grad.shape[0] // device_total]
    shard_len = sum(piece_lens)

    def shard_term(start, count):
        dev_count = count // shard_len
        dev_first = start // shard_len
        pieces = []
        for (left_rows, right_rows), piece_len in zip(pairs, piece_lens):
            window = window_term(
                left_rows, right_rows, dev_first * piece_len, dev_count * piece_len
            )
            pieces.append(window.reshape(dev_count, piece_len))
        vec_len = piece_lens[-1]
        window = vector_grad
        pieces.append(window.reshape(dev_count, vec_len))
        return jnp.concatenate(pieces, axis=1).reshape(-1)

    return (shard_term, shard_len, piece_lens)


def split_shard(summed, piece_lens):
    outputs = []
    offset = 0
    for piece_len in piece_lens:
        outputs.append(summed[offset : offset + piece_len])
        offset = offset + piece_len
    return outputs


def fetch_flat(w_qkv, w_out, w_up, w_down, vectors, width):
    fetched = tuple(
        lax.all_gather(part, "dp", axis=0, tiled=True)
        for part in (w_qkv, w_out, w_up, w_down, vectors)
    )
    return shape_params(fetched, width)


def reduce_flat(pairs, g_vec, device_total):
    all_term, all_len, all_lens = shard_terms(pairs, g_vec, device_total)
    return split_shard(
        lax.psum_scatter(
            all_term(jnp.int32(0), all_len * device_total),
            "dp",
            scatter_dimension=0,
            tiled=True,
        ),
        all_lens,
    )


def body_flat(block_input, out_cotangent, seq_lengths, w_qkv, w_out, w_up, w_down, vectors):
    rows, width = block_input.shape
    hidden = 4 * width
    scale = HEAD_DIM ** (-0.5)
    device_total = lax.axis_size("dp")
    mask = causal_mask(seq_lengths[0], rows)
    wqkv, wo, wup, wdn, vec = fetch_flat(w_qkv, w_out, w_up, w_down, vectors, width)
    inputs = block_input.astype(jnp.float32)
    normed1, inverse1, pre1 = layer_norm(inputs, vec[0:width], vec[width : 2 * width])
    first = pre1.astype(jnp.bfloat16)
    qkv = jnp.dot(first, wqkv, preferred_element_type=jnp.float32)
    query = (
        ((qkv[:, 0:width] + vec[2 * width : 3 * width]) * scale)
        .astype(jnp.bfloat16)
        .reshape(rows, HEADS, HEAD_DIM)
    )
    keys = qkv[:, width : 2 * width].astype(jnp.bfloat16).reshape(rows, HEADS, HEAD_DIM)
    values = (
        (qkv[:, 2 * width : 3 * width] + vec[3 * width : 4 * width])
        .astype(jnp.bfloat16)
        .reshape(rows, HEADS, HEAD_DIM)
    )
    scores = score_block(query, keys, mask)
    peak = jnp.max(scores, axis=2, keepdims=True)
    logsum = peak + jnp.log(jnp.sum(jnp.exp(scores - peak), axis=2, keepdims=True))
    probs_low = jnp.exp(scores - logsum).astype(jnp.bfloat16)
    mixed = jnp.einsum("hqk,khe->qhe", probs_low, values, preferred_element_type=jnp.float32)
    mixed = mixed.astype(jnp.bfloat16).reshape(rows, width)
    resid = (
        inputs + jnp.dot(mixed, wo, preferred_element_type=jnp.float32) + vec[4 * width : 5 * width]
    )
    normed2, inverse2, pre2 = layer_norm(
        resid, vec[5 * width : 6 * width], vec[6 * width : 7 * width]
    )
    second = pre2.astype(jnp.bfloat16)
    upper = (
        jnp.dot(second, wup, preferred_element_type=jnp.float32)
        + vec[7 * width : 7 * width + hidden]
    )
    active = gelu_exact(upper).astype(jnp.bfloat16)
    output = (
        resid + jnp.dot(active, wdn, preferred_element_type=jnp.float32) + vec[7 * width + hidden :]
    )
    block_output = output.astype(jnp.bfloat16)
    back_w = (wqkv, wo, wup, wdn)
    bqkv, bwo, bwup, bwdn = back_w
    grad_top = out_cotangent.astype(jnp.float32)
    d_upper = jnp.dot(out_cotangent, bwdn.T, preferred_element_type=jnp.float32) * gelu_slope(upper)
    d_upper_low = d_upper.astype(jnp.bfloat16)
    d_second = jnp.dot(d_upper_low, bwup.T, preferred_element_type=jnp.float32)
    d_resid = grad_top + norm_back(d_second, normed2, inverse2, vec[5 * width : 6 * width])
    d_resid_low = d_resid.astype(jnp.bfloat16)
    d_mixed = jnp.dot(d_resid_low, bwo.T, preferred_element_type=jnp.float32).astype(jnp.bfloat16)
    d_mixed = d_mixed.reshape(rows, HEADS, HEAD_DIM)
    probs = jnp.exp(score_block(query, keys, mask) - logsum)
    probs_low = probs.astype(jnp.bfloat16)
    d_values = jnp.einsum("hqk,qhe->khe", probs_low, d_mixed, preferred_element_type=jnp.float32)
    d_probs = jnp.einsum("qhe,khe->hqk", d_mixed, values, preferred_element_type=jnp.float32)
    delta = jnp.sum(probs * d_probs, axis=2, keepdims=True)
    d_scores = (probs * (d_probs - delta)).astype(jnp.bfloat16)
    d_query = (
        jnp.einsum("hqk,khe->qhe", d_scores, keys, preferred_element_type=jnp.float32).reshape(
            rows, width
        )
        * scale
    )
    d_keys = jnp.einsum(
        "hqk,qhe->khe", d_scores, query, preferred_element_type=jnp.float32
    ).reshape(rows, width)
    d_values = d_values.reshape(rows, width)
    d_qkv = jnp.concatenate([d_query, d_keys, d_values], axis=1).astype(jnp.bfloat16)
    d_first = jnp.dot(d_qkv, bqkv.T, preferred_element_type=jnp.float32)
    input_grad = d_resid + norm_back(d_first, normed1, inverse1, vec[0:width])
    g_vec = jnp.concatenate(
        [
            jnp.sum(d_first * normed1, axis=0),
            jnp.sum(d_first, axis=0),
            jnp.sum(d_query, axis=0),
            jnp.sum(d_values, axis=0),
            jnp.sum(d_resid, axis=0),
            jnp.sum(d_second * normed2, axis=0),
            jnp.sum(d_second, axis=0),
            jnp.sum(d_upper, axis=0),
            jnp.sum(grad_top, axis=0),
        ]
    )
    pairs = [(first, d_qkv), (mixed, d_resid_low), (second, d_upper_low), (active, out_cotangent)]
    grad_qkv, grad_out, grad_up, grad_down, grad_vectors = reduce_flat(pairs, g_vec, device_total)
    return (block_output, input_grad, grad_qkv, grad_out, grad_up, grad_down, grad_vectors)


GROUP = 8
CHIPS = 4
ROWS = 16
LANES = 128
MESH = pl.DeviceIdType.MESH


def ceil_to(count, unit):
    return -(-count // unit) * unit


def gather_kernel(
    depth, s_in, t_in, u_in, d_in, c_in, s_all, t_all, u_all, d_all, c_all, *sems
):
    (
        local,
        z_send,
        z_recv,
        s_send,
        s_recv,
        half_send,
        half_recv,
        core_send,
        core_recv,
        t_send,
        t_recv,
        u_send,
        u_recv,
        c_send,
        c_recv,
    ) = sems
    me = lax.axis_index("dp")
    layer = me // GROUP
    chip = (me % GROUP) // 2
    core = me % 2
    east = chip % 2
    north = chip // 2
    chip_at = (
        chip,
        north * 2 + (1 - east),
        (1 - north) * 2 + east,
        (1 - north) * 2 + (1 - east),
    )
    mates = tuple(layer * GROUP + at * 2 + core for at in chip_at)
    twin = layer * GROUP + chip * 2 + (1 - core)
    above = me + GROUP
    below = me - GROUP
    has_above = layer < depth - 1
    has_below = layer > 0

    barrier = pltpu.get_barrier_semaphore()
    for device in mates[1:] + (twin,):
        pl.semaphore_signal(barrier, inc=1, device_id=(device,), device_id_type=MESH)

    @pl.when(has_above)
    def _():
        pl.semaphore_signal(barrier, inc=1, device_id=(above,), device_id_type=MESH)

    @pl.when(has_below)
    def _():
        pl.semaphore_signal(barrier, inc=1, device_id=(below,), device_id_type=MESH)

    ends = (layer + depth - 1) // depth + (2 * depth - 2 - layer) // depth
    pl.semaphore_wait(barrier, CHIPS + ends)

    def send(source, target, send_sem, recv_sem, device):
        return pltpu.make_async_remote_copy(
            src_ref=source,
            dst_ref=target,
            send_sem=send_sem,
            recv_sem=recv_sem,
            device_id=(device,),
            device_id_type=MESH,
        )

    def layer_of(slot):
        return lax.rem(layer + slot, depth)

    def s_at(slot):
        return s_in if slot == 0 else s_all.at[0, 0, slot]

    def t_at(slot):
        return t_in if slot == 0 else t_all.at[layer_of(slot), chip, core]

    def d_at(slot):
        return d_in if slot == 0 else d_all.at[layer_of(slot), core]

    def u_at(slot):
        return u_all.at[0, :, slot]

    def s_to(slot, source):
        return s_all.at[0, 0, slot]

    def t_to(slot, source):
        return t_all.at[layer_of(source), chip, core]

    def d_to(slot, source):
        return d_all.at[layer_of(source), core]

    def u_to(slot, source):
        return u_all.at[0, :, slot]

    places = {"t": (0, t_at, t_to), "s": (1, s_at, s_to), "d": (2, d_at, d_to), "u": (3, u_at, u_to)}

    def z_copy(name, slot, up):
        index, source, target = places[name]
        there = (slot - 1) % depth if up else (slot + 1) % depth
        return send(
            source(slot),
            target(there, slot),
            z_send.at[index, slot, 0 if up else 1],
            z_recv.at[index, there],
            above if up else below,
        )

    def z_arrival(name, slot):
        index, source, target = places[name]
        here = target(slot, slot)
        return send(here, here, z_send.at[index, slot, 0], z_recv.at[index, slot], above)

    def routes():
        found = [(0, True, has_above), (0, False, has_below)]
        for far in range(1, depth - 1):
            found.append((depth - far, True, (layer >= far) & has_above))
            found.append((far, False, (layer + far < depth) & has_below))
        return found

    def z_forward(name, step):
        for slot, up, allowed in routes()[2 * step : 2 * step + 2]:

            @pl.when(allowed)
            def _(slot=slot, up=up):
                z_copy(name, slot, up).start()

    def z_land(name, far, then=None):
        for slot, came in ((depth - far, layer >= far), (far, layer + far < depth)):

            @pl.when(came)
            def _(slot=slot):
                z_arrival(name, slot).wait_recv()
                if then is not None:
                    then(slot)

    def s_plane(slot, way):
        return send(
            s_at(slot), s_all.at[0, way, slot], s_send.at[way, slot], s_recv.at[way, slot], mates[way]
        )

    def s_half(slot, way):
        rows = s_in.shape[0] // 2
        part = pl.ds(0 if way == 1 else rows, rows)
        return send(
            s_all.at[0, way, slot, part],
            s_all.at[0, 3, slot, part],
            half_send.at[way, slot],
            half_recv.at[way, slot],
            mates[3 - way],
        )

    def s_core(slot, way):
        source = s_at(slot) if way == 0 else s_all.at[0, way, slot]
        return send(
            source, s_all.at[1, way, slot], core_send.at[way, slot], core_recv.at[way, slot], twin
        )

    def s_spread(slot):
        s_plane(slot, 1).start()
        s_plane(slot, 2).start()
        s_core(slot, 0).start()

    def s_pass(slot):
        for way in (1, 2):
            s_plane(slot, way).wait_recv()
            s_half(slot, way).start()
            s_core(slot, way).start()

    def s_close(slot):
        for way in (1, 2):
            s_half(slot, way).wait_recv()
        s_core(slot, 3).start()

    def by_distance(far, act):
        if far == 0:
            act(0)
            return
        for slot, came in ((depth - far, layer >= far), (far, layer + far < depth)):

            @pl.when(came)
            def _(slot=slot):
                act(slot)

    def d_core(slot):
        return send(
            d_at(slot), d_to(slot, slot), core_send.at[4, slot], core_recv.at[4, slot], twin
        )

    def u_core(slot):
        return send(
            u_at(slot), u_all.at[1, :, slot], core_send.at[5, slot], core_recv.at[5, slot], twin
        )

    def d_twin_arrival(slot):
        here = d_all.at[layer_of(slot), 1 - core]
        return send(here, here, core_send.at[4, slot], core_recv.at[4, slot], twin)

    t_mine = t_all.at[:, chip, core]

    def t_plane(way):
        return send(t_mine, t_mine, t_send.at[way], t_recv.at[way], mates[way])

    def t_plane_arrival(way):
        here = t_all.at[:, chip_at[way], core]
        return send(here, here, t_send.at[way], t_recv.at[way], mates[way])

    t_core_block = t_all.at[:, :, core]
    t_twin_block = t_all.at[:, :, 1 - core]
    t_core = send(t_core_block, t_core_block, t_send.at[0], t_recv.at[0], twin)
    t_core_arrival = send(t_twin_block, t_twin_block, t_send.at[0], t_recv.at[0], twin)

    def u_plane(way):
        return send(
            u_in.at[chip_at[way]], u_all.at[0, way, 0], u_send.at[way], u_recv.at[way], mates[way]
        )

    def c_plane(way):
        return send(c_in, c_all.at[way], c_send.at[way], c_recv.at[way], mates[way])

    stay = [
        pltpu.make_async_copy(t_in, t_all.at[layer, chip, core], local.at[0]),
        pltpu.make_async_copy(u_in.at[chip], u_all.at[0, 0, 0], local.at[1]),
        pltpu.make_async_copy(s_in, s_all.at[0, 0, 0], local.at[2]),
        pltpu.make_async_copy(d_in, d_all.at[layer, core], local.at[3]),
        pltpu.make_async_copy(c_in, c_all.at[0], local.at[4]),
    ]

    z_forward("t", 0)
    z_forward("s", 0)
    for copy in stay:
        copy.start()
    for way in (1, 2, 3):
        u_plane(way).start()
    s_spread(0)
    for far in range(1, depth):
        z_land("t", far)
        if far < depth - 1:
            z_forward("t", far)
        z_land("s", far)
        if far < depth - 1:
            z_forward("s", far)
        if far == 1:
            z_forward("d", 0)
        by_distance(far, s_spread)
        if far == depth - 1:
            stay[0].wait()
            for way in (1, 2, 3):
                t_plane(way).start()
        if far == min(2, depth - 1):
            for way in (1, 2, 3):
                u_plane(way).wait_recv()
            stay[1].wait()
            z_forward("u", 0)
            u_core(0).start()
            d_core(0).start()
        by_distance(far - 1, s_pass)
    for way in (1, 2, 3):
        c_plane(way).start()
    for far in range(1, depth):
        z_land("d", far)
        if far < depth - 1:
            z_forward("d", far)
        by_distance(far, lambda slot: d_core(slot).start())
        if far == 1:
            by_distance(depth - 1, s_pass)
            for way in (1, 2, 3):
                t_plane_arrival(way).wait_recv()
            t_core.start()
        z_land("u", far)
        if far < depth - 1:
            z_forward("u", far)
        by_distance(far, lambda slot: u_core(slot).start())
        if far == 1:
            for near in range(depth):
                by_distance(near, s_close)
    for slot in range(depth):
        for way in range(CHIPS):
            s_core(slot, way).wait()
        u_core(slot).wait()
        d_core(slot).wait_send()
        d_twin_arrival(slot).wait_recv()
        for way in (1, 2):
            s_plane(slot, way).wait_send()
            s_half(slot, way).wait_send()
    for way in (1, 2, 3):
        u_plane(way).wait_send()
        t_plane(way).wait_send()
        c_plane(way).wait()
    t_core.wait_send()
    t_core_arrival.wait_recv()
    for copy in stay[2:]:
        copy.wait()
    for slot, up, allowed in routes():

        @pl.when(allowed)
        def _(slot=slot, up=up):
            for name in places:
                z_copy(name, slot, up).wait_send()


def gather_all(s_own, t_own, u_own, d_own, c_own, depth):
    low = jnp.bfloat16
    return pl.pallas_call(
        functools.partial(gather_kernel, depth),
        out_shape=[
            jax.ShapeDtypeStruct((2, CHIPS, depth) + s_own.shape, low),
            jax.ShapeDtypeStruct((depth, CHIPS, 2) + t_own.shape, low),
            jax.ShapeDtypeStruct((2, CHIPS, depth) + u_own.shape[1:], low),
            jax.ShapeDtypeStruct((depth, 2) + d_own.shape, low),
            jax.ShapeDtypeStruct((CHIPS,) + c_own.shape, low),
        ],
        in_specs=[pl.BlockSpec(memory_space=pl.ANY)] * 5,
        out_specs=[pl.BlockSpec(memory_space=pl.ANY)] * 5,
        scratch_shapes=[
            pltpu.SemaphoreType.DMA((5,)),
            pltpu.SemaphoreType.DMA((4, depth, 2)),
            pltpu.SemaphoreType.DMA((4, depth)),
            pltpu.SemaphoreType.DMA((3, depth)),
            pltpu.SemaphoreType.DMA((3, depth)),
            pltpu.SemaphoreType.DMA((3, depth)),
            pltpu.SemaphoreType.DMA((3, depth)),
            pltpu.SemaphoreType.DMA((6, depth)),
            pltpu.SemaphoreType.DMA((6, depth)),
            pltpu.SemaphoreType.DMA((4,)),
            pltpu.SemaphoreType.DMA((4,)),
            pltpu.SemaphoreType.DMA((4,)),
            pltpu.SemaphoreType.DMA((4,)),
            pltpu.SemaphoreType.DMA((4,)),
            pltpu.SemaphoreType.DMA((4,)),
        ],
        compiler_params=pltpu.CompilerParams(collective_id=0, has_side_effects=True),
        name="gather_params",
    )(s_own, t_own, u_own, d_own, c_own)


def add_blocks(count, pick, other):
    @pl.loop(0, count)
    def _(at):
        here, term = pick(at), other(at)
        here[...] = (here[...].astype(jnp.float32) + term[...].astype(jnp.float32)).astype(here.dtype)


def scatter_kernel(depth, *refs):
    ins, outs, refs = refs[:5], refs[5:10], refs[10:]
    (
        acc_q,
        rc_q,
        p1_q,
        p2_q,
        z_q,
        acc_o,
        rc_o,
        p1_o,
        p2_o,
        z_o,
        acc_u,
        rc_u,
        z_u,
        fin_u,
        out_u,
        in_u,
        acc_d,
        rc_d,
        z_d,
        acc_t,
        rc_t,
        p_t,
        fin_t,
        z_t,
        local,
        c_send,
        c_recv,
        p_send,
        p_recv,
        t_send,
        t_recv,
        z_send,
        z_recv,
        a_send,
        a_recv,
    ) = refs
    q_in, o_in, t_in, u_in, d_in = ins
    q_out, o_out, t_out, u_out, d_out = outs
    me = lax.axis_index("dp")
    layer = me // GROUP
    chip = (me % GROUP) // 2
    core = me % 2
    east = chip % 2
    north = chip // 2
    chip_at = (
        chip,
        north * 2 + (1 - east),
        (1 - north) * 2 + east,
        (1 - north) * 2 + (1 - east),
    )
    mates = tuple(layer * GROUP + at * 2 + core for at in chip_at)
    twin = layer * GROUP + chip * 2 + (1 - core)
    above = me + GROUP
    below = me - GROUP

    barrier = pltpu.get_barrier_semaphore()
    for device in mates[1:] + (twin,):
        pl.semaphore_signal(barrier, inc=1, device_id=(device,), device_id_type=MESH)

    @pl.when(layer < depth - 1)
    def _():
        pl.semaphore_signal(barrier, inc=1, device_id=(above,), device_id_type=MESH)

    @pl.when(layer > 0)
    def _():
        pl.semaphore_signal(barrier, inc=1, device_id=(below,), device_id_type=MESH)

    ends = (layer + depth - 1) // depth + (2 * depth - 2 - layer) // depth
    pl.semaphore_wait(barrier, CHIPS + ends)

    def send(source, target, send_sem, recv_sem, device):
        return pltpu.make_async_remote_copy(
            src_ref=source,
            dst_ref=target,
            send_sem=send_sem,
            recv_sem=recv_sem,
            device_id=(device,),
            device_id_type=MESH,
        )

    def layer_of(slot):
        return lax.rem(layer + slot, depth)

    bulk = ((0, q_in, acc_q, rc_q, p1_q, p2_q), (1, o_in, acc_o, rc_o, p1_o, p2_o))
    half = p1_q.shape[3]

    stay = [
        pltpu.make_async_copy(u_in.at[0], acc_u, local.at[0]),
        pltpu.make_async_copy(d_in.at[:, core], acc_d, local.at[1]),
        pltpu.make_async_copy(q_in.at[0], acc_q, local.at[2]),
        pltpu.make_async_copy(o_in.at[0], acc_o, local.at[3]),
        pltpu.make_async_copy(t_in.at[:, :, core], acc_t, local.at[4]),
    ]
    u_core = send(u_in.at[1], rc_u, c_send.at[2, 0], c_recv.at[2, 0], twin)
    d_core = send(d_in.at[:, 1 - core], rc_d, c_send.at[3, 0], c_recv.at[3, 0], twin)
    t_core = send(t_in.at[:, :, 1 - core], rc_t, c_send.at[4, 0], c_recv.at[4, 0], twin)

    def b_core(item, slot):
        index, whole, acc, rc, p1, p2 = item
        return send(
            whole.at[1, :, :, slot],
            rc.at[:, :, slot],
            c_send.at[index, slot],
            c_recv.at[index, slot],
            twin,
        )

    def b_first(item, slot, side):
        index, whole, acc, rc, p1, p2 = item
        if side == 0:
            source = acc.at[1, :, slot, pl.ds(0, half)]
        else:
            source = acc.at[:, 1, slot, pl.ds(half, half)]
        at = (index * 2 + side) * 2
        return send(
            source, p1.at[side, :, slot], p_send.at[at, slot], p_recv.at[at, slot], mates[2 - side]
        )

    def b_second(item, slot, side):
        index, whole, acc, rc, p1, p2 = item
        if side == 0:
            source = acc.at[0, 1, slot, pl.ds(0, half)]
        else:
            source = acc.at[1, 0, slot, pl.ds(half, half)]
        at = (index * 2 + side) * 2 + 1
        return send(
            source, p2.at[side, slot], p_send.at[at, slot], p_recv.at[at, slot], mates[1 + side]
        )

    def open_slot(slot):
        for item in bulk:
            index, whole, acc, rc, p1, p2 = item
            b_core(item, slot).wait_recv()
            add_blocks(
                CHIPS,
                lambda at, acc=acc: acc.at[at // 2, at % 2, slot],
                lambda at, rc=rc: rc.at[at // 2, at % 2, slot],
            )
            b_first(item, slot, 0).start()
            b_first(item, slot, 1).start()

    def middle_slot(slot):
        for item in bulk:
            index, whole, acc, rc, p1, p2 = item
            b_first(item, slot, 0).wait_recv()
            add_blocks(
                2,
                lambda at, acc=acc: acc.at[0, at, slot, pl.ds(0, half)],
                lambda at, p1=p1: p1.at[0, at, slot],
            )
            b_second(item, slot, 0).start()
            b_first(item, slot, 1).wait_recv()
            add_blocks(
                2,
                lambda at, acc=acc: acc.at[at, 0, slot, pl.ds(half, half)],
                lambda at, p1=p1: p1.at[1, at, slot],
            )
            b_second(item, slot, 1).start()

    def close_slot(slot):
        for item in bulk:
            index, whole, acc, rc, p1, p2 = item
            for side in (0, 1):
                b_second(item, slot, side).wait_recv()
                add_blocks(
                    1,
                    lambda at, acc=acc, side=side: acc.at[0, 0, slot, pl.ds(side * half, half)],
                    lambda at, p2=p2, side=side: p2.at[side, slot],
                )

    chains = (
        (0, lambda slot: acc_q.at[0, 0, slot], z_q, q_out),
        (1, lambda slot: acc_o.at[0, 0, slot], z_o, o_out),
        (2, lambda slot: acc_u.at[:, slot], z_u, fin_u),
        (3, lambda slot: acc_d.at[layer_of(slot)], z_d, d_out),
        (4, lambda slot: fin_t.at[layer_of(slot)], z_t, t_out),
    )

    def z_up(chain, step):
        index, block, landing, final = chain
        return send(
            block(depth - step),
            landing.at[0, step],
            z_send.at[index, 0, step],
            z_recv.at[index, 0, step],
            above,
        )

    def z_down(chain, step):
        index, block, landing, final = chain
        return send(
            block(step),
            landing.at[1, step],
            z_send.at[index, 1, step],
            z_recv.at[index, 1, step],
            below,
        )

    def z_start(chain, step):
        @pl.when(layer < step)
        def _():
            z_up(chain, step).start()

        @pl.when(layer >= depth - step)
        def _():
            z_down(chain, step).start()

    def z_take(chain, step):
        index, block, landing, final = chain
        last = step == depth - 1
        if last:
            final[...] = block(0)[...].astype(jnp.float32)
        targets = (depth - step - 1, (step + 1) % depth)
        came = (
            (layer >= 1) & (layer <= step),
            (layer <= depth - 2) & (layer >= depth - step - 1),
        )
        for way, make in enumerate((z_up, z_down)):

            @pl.when(came[way])
            def _(way=way, make=make):
                make(chain, step).wait_recv()
                here = final if last else block(targets[way])
                total = here[...].astype(jnp.float32) + landing[way, step].astype(jnp.float32)
                here[...] = total.astype(here.dtype)

    def z_next(chain, step):
        z_take(chain, step)
        if step < depth - 1:
            z_start(chain, step + 1)

    def t_plane(way):
        return send(
            acc_t.at[:, chip_at[way]], p_t.at[way], t_send.at[way], t_recv.at[way], mates[way]
        )

    def u_turn(way):
        return send(out_u.at[way], in_u.at[way], a_send.at[way], a_recv.at[way], mates[way])

    chain_q, chain_o, chain_u, chain_d, chain_t = chains
    order = tuple(range(1, depth)) + (0,)
    u_core.start()
    d_core.start()
    for copy in stay:
        copy.start()
    for slot in order:
        for item in bulk:
            b_core(item, slot).start()
    t_core.start()

    u_core.wait_recv()
    stay[0].wait()
    add_blocks(
        CHIPS * depth,
        lambda at: acc_u.at[at // depth, at % depth],
        lambda at: rc_u.at[at // depth, at % depth],
    )
    z_start(chain_u, 1)
    d_core.wait_recv()
    stay[1].wait()
    add_blocks(depth, lambda at: acc_d.at[at], lambda at: rc_d.at[at])
    z_start(chain_d, 1)
    stay[2].wait()
    stay[3].wait()
    open_slot(order[0])
    open_slot(order[1])
    t_core.wait_recv()
    stay[4].wait()
    add_blocks(
        CHIPS * depth,
        lambda at: acc_t.at[at // CHIPS, at % CHIPS],
        lambda at: rc_t.at[at // CHIPS, at % CHIPS],
    )
    for way in (1, 2, 3):
        t_plane(way).start()
    z_steps = [(chain, step) for step in range(1, depth) for chain in (chain_u, chain_d)]
    taken = 0
    for at in range(depth):
        if taken < len(z_steps):
            z_next(*z_steps[taken])
            taken = taken + 1
        middle_slot(order[at])
        if at + 2 < depth:
            open_slot(order[at + 2])
        if at >= 1:
            close_slot(order[at - 1])
    for way in (1, 2, 3):
        t_plane(way).wait_recv()

    @pl.loop(0, depth)
    def _(at):
        total = acc_t[at, chip].astype(jnp.float32)
        for way in (1, 2, 3):
            total = total + p_t[way, at].astype(jnp.float32)
        fin_t[at] = total.astype(jnp.bfloat16)

    z_start(chain_t, 1)
    close_slot(order[depth - 1])
    z_start(chain_q, 1)
    z_start(chain_o, 1)
    for chain, step in z_steps[taken:]:
        z_next(chain, step)
    for way in (1, 2, 3):
        out_u[way] = fin_u[way].astype(jnp.bfloat16)
        u_turn(way).start()
    for step in range(1, depth):
        for chain in (chain_t, chain_q, chain_o):
            z_next(chain, step)
    u_out[chip] = fin_u[0]
    for way in (1, 2, 3):
        u_turn(way).wait_recv()
        u_out[chip_at[way]] = in_u[way].astype(jnp.float32)

    for copy in (u_core, d_core, t_core):
        copy.wait_send()
    for slot in range(depth):
        for item in bulk:
            b_core(item, slot).wait_send()
            for side in (0, 1):
                b_first(item, slot, side).wait_send()
                b_second(item, slot, side).wait_send()
    for way in (1, 2, 3):
        t_plane(way).wait_send()
        u_turn(way).wait_send()
    for step in range(1, depth):

        @pl.when(layer < step)
        def _(step=step):
            for chain in chains:
                z_up(chain, step).wait_send()

        @pl.when(layer >= depth - step)
        def _(step=step):
            for chain in chains:
                z_down(chain, step).wait_send()


def scatter_sums(q_part, o_part, t_part, u_part, d_part, depth, main):
    low, full = jnp.bfloat16, jnp.float32
    half = main // 2

    def bulk_scratch(columns):
        return [
            pltpu.VMEM((2, 2, depth, main, columns), low),
            pltpu.VMEM((2, 2, depth, main, columns), low),
            pltpu.VMEM((2, 2, depth, half, columns), low),
            pltpu.VMEM((2, depth, half, columns), low),
            pltpu.VMEM((2, depth, main, columns), low),
        ]

    q_columns, o_columns, u_columns = q_part.shape[1], o_part.shape[1], u_part.shape[1]
    down = d_part.shape[2:]
    small = t_part.shape[1:]
    dma = pltpu.SemaphoreType.DMA
    return pl.pallas_call(
        functools.partial(scatter_kernel, depth),
        out_shape=[
            jax.ShapeDtypeStruct((main, q_columns), full),
            jax.ShapeDtypeStruct((main, o_columns), full),
            jax.ShapeDtypeStruct(small, full),
            jax.ShapeDtypeStruct((CHIPS, main, u_columns), full),
            jax.ShapeDtypeStruct(down, full),
        ],
        in_specs=[pl.BlockSpec(memory_space=pl.ANY)] * 5,
        out_specs=[pl.BlockSpec(memory_space=pltpu.VMEM)] * 5,
        scratch_shapes=bulk_scratch(q_columns)
        + bulk_scratch(o_columns)
        + [
            pltpu.VMEM((CHIPS, depth, main, u_columns), low),
            pltpu.VMEM((CHIPS, depth, main, u_columns), low),
            pltpu.VMEM((2, depth, CHIPS, main, u_columns), low),
            pltpu.VMEM((CHIPS, main, u_columns), full),
            pltpu.VMEM((CHIPS, main, u_columns), low),
            pltpu.VMEM((CHIPS, main, u_columns), low),
            pltpu.VMEM((depth,) + down, low),
            pltpu.VMEM((depth,) + down, low),
            pltpu.VMEM((2, depth) + down, low),
            pltpu.VMEM((depth, CHIPS) + small, low),
            pltpu.VMEM((depth, CHIPS) + small, low),
            pltpu.VMEM((CHIPS, depth) + small, low),
            pltpu.VMEM((depth,) + small, low),
            pltpu.VMEM((2, depth) + small, low),
            dma((5,)),
            dma((5, depth)),
            dma((5, depth)),
            dma((8, depth)),
            dma((8, depth)),
            dma((4,)),
            dma((4,)),
            dma((5, 2, depth)),
            dma((5, 2, depth)),
            dma((4,)),
            dma((4,)),
        ],
        compiler_params=pltpu.CompilerParams(
            collective_id=1, has_side_effects=True, vmem_limit_bytes=48 * 2**20
        ),
        name="scatter_sums",
    )(
        q_part.reshape(2, 2, 2, depth, main, q_columns),
        o_part.reshape(2, 2, 2, depth, main, o_columns),
        t_part.reshape((depth, CHIPS, 2) + small),
        u_part.reshape(2, CHIPS, depth, main, u_columns),
        d_part,
    )


def swap(value, offset):
    total = lax.axis_size("dp")
    return lax.ppermute(value, "dp", [(at, at ^ offset) for at in range(total)])


def lower(value):
    return value.astype(jnp.bfloat16)


def wide(value):
    return value.astype(jnp.float32)


def contract_rows(left, right):
    return lax.dot_general(left, right, (((0,), (0,)), ((), ())), preferred_element_type=jnp.float32)


def contract_columns(left, right):
    return lax.dot_general(left, right, (((1,), (1,)), ((), ())), preferred_element_type=jnp.float32)


def multiply(left, right):
    return jnp.dot(left, right, preferred_element_type=jnp.float32)


def two_parts(value):
    high = lax.reduce_precision(value, 8, 7)
    return jnp.concatenate([lower(high), lower(value - high)], axis=0)


def body_group(block_input, out_cotangent, seq_lengths, w_qkv, w_out, w_up, w_down, vectors):
    rows, width = block_input.shape
    hidden = 4 * width
    scale = HEAD_DIM ** (-0.5)
    total = lax.axis_size("dp")
    depth = total // GROUP
    own = width // total
    main = own // (2 * ROWS) * (2 * ROWS)
    tail = own - main
    step = hidden // total
    wide_step = ceil_to(step, ROWS)
    part = total // CHIPS * wide_step
    count = vectors.shape[0]
    me = lax.axis_index("dp")
    layer = me // GROUP
    chip = (me // 2) % CHIPS
    core = me % 2
    mask = causal_mask(seq_lengths[0], rows)

    side = jnp.concatenate([w_qkv.reshape(own, 3 * width), w_out.reshape(own, width)], axis=1)
    upper_own = jnp.pad(
        w_up.reshape(own, depth, CHIPS, 2, step), ((0, 0),) * 4 + ((0, wide_step - step),)
    )
    upper_own = upper_own.transpose(2, 0, 1, 3, 4).reshape(CHIPS, own, part)
    down_own = jnp.pad(w_down.reshape(step, width), ((0, wide_step - step), (0, 0)))
    side_rows = tail * hidden // LANES
    up_rows = tail * CHIPS * part // LANES
    vec_rows = ceil_to(count, LANES) // LANES
    used = side_rows + up_rows + vec_rows
    tail_rows = ceil_to(used, ROWS)
    extra = jnp.concatenate(
        [
            side[main:].reshape(side_rows, LANES),
            upper_own[:, main:].reshape(up_rows, LANES),
            jnp.pad(vectors, (0, vec_rows * LANES - count)).reshape(vec_rows, LANES),
            jnp.zeros((tail_rows - used, LANES), jnp.bfloat16),
        ],
        axis=0,
    )
    s_all, t_all, u_all, d_all, c_all = gather_all(
        side[:main], extra, upper_own[:, :main], down_own, out_cotangent, depth
    )
    bulk = total * main
    w_side = s_all.reshape(bulk, hidden)
    w_upper = u_all.reshape(bulk, part)
    w_lower = d_all.reshape(part, width)
    cots = c_all.reshape(CHIPS * rows, width)
    t_all = t_all.reshape(total, tail_rows, LANES)
    side_tail = t_all[:, :side_rows].reshape(total * tail, hidden)
    up_tail = t_all[:, side_rows : side_rows + up_rows].reshape(total, CHIPS, tail, part)
    up_tail = lax.dynamic_index_in_dim(up_tail, chip, 1, keepdims=False)
    up_tail = up_tail.reshape(total * tail, part)
    vec = t_all[:, side_rows + up_rows : used].reshape(total, vec_rows * LANES)[:, :count]
    vec = wide(vec.reshape(-1))
    bias_up = vec[7 * width : 7 * width + hidden].reshape(depth, CHIPS, 2, step)
    bias_up = lax.dynamic_index_in_dim(bias_up, chip, 1, keepdims=False)
    bias_up = jnp.pad(bias_up, ((0, 0), (0, 0), (0, wide_step - step))).reshape(1, part)

    place = jnp.arange(width, dtype=jnp.int32)
    slot = place // main
    there = (layer + slot % depth) % depth * GROUP
    there = there + jnp.bitwise_xor(chip, slot // depth % CHIPS) * 2
    there = there + jnp.bitwise_xor(core, slot // (depth * CHIPS))
    late = place - bulk
    origin = jnp.where(
        place < bulk, there * own + place % main, late // tail * own + main + late % tail
    )
    onehot = lower(place[:, None] == origin[None, :])

    def permute(value):
        return lower(multiply(value, onehot))

    def restore(value):
        return lower(contract_columns(value, onehot))

    def restore_wide(value):
        both = contract_columns(two_parts(value), onehot)
        return both[:rows] + both[rows:]

    wq, wo = w_side[:, : 3 * width], w_side[:, 3 * width :]
    wq_tail, wo_tail = side_tail[:, : 3 * width], side_tail[:, 3 * width :]

    inputs = wide(block_input)
    normed1, inverse1, pre1 = layer_norm(inputs, vec[0:width], vec[width : 2 * width])
    first = permute(lower(pre1))
    qkv = multiply(first[:, :bulk], wq) + multiply(first[:, bulk:], wq_tail)
    query = lower((qkv[:, 0:width] + vec[2 * width : 3 * width]) * scale)
    query = query.reshape(rows, HEADS, HEAD_DIM)
    keys = lower(qkv[:, width : 2 * width]).reshape(rows, HEADS, HEAD_DIM)
    values = lower(qkv[:, 2 * width : 3 * width] + vec[3 * width : 4 * width])
    values = values.reshape(rows, HEADS, HEAD_DIM)
    scores = score_block(query, keys, mask)
    peak = jnp.max(scores, axis=2, keepdims=True)
    logsum = peak + jnp.log(jnp.sum(jnp.exp(scores - peak), axis=2, keepdims=True))
    probs_low = lower(jnp.exp(scores - logsum))
    mixed = jnp.einsum("hqk,khe->qhe", probs_low, values, preferred_element_type=jnp.float32)
    mixed = permute(lower(mixed).reshape(rows, width))
    resid = inputs + multiply(mixed[:, :bulk], wo) + multiply(mixed[:, bulk:], wo_tail)
    resid = resid + vec[4 * width : 5 * width]
    gain2 = vec[5 * width : 6 * width]
    normed2, inverse2, pre2 = layer_norm(resid, gain2, vec[6 * width : 7 * width])
    second = lower(pre2)
    second = jnp.concatenate([second] + [swap(second, 2 * way) for way in range(1, CHIPS)], axis=0)
    second = permute(second)

    upper = multiply(second[:, :bulk], w_upper) + multiply(second[:, bulk:], up_tail) + bias_up
    active = lower(gelu_exact(upper))
    d_upper = contract_columns(cots, w_lower) * gelu_slope(upper)
    d_upper_low = lower(d_upper)
    d_second = jnp.concatenate(
        [contract_columns(d_upper_low, w_upper), contract_columns(d_upper_low, up_tail)], axis=1
    )
    d_second = contract_columns(lower(d_second), onehot).reshape(CHIPS, rows, width)
    d_second_low = lower(d_second)
    d_second = d_second[0] + sum(
        wide(swap(d_second_low[way], 2 * way)) for way in range(1, CHIPS)
    )
    lifted = multiply(active, w_lower).reshape(CHIPS, rows, width)
    lifted_low = lower(lifted)
    lifted = lifted[0] + sum(wide(swap(lifted_low[way], 2 * way)) for way in range(1, CHIPS))
    block_output = lower(resid + lifted + vec[7 * width + hidden :])

    g_up_tail = lower(contract_rows(second[:, bulk:], d_upper_low)).reshape(total, 1, tail, part)
    g_up = lower(contract_rows(second[:, :bulk], d_upper_low))
    g_down = lower(contract_rows(active, cots)).reshape(depth, 2, wide_step, width)

    grad_top = wide(out_cotangent)
    d_resid = grad_top + norm_back(d_second, normed2, inverse2, gain2)
    d_resid_low = lower(d_resid)
    g_out_tail = contract_rows(mixed[:, bulk:], d_resid_low)
    g_out = lower(contract_rows(mixed[:, :bulk], d_resid_low))
    d_mixed = jnp.concatenate(
        [contract_columns(d_resid_low, wo), contract_columns(d_resid_low, wo_tail)], axis=1
    )
    d_mixed = restore(lower(d_mixed)).reshape(rows, HEADS, HEAD_DIM)
    probs = jnp.exp(score_block(query, keys, mask) - logsum)
    probs_low = lower(probs)
    d_values = jnp.einsum("hqk,qhe->khe", probs_low, d_mixed, preferred_element_type=jnp.float32)
    d_probs = jnp.einsum("qhe,khe->hqk", d_mixed, values, preferred_element_type=jnp.float32)
    delta = jnp.sum(probs * d_probs, axis=2, keepdims=True)
    d_scores = lower(probs * (d_probs - delta))
    d_query = jnp.einsum("hqk,khe->qhe", d_scores, keys, preferred_element_type=jnp.float32)
    d_query = d_query.reshape(rows, width) * scale
    d_keys = jnp.einsum("hqk,qhe->khe", d_scores, query, preferred_element_type=jnp.float32)
    d_keys = d_keys.reshape(rows, width)
    d_values = d_values.reshape(rows, width)
    d_qkv = lower(jnp.concatenate([d_query, d_keys, d_values], axis=1))
    g_qkv_tail = contract_rows(first[:, bulk:], d_qkv)
    g_qkv = lower(contract_rows(first[:, :bulk], d_qkv))
    d_first = jnp.concatenate(
        [contract_columns(d_qkv, wq), contract_columns(d_qkv, wq_tail)], axis=1
    )
    d_first = restore_wide(d_first)
    input_grad = d_resid + norm_back(d_first, normed1, inverse1, vec[0:width])

    d_bias_up = jnp.sum(d_upper, axis=0).reshape(depth, 1, 2, wide_step)[..., :step]
    turn = jnp.arange(CHIPS, dtype=jnp.int32)
    d_bias_up = jnp.where(turn[None, :, None, None] == chip, d_bias_up, 0.0)
    g_vec = jnp.concatenate(
        [
            jnp.sum(d_first * normed1, axis=0),
            jnp.sum(d_first, axis=0),
            jnp.sum(d_query, axis=0),
            jnp.sum(d_values, axis=0),
            jnp.sum(d_resid, axis=0),
            jnp.sum(d_second * normed2, axis=0),
            jnp.sum(d_second, axis=0),
            d_bias_up.reshape(hidden),
            jnp.sum(grad_top, axis=0),
        ]
    )
    g_side_tail = lower(jnp.concatenate([g_qkv_tail, g_out_tail], axis=1))
    g_up_tail = jnp.where(turn[None, :, None, None] == chip, g_up_tail, jnp.bfloat16(0))
    g_vec = jnp.pad(lower(g_vec).reshape(total, count), ((0, 0), (0, vec_rows * LANES - count)))
    g_extra = jnp.concatenate(
        [
            g_side_tail.reshape(total, side_rows, LANES),
            g_up_tail.reshape(total, up_rows, LANES),
            g_vec.reshape(total, vec_rows, LANES),
            jnp.zeros((total, tail_rows - used, LANES), jnp.bfloat16),
        ],
        axis=1,
    )
    g_qkv, g_out, g_extra, g_up, g_down = scatter_sums(
        g_qkv, g_out, g_extra, g_up, g_down, depth, main
    )
    g_side_tail = g_extra[:side_rows].reshape(tail, hidden)
    g_up_tail = g_extra[side_rows : side_rows + up_rows].reshape(CHIPS, tail, part)
    grad_vectors = g_extra[side_rows + up_rows : used].reshape(-1)[:count]
    grad_qkv = jnp.concatenate([g_qkv, g_side_tail[:, : 3 * width]], axis=0).reshape(-1)
    grad_out = jnp.concatenate([g_out, g_side_tail[:, 3 * width :]], axis=0).reshape(-1)
    grad_up = jnp.concatenate([g_up, g_up_tail], axis=1)
    grad_up = grad_up.reshape(CHIPS, own, depth, 2, wide_step)[..., :step]
    grad_up = grad_up.transpose(1, 2, 0, 3, 4).reshape(-1)
    grad_down = g_down[:step].reshape(-1)
    return (block_output, input_grad, grad_qkv, grad_out, grad_up, grad_down, grad_vectors)


def solution(mesh):
    in_specs = (
        P("dp", None),
        P("dp", None),
        P("dp", None),
        P("dp"),
        P("dp"),
        P("dp"),
        P("dp"),
        P("dp"),
    )
    out_specs = (P("dp", None), P("dp", None), P("dp"), P("dp"), P("dp"), P("dp"), P("dp"))
    total = mesh.shape["dp"]

    def body(*blocks):
        width = blocks[0].shape[1]
        own = width // total
        small = own % (2 * ROWS) * 4 * width
        tidy = total % (2 * GROUP) == 0 and width % total == 0 and own >= 2 * ROWS
        if tidy and small > 0 and small % LANES == 0:
            return body_group(*blocks)
        return body_flat(*blocks)

    return jax.shard_map(body, mesh=mesh, in_specs=in_specs, out_specs=out_specs, check_vma=False)
```

```python
import functools

import jax
import jax.numpy as jnp
from jax import lax
from jax.experimental import pallas as pl
from jax.experimental.pallas import tpu as pltpu
from jax.sharding import PartitionSpec as P

HEADS = 17
HEAD_DIM = 64


EPS = 1e-05
ROOT_HALF = 0.7071067811865476
INV_ROOT_TAU = 0.3989422804014327


def layer_norm(rows, gain, shift):
    mean = jnp.mean(rows, axis=1, keepdims=True)
    centered = rows - mean
    inverse = lax.rsqrt(jnp.mean(centered * centered, axis=1, keepdims=True) + EPS)
    normed = centered * inverse
    return (normed, inverse, normed * gain + shift)


def norm_back(grad_rows, normed, inverse, gain):
    scaled = grad_rows * gain
    inner = jnp.mean(scaled * normed, axis=1, keepdims=True)
    return inverse * (scaled - jnp.mean(scaled, axis=1, keepdims=True) - normed * inner)


def gelu_exact(value):
    return 0.5 * value * (1.0 + lax.erf(value * ROOT_HALF))


def gelu_slope(value):
    return (
        0.5 * (1.0 + lax.erf(value * ROOT_HALF))
        + value * jnp.exp(-0.5 * value * value) * INV_ROOT_TAU
    )


def causal_mask(lengths, rows):
    count = lengths.shape[0]
    order = jnp.arange(count, dtype=jnp.int32)
    ends = jnp.sum(jnp.where(order[:, None] <= order[None, :], lengths[:, None], 0), axis=0)
    position = jnp.arange(rows, dtype=jnp.int32)
    segment = jnp.sum((position[:, None] >= ends[None, :]).astype(jnp.int32), axis=1)
    return (segment[:, None] == segment[None, :]) & (position[None, :] <= position[:, None])


def score_block(query, keys, mask):
    scores = jnp.einsum("qhe,khe->hqk", query, keys, preferred_element_type=jnp.float32)
    return jnp.where(mask[None], scores, -1e30)


def shape_params(flat_parts, width):
    hidden = 4 * width
    return (
        flat_parts[0].reshape(width, 3 * width),
        flat_parts[1].reshape(width, width),
        flat_parts[2].reshape(width, hidden),
        flat_parts[3].reshape(hidden, width),
        flat_parts[4].astype(jnp.float32),
    )


def window_term(left_rows, right_rows, flat_start, flat_count):
    inner_len = left_rows.shape[1]
    columns = right_rows.shape[1]
    row_count = min(inner_len, flat_count // columns + 2)
    row_first = jnp.clip(flat_start // columns, 0, inner_len - row_count)
    product = lax.dot_general(
        left_rows, right_rows, (((0,), (0,)), ((), ())), preferred_element_type=jnp.float32
    ).reshape(-1)
    padded = jnp.concatenate([product, jnp.zeros((flat_count,), jnp.float32)])
    return lax.dynamic_slice_in_dim(padded, flat_start - row_first * columns, flat_count, 0)


def shard_terms(pairs, vector_grad, device_total):
    piece_lens = [
        left_rows.shape[1] * right_rows.shape[1] // device_total for left_rows, right_rows in pairs
    ]
    piece_lens = piece_lens + [vector_grad.shape[0] // device_total]
    shard_len = sum(piece_lens)

    def shard_term(start, count):
        dev_count = count // shard_len
        dev_first = start // shard_len
        pieces = []
        for (left_rows, right_rows), piece_len in zip(pairs, piece_lens):
            window = window_term(
                left_rows, right_rows, dev_first * piece_len, dev_count * piece_len
            )
            pieces.append(window.reshape(dev_count, piece_len))
        vec_len = piece_lens[-1]
        window = vector_grad
        pieces.append(window.reshape(dev_count, vec_len))
        return jnp.concatenate(pieces, axis=1).reshape(-1)

    return (shard_term, shard_len, piece_lens)


def split_shard(summed, piece_lens):
    outputs = []
    offset = 0
    for piece_len in piece_lens:
        outputs.append(summed[offset : offset + piece_len])
        offset = offset + piece_len
    return outputs


def fetch_flat(w_qkv, w_out, w_up, w_down, vectors, width):
    fetched = tuple(
        lax.all_gather(part, "dp", axis=0, tiled=True)
        for part in (w_qkv, w_out, w_up, w_down, vectors)
    )
    return shape_params(fetched, width)


def reduce_flat(pairs, g_vec, device_total):
    all_term, all_len, all_lens = shard_terms(pairs, g_vec, device_total)
    return split_shard(
        lax.psum_scatter(
            all_term(jnp.int32(0), all_len * device_total),
            "dp",
            scatter_dimension=0,
            tiled=True,
        ),
        all_lens,
    )


def body_flat(block_input, out_cotangent, seq_lengths, w_qkv, w_out, w_up, w_down, vectors):
    rows, width = block_input.shape
    hidden = 4 * width
    scale = HEAD_DIM ** (-0.5)
    device_total = lax.axis_size("dp")
    mask = causal_mask(seq_lengths[0], rows)
    wqkv, wo, wup, wdn, vec = fetch_flat(w_qkv, w_out, w_up, w_down, vectors, width)
    inputs = block_input.astype(jnp.float32)
    normed1, inverse1, pre1 = layer_norm(inputs, vec[0:width], vec[width : 2 * width])
    first = pre1.astype(jnp.bfloat16)
    qkv = jnp.dot(first, wqkv, preferred_element_type=jnp.float32)
    query = (
        ((qkv[:, 0:width] + vec[2 * width : 3 * width]) * scale)
        .astype(jnp.bfloat16)
        .reshape(rows, HEADS, HEAD_DIM)
    )
    keys = qkv[:, width : 2 * width].astype(jnp.bfloat16).reshape(rows, HEADS, HEAD_DIM)
    values = (
        (qkv[:, 2 * width : 3 * width] + vec[3 * width : 4 * width])
        .astype(jnp.bfloat16)
        .reshape(rows, HEADS, HEAD_DIM)
    )
    scores = score_block(query, keys, mask)
    peak = jnp.max(scores, axis=2, keepdims=True)
    logsum = peak + jnp.log(jnp.sum(jnp.exp(scores - peak), axis=2, keepdims=True))
    probs_low = jnp.exp(scores - logsum).astype(jnp.bfloat16)
    mixed = jnp.einsum("hqk,khe->qhe", probs_low, values, preferred_element_type=jnp.float32)
    mixed = mixed.astype(jnp.bfloat16).reshape(rows, width)
    resid = (
        inputs + jnp.dot(mixed, wo, preferred_element_type=jnp.float32) + vec[4 * width : 5 * width]
    )
    normed2, inverse2, pre2 = layer_norm(
        resid, vec[5 * width : 6 * width], vec[6 * width : 7 * width]
    )
    second = pre2.astype(jnp.bfloat16)
    upper = (
        jnp.dot(second, wup, preferred_element_type=jnp.float32)
        + vec[7 * width : 7 * width + hidden]
    )
    active = gelu_exact(upper).astype(jnp.bfloat16)
    output = (
        resid + jnp.dot(active, wdn, preferred_element_type=jnp.float32) + vec[7 * width + hidden :]
    )
    block_output = output.astype(jnp.bfloat16)
    back_w = (wqkv, wo, wup, wdn)
    bqkv, bwo, bwup, bwdn = back_w
    grad_top = out_cotangent.astype(jnp.float32)
    d_upper = jnp.dot(out_cotangent, bwdn.T, preferred_element_type=jnp.float32) * gelu_slope(upper)
    d_upper_low = d_upper.astype(jnp.bfloat16)
    d_second = jnp.dot(d_upper_low, bwup.T, preferred_element_type=jnp.float32)
    d_resid = grad_top + norm_back(d_second, normed2, inverse2, vec[5 * width : 6 * width])
    d_resid_low = d_resid.astype(jnp.bfloat16)
    d_mixed = jnp.dot(d_resid_low, bwo.T, preferred_element_type=jnp.float32).astype(jnp.bfloat16)
    d_mixed = d_mixed.reshape(rows, HEADS, HEAD_DIM)
    probs = jnp.exp(score_block(query, keys, mask) - logsum)
    probs_low = probs.astype(jnp.bfloat16)
    d_values = jnp.einsum("hqk,qhe->khe", probs_low, d_mixed, preferred_element_type=jnp.float32)
    d_probs = jnp.einsum("qhe,khe->hqk", d_mixed, values, preferred_element_type=jnp.float32)
    delta = jnp.sum(probs * d_probs, axis=2, keepdims=True)
    d_scores = (probs * (d_probs - delta)).astype(jnp.bfloat16)
    d_query = (
        jnp.einsum("hqk,khe->qhe", d_scores, keys, preferred_element_type=jnp.float32).reshape(
            rows, width
        )
        * scale
    )
    d_keys = jnp.einsum(
        "hqk,qhe->khe", d_scores, query, preferred_element_type=jnp.float32
    ).reshape(rows, width)
    d_values = d_values.reshape(rows, width)
    d_qkv = jnp.concatenate([d_query, d_keys, d_values], axis=1).astype(jnp.bfloat16)
    d_first = jnp.dot(d_qkv, bqkv.T, preferred_element_type=jnp.float32)
    input_grad = d_resid + norm_back(d_first, normed1, inverse1, vec[0:width])
    g_vec = jnp.concatenate(
        [
            jnp.sum(d_first * normed1, axis=0),
            jnp.sum(d_first, axis=0),
            jnp.sum(d_query, axis=0),
            jnp.sum(d_values, axis=0),
            jnp.sum(d_resid, axis=0),
            jnp.sum(d_second * normed2, axis=0),
            jnp.sum(d_second, axis=0),
            jnp.sum(d_upper, axis=0),
            jnp.sum(grad_top, axis=0),
        ]
    )
    pairs = [(first, d_qkv), (mixed, d_resid_low), (second, d_upper_low), (active, out_cotangent)]
    grad_qkv, grad_out, grad_up, grad_down, grad_vectors = reduce_flat(pairs, g_vec, device_total)
    return (block_output, input_grad, grad_qkv, grad_out, grad_up, grad_down, grad_vectors)


GROUP = 8
CHIPS = 4
ROWS = 16
LANES = 128
MESH = pl.DeviceIdType.MESH


def ceil_to(count, unit):
    return -(-count // unit) * unit


def gather_kernel(
    depth, s_in, t_in, u_in, d_in, c_in, s_all, t_all, u_all, d_all, c_all, *sems
):
    (
        local,
        z_send,
        z_recv,
        s_send,
        s_recv,
        half_send,
        half_recv,
        core_send,
        core_recv,
        t_send,
        t_recv,
        u_send,
        u_recv,
        c_send,
        c_recv,
    ) = sems
    me = lax.axis_index("dp")
    layer = me // GROUP
    chip = (me % GROUP) // 2
    core = me % 2
    east = chip % 2
    north = chip // 2
    chip_at = (
        chip,
        north * 2 + (1 - east),
        (1 - north) * 2 + east,
        (1 - north) * 2 + (1 - east),
    )
    mates = tuple(layer * GROUP + at * 2 + core for at in chip_at)
    twin = layer * GROUP + chip * 2 + (1 - core)
    above = me + GROUP
    below = me - GROUP
    has_above = layer < depth - 1
    has_below = layer > 0

    barrier = pltpu.get_barrier_semaphore()
    for device in mates[1:] + (twin,):
        pl.semaphore_signal(barrier, inc=1, device_id=(device,), device_id_type=MESH)

    @pl.when(has_above)
    def _():
        pl.semaphore_signal(barrier, inc=1, device_id=(above,), device_id_type=MESH)

    @pl.when(has_below)
    def _():
        pl.semaphore_signal(barrier, inc=1, device_id=(below,), device_id_type=MESH)

    ends = (layer + depth - 1) // depth + (2 * depth - 2 - layer) // depth
    pl.semaphore_wait(barrier, CHIPS + ends)

    def send(source, target, send_sem, recv_sem, device):
        return pltpu.make_async_remote_copy(
            src_ref=source,
            dst_ref=target,
            send_sem=send_sem,
            recv_sem=recv_sem,
            device_id=(device,),
            device_id_type=MESH,
        )

    def layer_of(slot):
        return lax.rem(layer + slot, depth)

    def s_at(slot):
        return s_in if slot == 0 else s_all.at[0, 0, slot]

    def t_at(slot):
        return t_in if slot == 0 else t_all.at[layer_of(slot), chip, core]

    def d_at(slot):
        return d_in if slot == 0 else d_all.at[layer_of(slot), core]

    def u_at(slot):
        return u_all.at[0, :, slot]

    def s_to(slot, source):
        return s_all.at[0, 0, slot]

    def t_to(slot, source):
        return t_all.at[layer_of(source), chip, core]

    def d_to(slot, source):
        return d_all.at[layer_of(source), core]

    def u_to(slot, source):
        return u_all.at[0, :, slot]

    places = {"t": (0, t_at, t_to), "s": (1, s_at, s_to), "d": (2, d_at, d_to), "u": (3, u_at, u_to)}

    def z_copy(name, slot, up):
        index, source, target = places[name]
        there = (slot - 1) % depth if up else (slot + 1) % depth
        return send(
            source(slot),
            target(there, slot),
            z_send.at[index, slot, 0 if up else 1],
            z_recv.at[index, there],
            above if up else below,
        )

    def z_arrival(name, slot):
        index, source, target = places[name]
        here = target(slot, slot)
        return send(here, here, z_send.at[index, slot, 0], z_recv.at[index, slot], above)

    def routes():
        found = [(0, True, has_above), (0, False, has_below)]
        for far in range(1, depth - 1):
            found.append((depth - far, True, (layer >= far) & has_above))
            found.append((far, False, (layer + far < depth) & has_below))
        return found

    def z_forward(name, step):
        for slot, up, allowed in routes()[2 * step : 2 * step + 2]:

            @pl.when(allowed)
            def _(slot=slot, up=up):
                z_copy(name, slot, up).start()

    def z_land(name, far, then=None):
        for slot, came in ((depth - far, layer >= far), (far, layer + far < depth)):

            @pl.when(came)
            def _(slot=slot):
                z_arrival(name, slot).wait_recv()
                if then is not None:
                    then(slot)

    def s_plane(slot, way):
        return send(
            s_at(slot), s_all.at[0, way, slot], s_send.at[way, slot], s_recv.at[way, slot], mates[way]
        )

    def s_half(slot, way):
        rows = s_in.shape[0] // 2
        part = pl.ds(0 if way == 1 else rows, rows)
        return send(
            s_all.at[0, way, slot, part],
            s_all.at[0, 3, slot, part],
            half_send.at[way, slot],
            half_recv.at[way, slot],
            mates[3 - way],
        )

    def s_core(slot, way):
        source = s_at(slot) if way == 0 else s_all.at[0, way, slot]
        return send(
            source, s_all.at[1, way, slot], core_send.at[way, slot], core_recv.at[way, slot], twin
        )

    def s_spread(slot):
        s_plane(slot, 1).start()
        s_plane(slot, 2).start()
        s_core(slot, 0).start()

    def s_pass(slot):
        for way in (1, 2):
            s_plane(slot, way).wait_recv()
            s_half(slot, way).start()
            s_core(slot, way).start()

    def s_close(slot):
        for way in (1, 2):
            s_half(slot, way).wait_recv()
        s_core(slot, 3).start()

    def by_distance(far, act):
        if far == 0:
            act(0)
            return
        for slot, came in ((depth - far, layer >= far), (far, layer + far < depth)):

            @pl.when(came)
            def _(slot=slot):
                act(slot)

    def d_core(slot):
        return send(
            d_at(slot), d_to(slot, slot), core_send.at[4, slot], core_recv.at[4, slot], twin
        )

    def u_core(slot):
        return send(
            u_at(slot), u_all.at[1, :, slot], core_send.at[5, slot], core_recv.at[5, slot], twin
        )

    def d_twin_arrival(slot):
        here = d_all.at[layer_of(slot), 1 - core]
        return send(here, here, core_send.at[4, slot], core_recv.at[4, slot], twin)

    t_mine = t_all.at[:, chip, core]

    def t_plane(way):
        return send(t_mine, t_mine, t_send.at[way], t_recv.at[way], mates[way])

    def t_plane_arrival(way):
        here = t_all.at[:, chip_at[way], core]
        return send(here, here, t_send.at[way], t_recv.at[way], mates[way])

    t_core_block = t_all.at[:, :, core]
    t_twin_block = t_all.at[:, :, 1 - core]
    t_core = send(t_core_block, t_core_block, t_send.at[0], t_recv.at[0], twin)
    t_core_arrival = send(t_twin_block, t_twin_block, t_send.at[0], t_recv.at[0], twin)

    def u_plane(way):
        return send(
            u_in.at[chip_at[way]], u_all.at[0, way, 0], u_send.at[way], u_recv.at[way], mates[way]
        )

    def c_plane(way):
        return send(c_in, c_all.at[way], c_send.at[way], c_recv.at[way], mates[way])

    stay = [
        pltpu.make_async_copy(t_in, t_all.at[layer, chip, core], local.at[0]),
        pltpu.make_async_copy(u_in.at[chip], u_all.at[0, 0, 0], local.at[1]),
        pltpu.make_async_copy(s_in, s_all.at[0, 0, 0], local.at[2]),
        pltpu.make_async_copy(d_in, d_all.at[layer, core], local.at[3]),
        pltpu.make_async_copy(c_in, c_all.at[0], local.at[4]),
    ]

    z_forward("t", 0)
    z_forward("s", 0)
    for copy in stay:
        copy.start()
    for way in (1, 2, 3):
        u_plane(way).start()
    s_spread(0)
    for far in range(1, depth):
        z_land("t", far)
        if far < depth - 1:
            z_forward("t", far)
        z_land("s", far)
        if far < depth - 1:
            z_forward("s", far)
        if far == 1:
            z_forward("d", 0)
        by_distance(far, s_spread)
        if far == depth - 1:
            stay[0].wait()
            for way in (1, 2, 3):
                t_plane(way).start()
        if far == min(2, depth - 1):
            for way in (1, 2, 3):
                u_plane(way).wait_recv()
            stay[1].wait()
            z_forward("u", 0)
            u_core(0).start()
            d_core(0).start()
        by_distance(far - 1, s_pass)
    for way in (1, 2, 3):
        c_plane(way).start()
    for far in range(1, depth):
        z_land("d", far)
        if far < depth - 1:
            z_forward("d", far)
        by_distance(far, lambda slot: d_core(slot).start())
        if far == 1:
            by_distance(depth - 1, s_pass)
            for way in (1, 2, 3):
                t_plane_arrival(way).wait_recv()
            t_core.start()
        z_land("u", far)
        if far < depth - 1:
            z_forward("u", far)
        by_distance(far, lambda slot: u_core(slot).start())
        if far == 1:
            for near in range(depth):
                by_distance(near, s_close)
    for slot in range(depth):
        for way in range(CHIPS):
            s_core(slot, way).wait()
        u_core(slot).wait()
        d_core(slot).wait_send()
        d_twin_arrival(slot).wait_recv()
        for way in (1, 2):
            s_plane(slot, way).wait_send()
            s_half(slot, way).wait_send()
    for way in (1, 2, 3):
        u_plane(way).wait_send()
        t_plane(way).wait_send()
        c_plane(way).wait()
    t_core.wait_send()
    t_core_arrival.wait_recv()
    for copy in stay[2:]:
        copy.wait()
    for slot, up, allowed in routes():

        @pl.when(allowed)
        def _(slot=slot, up=up):
            for name in places:
                z_copy(name, slot, up).wait_send()


def gather_all(s_own, t_own, u_own, d_own, c_own, depth):
    low = jnp.bfloat16
    return pl.pallas_call(
        functools.partial(gather_kernel, depth),
        out_shape=[
            jax.ShapeDtypeStruct((2, CHIPS, depth) + s_own.shape, low),
            jax.ShapeDtypeStruct((depth, CHIPS, 2) + t_own.shape, low),
            jax.ShapeDtypeStruct((2, CHIPS, depth) + u_own.shape[1:], low),
            jax.ShapeDtypeStruct((depth, 2) + d_own.shape, low),
            jax.ShapeDtypeStruct((CHIPS,) + c_own.shape, low),
        ],
        in_specs=[pl.BlockSpec(memory_space=pl.ANY)] * 5,
        out_specs=[pl.BlockSpec(memory_space=pl.ANY)] * 5,
        scratch_shapes=[
            pltpu.SemaphoreType.DMA((5,)),
            pltpu.SemaphoreType.DMA((4, depth, 2)),
            pltpu.SemaphoreType.DMA((4, depth)),
            pltpu.SemaphoreType.DMA((3, depth)),
            pltpu.SemaphoreType.DMA((3, depth)),
            pltpu.SemaphoreType.DMA((3, depth)),
            pltpu.SemaphoreType.DMA((3, depth)),
            pltpu.SemaphoreType.DMA((6, depth)),
            pltpu.SemaphoreType.DMA((6, depth)),
            pltpu.SemaphoreType.DMA((4,)),
            pltpu.SemaphoreType.DMA((4,)),
            pltpu.SemaphoreType.DMA((4,)),
            pltpu.SemaphoreType.DMA((4,)),
            pltpu.SemaphoreType.DMA((4,)),
            pltpu.SemaphoreType.DMA((4,)),
        ],
        compiler_params=pltpu.CompilerParams(collective_id=0, has_side_effects=True),
        name="gather_params",
    )(s_own, t_own, u_own, d_own, c_own)


def add_blocks(count, pick, other):
    @pl.loop(0, count)
    def _(at):
        here, term = pick(at), other(at)
        here[...] = (here[...].astype(jnp.float32) + term[...].astype(jnp.float32)).astype(here.dtype)


def scatter_kernel(depth, *refs):
    ins, outs, refs = refs[:7], refs[7:12], refs[12:]
    (
        acc_q,
        out_q,
        rc_q,
        p1_q,
        p2_q,
        z_q,
        acc_o,
        out_o,
        rc_o,
        p1_o,
        p2_o,
        z_o,
        acc_u,
        rc_u,
        z_u,
        fin_u,
        out_u,
        in_u,
        acc_d,
        rc_d,
        z_d,
        acc_t,
        rc_t,
        p_t,
        fin_t,
        z_t,
        local,
        c_send,
        c_recv,
        p_send,
        p_recv,
        t_send,
        t_recv,
        z_send,
        z_recv,
        a_send,
        a_recv,
    ) = refs
    q_left, q_right, o_left, o_right, t_in, u_in, d_in = ins
    q_out, o_out, t_out, u_out, d_out = outs
    me = lax.axis_index("dp")
    layer = me // GROUP
    chip = (me % GROUP) // 2
    core = me % 2
    east = chip % 2
    north = chip // 2
    chip_at = (
        chip,
        north * 2 + (1 - east),
        (1 - north) * 2 + east,
        (1 - north) * 2 + (1 - east),
    )
    mates = tuple(layer * GROUP + at * 2 + core for at in chip_at)
    twin = layer * GROUP + chip * 2 + (1 - core)
    above = me + GROUP
    below = me - GROUP

    barrier = pltpu.get_barrier_semaphore()
    for device in mates[1:] + (twin,):
        pl.semaphore_signal(barrier, inc=1, device_id=(device,), device_id_type=MESH)

    @pl.when(layer < depth - 1)
    def _():
        pl.semaphore_signal(barrier, inc=1, device_id=(above,), device_id_type=MESH)

    @pl.when(layer > 0)
    def _():
        pl.semaphore_signal(barrier, inc=1, device_id=(below,), device_id_type=MESH)

    ends = (layer + depth - 1) // depth + (2 * depth - 2 - layer) // depth
    pl.semaphore_wait(barrier, CHIPS + ends)

    def send(source, target, send_sem, recv_sem, device):
        return pltpu.make_async_remote_copy(
            src_ref=source,
            dst_ref=target,
            send_sem=send_sem,
            recv_sem=recv_sem,
            device_id=(device,),
            device_id_type=MESH,
        )

    def layer_of(slot):
        return lax.rem(layer + slot, depth)

    bulk = ((0, out_q, acc_q, rc_q, p1_q, p2_q), (1, out_o, acc_o, rc_o, p1_o, p2_o))
    half = p1_q.shape[3]

    def products(left, right, place, other):
        across = place.shape[2] * place.shape[3]
        for at in range(CHIPS):
            first = (other * CHIPS + at) * across
            block = contract_rows(left[:, first : first + across], right[...])
            place[at // 2, at % 2] = lower(block).reshape(place.shape[2:])

    stay = [
        pltpu.make_async_copy(u_in.at[0], acc_u, local.at[0]),
        pltpu.make_async_copy(d_in.at[:, core], acc_d, local.at[1]),
        pltpu.make_async_copy(t_in.at[:, :, core], acc_t, local.at[2]),
    ]
    u_core = send(u_in.at[1], rc_u, c_send.at[2, 0], c_recv.at[2, 0], twin)
    d_core = send(d_in.at[:, 1 - core], rc_d, c_send.at[3, 0], c_recv.at[3, 0], twin)
    t_core = send(t_in.at[:, :, 1 - core], rc_t, c_send.at[4, 0], c_recv.at[4, 0], twin)

    def b_core(item, slot):
        index, whole, acc, rc, p1, p2 = item
        return send(
            whole.at[:, :, slot],
            rc.at[:, :, slot],
            c_send.at[index, slot],
            c_recv.at[index, slot],
            twin,
        )

    def b_first(item, slot, side):
        index, whole, acc, rc, p1, p2 = item
        if side == 0:
            source = acc.at[1, :, slot, pl.ds(0, half)]
        else:
            source = acc.at[:, 1, slot, pl.ds(half, half)]
        at = (index * 2 + side) * 2
        return send(
            source, p1.at[side, :, slot], p_send.at[at, slot], p_recv.at[at, slot], mates[2 - side]
        )

    def b_second(item, slot, side):
        index, whole, acc, rc, p1, p2 = item
        if side == 0:
            source = acc.at[0, 1, slot, pl.ds(0, half)]
        else:
            source = acc.at[1, 0, slot, pl.ds(half, half)]
        at = (index * 2 + side) * 2 + 1
        return send(
            source, p2.at[side, slot], p_send.at[at, slot], p_recv.at[at, slot], mates[1 + side]
        )

    def open_slot(slot):
        for item in bulk:
            index, whole, acc, rc, p1, p2 = item
            b_core(item, slot).wait_recv()
            add_blocks(
                CHIPS,
                lambda at, acc=acc: acc.at[at // 2, at % 2, slot],
                lambda at, rc=rc: rc.at[at // 2, at % 2, slot],
            )
            b_first(item, slot, 0).start()
            b_first(item, slot, 1).start()

    def middle_slot(slot):
        for item in bulk:
            index, whole, acc, rc, p1, p2 = item
            b_first(item, slot, 0).wait_recv()
            add_blocks(
                2,
                lambda at, acc=acc: acc.at[0, at, slot, pl.ds(0, half)],
                lambda at, p1=p1: p1.at[0, at, slot],
            )
            b_second(item, slot, 0).start()
            b_first(item, slot, 1).wait_recv()
            add_blocks(
                2,
                lambda at, acc=acc: acc.at[at, 0, slot, pl.ds(half, half)],
                lambda at, p1=p1: p1.at[1, at, slot],
            )
            b_second(item, slot, 1).start()

    def close_slot(slot):
        for item in bulk:
            index, whole, acc, rc, p1, p2 = item
            for side in (0, 1):
                b_second(item, slot, side).wait_recv()
                add_blocks(
                    1,
                    lambda at, acc=acc, side=side: acc.at[0, 0, slot, pl.ds(side * half, half)],
                    lambda at, p2=p2, side=side: p2.at[side, slot],
                )

    chains = (
        (0, lambda slot: acc_q.at[0, 0, slot], z_q, q_out),
        (1, lambda slot: acc_o.at[0, 0, slot], z_o, o_out),
        (2, lambda slot: acc_u.at[:, slot], z_u, fin_u),
        (3, lambda slot: acc_d.at[layer_of(slot)], z_d, d_out),
        (4, lambda slot: fin_t.at[layer_of(slot)], z_t, t_out),
    )

    def z_up(chain, step):
        index, block, landing, final = chain
        return send(
            block(depth - step),
            landing.at[0, step],
            z_send.at[index, 0, step],
            z_recv.at[index, 0, step],
            above,
        )

    def z_down(chain, step):
        index, block, landing, final = chain
        return send(
            block(step),
            landing.at[1, step],
            z_send.at[index, 1, step],
            z_recv.at[index, 1, step],
            below,
        )

    def z_start(chain, step):
        @pl.when(layer < step)
        def _():
            z_up(chain, step).start()

        @pl.when(layer >= depth - step)
        def _():
            z_down(chain, step).start()

    def z_take(chain, step):
        index, block, landing, final = chain
        last = step == depth - 1
        if last:
            final[...] = block(0)[...].astype(jnp.float32)
        targets = (depth - step - 1, (step + 1) % depth)
        came = (
            (layer >= 1) & (layer <= step),
            (layer <= depth - 2) & (layer >= depth - step - 1),
        )
        for way, make in enumerate((z_up, z_down)):

            @pl.when(came[way])
            def _(way=way, make=make):
                make(chain, step).wait_recv()
                here = final if last else block(targets[way])
                total = here[...].astype(jnp.float32) + landing[way, step].astype(jnp.float32)
                here[...] = total.astype(here.dtype)

    def z_next(chain, step):
        z_take(chain, step)
        if step < depth - 1:
            z_start(chain, step + 1)

    def t_plane(way):
        return send(
            acc_t.at[:, chip_at[way]], p_t.at[way], t_send.at[way], t_recv.at[way], mates[way]
        )

    def u_turn(way):
        return send(out_u.at[way], in_u.at[way], a_send.at[way], a_recv.at[way], mates[way])

    chain_q, chain_o, chain_u, chain_d, chain_t = chains
    order = tuple(range(1, depth)) + (0,)
    u_core.start()
    d_core.start()
    for copy in stay:
        copy.start()
    t_core.start()
    products(o_left, o_right, out_o, 1)
    products(q_left, q_right, out_q, 1)
    for slot in order:
        for item in bulk:
            b_core(item, slot).start()

    u_core.wait_recv()
    stay[0].wait()
    add_blocks(
        CHIPS * depth,
        lambda at: acc_u.at[at // depth, at % depth],
        lambda at: rc_u.at[at // depth, at % depth],
    )
    z_start(chain_u, 1)
    d_core.wait_recv()
    stay[1].wait()
    add_blocks(depth, lambda at: acc_d.at[at], lambda at: rc_d.at[at])
    z_start(chain_d, 1)
    products(o_left, o_right, acc_o, 0)
    products(q_left, q_right, acc_q, 0)
    open_slot(order[0])
    open_slot(order[1])
    t_core.wait_recv()
    stay[2].wait()
    add_blocks(
        CHIPS * depth,
        lambda at: acc_t.at[at // CHIPS, at % CHIPS],
        lambda at: rc_t.at[at // CHIPS, at % CHIPS],
    )
    for way in (1, 2, 3):
        t_plane(way).start()
    z_steps = [(chain, step) for step in range(1, depth) for chain in (chain_u, chain_d)]
    taken = 0
    for at in range(depth):
        if taken < len(z_steps):
            z_next(*z_steps[taken])
            taken = taken + 1
        middle_slot(order[at])
        if at + 2 < depth:
            open_slot(order[at + 2])
        if at >= 1:
            close_slot(order[at - 1])
    for way in (1, 2, 3):
        t_plane(way).wait_recv()

    @pl.loop(0, depth)
    def _(at):
        total = acc_t[at, chip].astype(jnp.float32)
        for way in (1, 2, 3):
            total = total + p_t[way, at].astype(jnp.float32)
        fin_t[at] = total.astype(jnp.bfloat16)

    z_start(chain_t, 1)
    close_slot(order[depth - 1])
    z_start(chain_q, 1)
    z_start(chain_o, 1)
    for chain, step in z_steps[taken:]:
        z_next(chain, step)
    for way in (1, 2, 3):
        out_u[way] = fin_u[way].astype(jnp.bfloat16)
        u_turn(way).start()
    for step in range(1, depth):
        for chain in (chain_t, chain_q, chain_o):
            z_next(chain, step)
    u_out[chip] = fin_u[0]
    for way in (1, 2, 3):
        u_turn(way).wait_recv()
        u_out[chip_at[way]] = in_u[way].astype(jnp.float32)

    for copy in (u_core, d_core, t_core):
        copy.wait_send()
    for slot in range(depth):
        for item in bulk:
            b_core(item, slot).wait_send()
            for side in (0, 1):
                b_first(item, slot, side).wait_send()
                b_second(item, slot, side).wait_send()
    for way in (1, 2, 3):
        t_plane(way).wait_send()
        u_turn(way).wait_send()
    for step in range(1, depth):

        @pl.when(layer < step)
        def _(step=step):
            for chain in chains:
                z_up(chain, step).wait_send()

        @pl.when(layer >= depth - step)
        def _(step=step):
            for chain in chains:
                z_down(chain, step).wait_send()


def scatter_sums(q_left, q_right, o_left, o_right, t_part, u_part, d_part, depth, main):
    low, full = jnp.bfloat16, jnp.float32
    half = main // 2

    def bulk_scratch(columns):
        return [
            pltpu.VMEM((2, 2, depth, main, columns), low),
            pltpu.VMEM((2, 2, depth, main, columns), low),
            pltpu.VMEM((2, 2, depth, main, columns), low),
            pltpu.VMEM((2, 2, depth, half, columns), low),
            pltpu.VMEM((2, depth, half, columns), low),
            pltpu.VMEM((2, depth, main, columns), low),
        ]

    q_columns, o_columns, u_columns = q_right.shape[1], o_right.shape[1], u_part.shape[1]
    down = d_part.shape[2:]
    small = t_part.shape[1:]
    dma = pltpu.SemaphoreType.DMA
    return pl.pallas_call(
        functools.partial(scatter_kernel, depth),
        out_shape=[
            jax.ShapeDtypeStruct((main, q_columns), full),
            jax.ShapeDtypeStruct((main, o_columns), full),
            jax.ShapeDtypeStruct(small, full),
            jax.ShapeDtypeStruct((CHIPS, main, u_columns), full),
            jax.ShapeDtypeStruct(down, full),
        ],
        in_specs=[pl.BlockSpec(memory_space=pltpu.VMEM)] * 4
        + [pl.BlockSpec(memory_space=pl.ANY)] * 3,
        out_specs=[pl.BlockSpec(memory_space=pltpu.VMEM)] * 5,
        scratch_shapes=bulk_scratch(q_columns)
        + bulk_scratch(o_columns)
        + [
            pltpu.VMEM((CHIPS, depth, main, u_columns), low),
            pltpu.VMEM((CHIPS, depth, main, u_columns), low),
            pltpu.VMEM((2, depth, CHIPS, main, u_columns), low),
            pltpu.VMEM((CHIPS, main, u_columns), full),
            pltpu.VMEM((CHIPS, main, u_columns), low),
            pltpu.VMEM((CHIPS, main, u_columns), low),
            pltpu.VMEM((depth,) + down, low),
            pltpu.VMEM((depth,) + down, low),
            pltpu.VMEM((2, depth) + down, low),
            pltpu.VMEM((depth, CHIPS) + small, low),
            pltpu.VMEM((depth, CHIPS) + small, low),
            pltpu.VMEM((CHIPS, depth) + small, low),
            pltpu.VMEM((depth,) + small, low),
            pltpu.VMEM((2, depth) + small, low),
            dma((3,)),
            dma((5, depth)),
            dma((5, depth)),
            dma((8, depth)),
            dma((8, depth)),
            dma((4,)),
            dma((4,)),
            dma((5, 2, depth)),
            dma((5, 2, depth)),
            dma((4,)),
            dma((4,)),
        ],
        compiler_params=pltpu.CompilerParams(
            collective_id=1, has_side_effects=True, vmem_limit_bytes=56 * 2**20
        ),
        name="scatter_sums",
    )(
        q_left,
        q_right,
        o_left,
        o_right,
        t_part.reshape((depth, CHIPS, 2) + small),
        u_part.reshape(2, CHIPS, depth, main, u_columns),
        d_part,
    )


def lower(value):
    return value.astype(jnp.bfloat16)


def wide(value):
    return value.astype(jnp.float32)


def contract_rows(left, right):
    return lax.dot_general(left, right, (((0,), (0,)), ((), ())), preferred_element_type=jnp.float32)


def contract_columns(left, right):
    return lax.dot_general(left, right, (((1,), (1,)), ((), ())), preferred_element_type=jnp.float32)


def multiply(left, right):
    return jnp.dot(left, right, preferred_element_type=jnp.float32)


def middle_kernel(*refs):
    second, onehot, bias, u_hbm, t_hbm, d_hbm, c_hbm = refs[:7]
    d_second, lifted, g_up, g_tail, g_down, g_bias = refs[7:13]
    (
        w_up,
        w_tail,
        w_down,
        cots,
        tokens,
        slopes,
        active,
        spread,
        steep,
        y_out,
        y_in,
        s_out,
        s_in,
        local,
        h_send,
        h_recv,
        y_send,
        y_recv,
        s_send,
        s_recv,
    ) = refs[13:]
    rows = second.shape[0]
    bulk = w_up.shape[0]
    me = lax.axis_index("dp")
    layer = me // GROUP
    chip = (me % GROUP) // 2
    core = me % 2
    east = chip % 2
    north = chip // 2
    chip_at = (
        chip,
        north * 2 + (1 - east),
        (1 - north) * 2 + east,
        (1 - north) * 2 + (1 - east),
    )
    mates = tuple(layer * GROUP + at * 2 + core for at in chip_at)
    barrier = pltpu.get_barrier_semaphore()
    for device in mates[1:]:
        pl.semaphore_signal(barrier, inc=1, device_id=(device,), device_id_type=MESH)
    loads = [
        pltpu.make_async_copy(d_hbm, w_down, local.at[0]),
        pltpu.make_async_copy(c_hbm, cots, local.at[1]),
        pltpu.make_async_copy(u_hbm, w_up, local.at[2]),
        pltpu.make_async_copy(t_hbm, w_tail, local.at[3]),
    ]
    for load in loads:
        load.start()
    pl.semaphore_wait(barrier, CHIPS - 1)

    def send(source, target, send_sem, recv_sem, way):
        return pltpu.make_async_remote_copy(
            src_ref=source,
            dst_ref=target,
            send_sem=send_sem.at[way],
            recv_sem=recv_sem.at[way],
            device_id=(mates[way],),
            device_id_type=MESH,
        )

    ways = (1, 2, 3)
    hidden = {way: send(second, tokens.at[way], h_send, h_recv, way) for way in ways}
    lifts = {way: send(y_out.at[way], y_in.at[way], y_send, y_recv, way) for way in ways}
    backs = {way: send(s_out.at[way], s_in.at[way], s_send, s_recv, way) for way in ways}
    for way in (1, 2, 3):
        hidden[way].start()
    tokens[0] = second[...]
    loads[0].wait()
    loads[1].wait()
    slopes[...] = contract_columns(cots[...], w_down[...])
    loads[2].wait()
    loads[3].wait()
    for way in range(CHIPS):
        if way > 0:
            hidden[way].wait_recv()
        span = pl.ds(way * rows, rows)
        mine = lower(multiply(tokens[way], onehot[...]))
        spread[span] = mine
        upper = multiply(mine[:, :bulk], w_up[...]) + multiply(mine[:, bulk:], w_tail[...])
        upper = upper + bias[...]
        phi = 0.5 * (1.0 + lax.erf(upper * ROOT_HALF))
        active[span] = lower(upper * phi)
        steep_rows = slopes[span] * (phi + upper * jnp.exp(-0.5 * upper * upper) * INV_ROOT_TAU)
        slopes[span] = steep_rows
        steep[span] = lower(steep_rows)
        back = jnp.concatenate(
            [contract_columns(steep[span], w_up[...]), contract_columns(steep[span], w_tail[...])],
            axis=1,
        )
        s_out[way] = lower(contract_columns(lower(back), onehot[...]))
        if way > 0:
            backs[way].start()
        y_out[way] = lower(multiply(active[span], w_down[...]))
        if way > 0:
            lifts[way].start()
    g_bias[...] = jnp.sum(slopes[...], axis=0, keepdims=True)
    g_up[...] = lower(contract_rows(spread[:, :bulk], steep[...]))
    g_tail[...] = lower(contract_rows(spread[:, bulk:], steep[...]))
    g_down[...] = lower(contract_rows(active[...], cots[...]))
    total = wide(s_out[0])
    for way in (1, 2, 3):
        backs[way].wait_recv()
        total = total + wide(s_in[way])
    d_second[...] = total
    total = wide(y_out[0])
    for way in (1, 2, 3):
        lifts[way].wait_recv()
        total = total + wide(y_in[way])
    lifted[...] = total
    for way in (1, 2, 3):
        hidden[way].wait_send()
        backs[way].wait_send()
        lifts[way].wait_send()


def middle(second, onehot, bias, w_up, w_tail, w_down, cots):
    rows, width = second.shape
    part = w_down.shape[0]
    bulk, left = w_up.shape[0], w_tail.shape[0]
    group = CHIPS * rows
    low, full = jnp.bfloat16, jnp.float32
    vmem = pl.BlockSpec(memory_space=pltpu.VMEM)
    dma = pltpu.SemaphoreType.DMA
    return pl.pallas_call(
        middle_kernel,
        out_shape=[
            jax.ShapeDtypeStruct((rows, width), full),
            jax.ShapeDtypeStruct((rows, width), full),
            jax.ShapeDtypeStruct((bulk, part), low),
            jax.ShapeDtypeStruct((left, part), low),
            jax.ShapeDtypeStruct((part, width), low),
            jax.ShapeDtypeStruct((1, part), full),
        ],
        in_specs=[vmem] * 3 + [pl.BlockSpec(memory_space=pl.ANY)] * 4,
        out_specs=[vmem] * 6,
        scratch_shapes=[
            pltpu.VMEM((bulk, part), low),
            pltpu.VMEM((left, part), low),
            pltpu.VMEM((part, width), low),
            pltpu.VMEM((group, width), low),
            pltpu.VMEM((CHIPS, rows, width), low),
            pltpu.VMEM((group, part), full),
            pltpu.VMEM((group, part), low),
            pltpu.VMEM((group, width), low),
            pltpu.VMEM((group, part), low),
            pltpu.VMEM((CHIPS, rows, width), low),
            pltpu.VMEM((CHIPS, rows, width), low),
            pltpu.VMEM((CHIPS, rows, width), low),
            pltpu.VMEM((CHIPS, rows, width), low),
            dma((4,)),
        ]
        + [dma((CHIPS,))] * 6,
        compiler_params=pltpu.CompilerParams(
            collective_id=2, has_side_effects=True, vmem_limit_bytes=50 * 2**20
        ),
        name="middle",
    )(second, onehot, bias, w_up, w_tail, w_down, cots)


def two_parts(value):
    high = lax.reduce_precision(value, 8, 7)
    return jnp.concatenate([lower(high), lower(value - high)], axis=0)


def body_group(block_input, out_cotangent, seq_lengths, w_qkv, w_out, w_up, w_down, vectors):
    rows, width = block_input.shape
    hidden = 4 * width
    scale = HEAD_DIM ** (-0.5)
    total = lax.axis_size("dp")
    depth = total // GROUP
    own = width // total
    main = own // (2 * ROWS) * (2 * ROWS)
    tail = own - main
    step = hidden // total
    wide_step = ceil_to(step, ROWS)
    part = total // CHIPS * wide_step
    count = vectors.shape[0]
    me = lax.axis_index("dp")
    layer = me // GROUP
    chip = (me // 2) % CHIPS
    core = me % 2
    mask = causal_mask(seq_lengths[0], rows)

    side = jnp.concatenate([w_qkv.reshape(own, 3 * width), w_out.reshape(own, width)], axis=1)
    upper_own = jnp.pad(
        w_up.reshape(own, depth, CHIPS, 2, step), ((0, 0),) * 4 + ((0, wide_step - step),)
    )
    upper_own = upper_own.transpose(2, 0, 1, 3, 4).reshape(CHIPS, own, part)
    down_own = jnp.pad(w_down.reshape(step, width), ((0, wide_step - step), (0, 0)))
    side_rows = tail * hidden // LANES
    up_rows = tail * CHIPS * part // LANES
    vec_rows = ceil_to(count, LANES) // LANES
    used = side_rows + up_rows + vec_rows
    tail_rows = ceil_to(used, ROWS)
    extra = jnp.concatenate(
        [
            side[main:].reshape(side_rows, LANES),
            upper_own[:, main:].reshape(up_rows, LANES),
            jnp.pad(vectors, (0, vec_rows * LANES - count)).reshape(vec_rows, LANES),
            jnp.zeros((tail_rows - used, LANES), jnp.bfloat16),
        ],
        axis=0,
    )
    s_all, t_all, u_all, d_all, c_all = gather_all(
        side[:main], extra, upper_own[:, :main], down_own, out_cotangent, depth
    )
    bulk = total * main
    w_side = s_all.reshape(bulk, hidden)
    w_upper = u_all.reshape(bulk, part)
    w_lower = d_all.reshape(part, width)
    cots = c_all.reshape(CHIPS * rows, width)
    t_all = t_all.reshape(total, tail_rows, LANES)
    side_tail = t_all[:, :side_rows].reshape(total * tail, hidden)
    up_tail = t_all[:, side_rows : side_rows + up_rows].reshape(total, CHIPS, tail, part)
    up_tail = lax.dynamic_index_in_dim(up_tail, chip, 1, keepdims=False)
    up_tail = up_tail.reshape(total * tail, part)
    vec = t_all[:, side_rows + up_rows : used].reshape(total, vec_rows * LANES)[:, :count]
    vec = wide(vec.reshape(-1))
    bias_up = vec[7 * width : 7 * width + hidden].reshape(depth, CHIPS, 2, step)
    bias_up = lax.dynamic_index_in_dim(bias_up, chip, 1, keepdims=False)
    bias_up = jnp.pad(bias_up, ((0, 0), (0, 0), (0, wide_step - step))).reshape(1, part)

    place = jnp.arange(width, dtype=jnp.int32)
    slot = place // main
    there = (layer + slot % depth) % depth * GROUP
    there = there + jnp.bitwise_xor(chip, slot // depth % CHIPS) * 2
    there = there + jnp.bitwise_xor(core, slot // (depth * CHIPS))
    late = place - bulk
    origin = jnp.where(
        place < bulk, there * own + place % main, late // tail * own + main + late % tail
    )
    onehot = lower(place[:, None] == origin[None, :])

    def permute(value):
        return lower(multiply(value, onehot))

    def restore(value):
        return lower(contract_columns(value, onehot))

    def restore_wide(value):
        both = contract_columns(two_parts(value), onehot)
        return both[:rows] + both[rows:]

    wq, wo = w_side[:, : 3 * width], w_side[:, 3 * width :]
    wq_tail, wo_tail = side_tail[:, : 3 * width], side_tail[:, 3 * width :]

    inputs = wide(block_input)
    normed1, inverse1, pre1 = layer_norm(inputs, vec[0:width], vec[width : 2 * width])
    first = permute(lower(pre1))
    qkv = multiply(first[:, :bulk], wq) + multiply(first[:, bulk:], wq_tail)
    query = lower((qkv[:, 0:width] + vec[2 * width : 3 * width]) * scale)
    query = query.reshape(rows, HEADS, HEAD_DIM)
    keys = lower(qkv[:, width : 2 * width]).reshape(rows, HEADS, HEAD_DIM)
    values = lower(qkv[:, 2 * width : 3 * width] + vec[3 * width : 4 * width])
    values = values.reshape(rows, HEADS, HEAD_DIM)
    scores = score_block(query, keys, mask)
    peak = jnp.max(scores, axis=2, keepdims=True)
    logsum = peak + jnp.log(jnp.sum(jnp.exp(scores - peak), axis=2, keepdims=True))
    probs_low = lower(jnp.exp(scores - logsum))
    mixed = jnp.einsum("hqk,khe->qhe", probs_low, values, preferred_element_type=jnp.float32)
    mixed = permute(lower(mixed).reshape(rows, width))
    resid = inputs + multiply(mixed[:, :bulk], wo) + multiply(mixed[:, bulk:], wo_tail)
    resid = resid + vec[4 * width : 5 * width]
    gain2 = vec[5 * width : 6 * width]
    normed2, inverse2, pre2 = layer_norm(resid, gain2, vec[6 * width : 7 * width])
    second = lower(pre2)
    d_second, lifted, g_up, g_up_tail, g_down, d_bias_up = middle(
        second, onehot, bias_up, w_upper, up_tail, w_lower, cots
    )
    block_output = lower(resid + lifted + vec[7 * width + hidden :])
    g_down = g_down.reshape(depth, 2, wide_step, width)
    turn = jnp.arange(CHIPS, dtype=jnp.int32)
    g_up_tail = g_up_tail.reshape(total, tail * part // LANES, LANES)
    g_up_tail = jnp.concatenate(
        [jnp.where(chip == at, g_up_tail, jnp.bfloat16(0)) for at in range(CHIPS)], axis=1
    )
    g_up_tail = lax.optimization_barrier(g_up_tail)

    grad_top = wide(out_cotangent)
    d_resid = grad_top + norm_back(d_second, normed2, inverse2, gain2)
    d_resid_low = lower(d_resid)
    g_out_tail = contract_rows(mixed[:, bulk:], d_resid_low)
    d_mixed = jnp.concatenate(
        [contract_columns(d_resid_low, wo), contract_columns(d_resid_low, wo_tail)], axis=1
    )
    d_mixed = restore(lower(d_mixed)).reshape(rows, HEADS, HEAD_DIM)
    probs = jnp.exp(score_block(query, keys, mask) - logsum)
    probs_low = lower(probs)
    d_values = jnp.einsum("hqk,qhe->khe", probs_low, d_mixed, preferred_element_type=jnp.float32)
    d_probs = jnp.einsum("qhe,khe->hqk", d_mixed, values, preferred_element_type=jnp.float32)
    delta = jnp.sum(probs * d_probs, axis=2, keepdims=True)
    d_scores = lower(probs * (d_probs - delta))
    d_query = jnp.einsum("hqk,khe->qhe", d_scores, keys, preferred_element_type=jnp.float32)
    d_query = d_query.reshape(rows, width) * scale
    d_keys = jnp.einsum("hqk,qhe->khe", d_scores, query, preferred_element_type=jnp.float32)
    d_keys = d_keys.reshape(rows, width)
    d_values = d_values.reshape(rows, width)
    d_qkv = lower(jnp.concatenate([d_query, d_keys, d_values], axis=1))
    g_qkv_tail = contract_rows(first[:, bulk:], d_qkv)
    d_first = jnp.concatenate(
        [contract_columns(d_qkv, wq), contract_columns(d_qkv, wq_tail)], axis=1
    )
    d_first = restore_wide(d_first)
    input_grad = d_resid + norm_back(d_first, normed1, inverse1, vec[0:width])

    d_bias_up = d_bias_up.reshape(depth, 1, 2, wide_step)[..., :step]
    d_bias_up = jnp.where(turn[None, :, None, None] == chip, d_bias_up, 0.0)
    g_vec = jnp.concatenate(
        [
            jnp.sum(d_first * normed1, axis=0),
            jnp.sum(d_first, axis=0),
            jnp.sum(d_query, axis=0),
            jnp.sum(d_values, axis=0),
            jnp.sum(d_resid, axis=0),
            jnp.sum(d_second * normed2, axis=0),
            jnp.sum(d_second, axis=0),
            d_bias_up.reshape(hidden),
            jnp.sum(grad_top, axis=0),
        ]
    )
    g_side_tail = jnp.concatenate([lower(g_qkv_tail), lower(g_out_tail)], axis=1)
    g_side_tail = lax.optimization_barrier(g_side_tail)
    g_side_tail = lax.optimization_barrier(g_side_tail.reshape(total, side_rows, LANES))
    g_vec = jnp.pad(lower(g_vec).reshape(total, count), ((0, 0), (0, vec_rows * LANES - count)))
    g_extra = jnp.concatenate(
        [
            g_side_tail,
            g_up_tail,
            g_vec.reshape(total, vec_rows, LANES),
            jnp.zeros((total, tail_rows - used, LANES), jnp.bfloat16),
        ],
        axis=1,
    )
    g_extra = lax.optimization_barrier(g_extra)
    g_qkv, g_out, g_extra, g_up, g_down = scatter_sums(
        first[:, :bulk],
        d_qkv,
        mixed[:, :bulk],
        d_resid_low,
        g_extra,
        g_up,
        g_down,
        depth,
        main,
    )
    g_side_tail = g_extra[:side_rows].reshape(tail, hidden)
    g_up_tail = g_extra[side_rows : side_rows + up_rows].reshape(CHIPS, tail, part)
    grad_vectors = g_extra[side_rows + up_rows : used].reshape(-1)[:count]
    grad_qkv = jnp.concatenate([g_qkv, g_side_tail[:, : 3 * width]], axis=0).reshape(-1)
    grad_out = jnp.concatenate([g_out, g_side_tail[:, 3 * width :]], axis=0).reshape(-1)
    grad_up = jnp.concatenate([g_up, g_up_tail], axis=1)
    grad_up = grad_up.reshape(CHIPS, own, depth, 2, wide_step)[..., :step]
    grad_up = grad_up.transpose(1, 2, 0, 3, 4).reshape(-1)
    grad_down = g_down[:step].reshape(-1)
    return (block_output, input_grad, grad_qkv, grad_out, grad_up, grad_down, grad_vectors)


def solution(mesh):
    in_specs = (
        P("dp", None),
        P("dp", None),
        P("dp", None),
        P("dp"),
        P("dp"),
        P("dp"),
        P("dp"),
        P("dp"),
    )
    out_specs = (P("dp", None), P("dp", None), P("dp"), P("dp"), P("dp"), P("dp"), P("dp"))
    total = mesh.shape["dp"]

    def body(*blocks):
        width = blocks[0].shape[1]
        own = width // total
        small = own % (2 * ROWS) * 4 * width
        tidy = total % (2 * GROUP) == 0 and width % total == 0 and own >= 2 * ROWS
        if tidy and small > 0 and small % LANES == 0:
            return body_group(*blocks)
        return body_flat(*blocks)

    return jax.shard_map(body, mesh=mesh, in_specs=in_specs, out_specs=out_specs, check_vma=False)
```

```python
import functools

import jax
import jax.numpy as jnp
from jax import lax
from jax.experimental import pallas as pl
from jax.experimental.pallas import tpu as pltpu
from jax.sharding import PartitionSpec as P

HEADS = 17
HEAD_DIM = 64


EPS = 1e-05
ROOT_HALF = 0.7071067811865476
INV_ROOT_TAU = 0.3989422804014327


def layer_norm(rows, gain, shift):
    mean = jnp.mean(rows, axis=1, keepdims=True)
    centered = rows - mean
    inverse = lax.rsqrt(jnp.mean(centered * centered, axis=1, keepdims=True) + EPS)
    normed = centered * inverse
    return (normed, inverse, normed * gain + shift)


def norm_back(grad_rows, normed, inverse, gain):
    scaled = grad_rows * gain
    inner = jnp.mean(scaled * normed, axis=1, keepdims=True)
    return inverse * (scaled - jnp.mean(scaled, axis=1, keepdims=True) - normed * inner)


def gelu_exact(value):
    return 0.5 * value * (1.0 + lax.erf(value * ROOT_HALF))


def gelu_slope(value):
    return (
        0.5 * (1.0 + lax.erf(value * ROOT_HALF))
        + value * jnp.exp(-0.5 * value * value) * INV_ROOT_TAU
    )


def causal_mask(lengths, rows):
    count = lengths.shape[0]
    order = jnp.arange(count, dtype=jnp.int32)
    ends = jnp.sum(jnp.where(order[:, None] <= order[None, :], lengths[:, None], 0), axis=0)
    position = jnp.arange(rows, dtype=jnp.int32)
    segment = jnp.sum((position[:, None] >= ends[None, :]).astype(jnp.int32), axis=1)
    return (segment[:, None] == segment[None, :]) & (position[None, :] <= position[:, None])


def score_block(query, keys, mask):
    scores = jnp.einsum("qhe,khe->hqk", query, keys, preferred_element_type=jnp.float32)
    return jnp.where(mask[None], scores, -1e30)


def shape_params(flat_parts, width):
    hidden = 4 * width
    return (
        flat_parts[0].reshape(width, 3 * width),
        flat_parts[1].reshape(width, width),
        flat_parts[2].reshape(width, hidden),
        flat_parts[3].reshape(hidden, width),
        flat_parts[4].astype(jnp.float32),
    )


def window_term(left_rows, right_rows, flat_start, flat_count):
    inner_len = left_rows.shape[1]
    columns = right_rows.shape[1]
    row_count = min(inner_len, flat_count // columns + 2)
    row_first = jnp.clip(flat_start // columns, 0, inner_len - row_count)
    product = lax.dot_general(
        left_rows, right_rows, (((0,), (0,)), ((), ())), preferred_element_type=jnp.float32
    ).reshape(-1)
    padded = jnp.concatenate([product, jnp.zeros((flat_count,), jnp.float32)])
    return lax.dynamic_slice_in_dim(padded, flat_start - row_first * columns, flat_count, 0)


def shard_terms(pairs, vector_grad, device_total):
    piece_lens = [
        left_rows.shape[1] * right_rows.shape[1] // device_total for left_rows, right_rows in pairs
    ]
    piece_lens = piece_lens + [vector_grad.shape[0] // device_total]
    shard_len = sum(piece_lens)

    def shard_term(start, count):
        dev_count = count // shard_len
        dev_first = start // shard_len
        pieces = []
        for (left_rows, right_rows), piece_len in zip(pairs, piece_lens):
            window = window_term(
                left_rows, right_rows, dev_first * piece_len, dev_count * piece_len
            )
            pieces.append(window.reshape(dev_count, piece_len))
        vec_len = piece_lens[-1]
        window = vector_grad
        pieces.append(window.reshape(dev_count, vec_len))
        return jnp.concatenate(pieces, axis=1).reshape(-1)

    return (shard_term, shard_len, piece_lens)


def split_shard(summed, piece_lens):
    outputs = []
    offset = 0
    for piece_len in piece_lens:
        outputs.append(summed[offset : offset + piece_len])
        offset = offset + piece_len
    return outputs


def fetch_flat(w_qkv, w_out, w_up, w_down, vectors, width):
    fetched = tuple(
        lax.all_gather(part, "dp", axis=0, tiled=True)
        for part in (w_qkv, w_out, w_up, w_down, vectors)
    )
    return shape_params(fetched, width)


def reduce_flat(pairs, g_vec, device_total):
    all_term, all_len, all_lens = shard_terms(pairs, g_vec, device_total)
    return split_shard(
        lax.psum_scatter(
            all_term(jnp.int32(0), all_len * device_total),
            "dp",
            scatter_dimension=0,
            tiled=True,
        ),
        all_lens,
    )


def body_flat(block_input, out_cotangent, seq_lengths, w_qkv, w_out, w_up, w_down, vectors):
    rows, width = block_input.shape
    hidden = 4 * width
    scale = HEAD_DIM ** (-0.5)
    device_total = lax.axis_size("dp")
    mask = causal_mask(seq_lengths[0], rows)
    wqkv, wo, wup, wdn, vec = fetch_flat(w_qkv, w_out, w_up, w_down, vectors, width)
    inputs = block_input.astype(jnp.float32)
    normed1, inverse1, pre1 = layer_norm(inputs, vec[0:width], vec[width : 2 * width])
    first = pre1.astype(jnp.bfloat16)
    qkv = jnp.dot(first, wqkv, preferred_element_type=jnp.float32)
    query = (
        ((qkv[:, 0:width] + vec[2 * width : 3 * width]) * scale)
        .astype(jnp.bfloat16)
        .reshape(rows, HEADS, HEAD_DIM)
    )
    keys = qkv[:, width : 2 * width].astype(jnp.bfloat16).reshape(rows, HEADS, HEAD_DIM)
    values = (
        (qkv[:, 2 * width : 3 * width] + vec[3 * width : 4 * width])
        .astype(jnp.bfloat16)
        .reshape(rows, HEADS, HEAD_DIM)
    )
    scores = score_block(query, keys, mask)
    peak = jnp.max(scores, axis=2, keepdims=True)
    logsum = peak + jnp.log(jnp.sum(jnp.exp(scores - peak), axis=2, keepdims=True))
    probs_low = jnp.exp(scores - logsum).astype(jnp.bfloat16)
    mixed = jnp.einsum("hqk,khe->qhe", probs_low, values, preferred_element_type=jnp.float32)
    mixed = mixed.astype(jnp.bfloat16).reshape(rows, width)
    resid = (
        inputs + jnp.dot(mixed, wo, preferred_element_type=jnp.float32) + vec[4 * width : 5 * width]
    )
    normed2, inverse2, pre2 = layer_norm(
        resid, vec[5 * width : 6 * width], vec[6 * width : 7 * width]
    )
    second = pre2.astype(jnp.bfloat16)
    upper = (
        jnp.dot(second, wup, preferred_element_type=jnp.float32)
        + vec[7 * width : 7 * width + hidden]
    )
    active = gelu_exact(upper).astype(jnp.bfloat16)
    output = (
        resid + jnp.dot(active, wdn, preferred_element_type=jnp.float32) + vec[7 * width + hidden :]
    )
    block_output = output.astype(jnp.bfloat16)
    back_w = (wqkv, wo, wup, wdn)
    bqkv, bwo, bwup, bwdn = back_w
    grad_top = out_cotangent.astype(jnp.float32)
    d_upper = jnp.dot(out_cotangent, bwdn.T, preferred_element_type=jnp.float32) * gelu_slope(upper)
    d_upper_low = d_upper.astype(jnp.bfloat16)
    d_second = jnp.dot(d_upper_low, bwup.T, preferred_element_type=jnp.float32)
    d_resid = grad_top + norm_back(d_second, normed2, inverse2, vec[5 * width : 6 * width])
    d_resid_low = d_resid.astype(jnp.bfloat16)
    d_mixed = jnp.dot(d_resid_low, bwo.T, preferred_element_type=jnp.float32).astype(jnp.bfloat16)
    d_mixed = d_mixed.reshape(rows, HEADS, HEAD_DIM)
    probs = jnp.exp(score_block(query, keys, mask) - logsum)
    probs_low = probs.astype(jnp.bfloat16)
    d_values = jnp.einsum("hqk,qhe->khe", probs_low, d_mixed, preferred_element_type=jnp.float32)
    d_probs = jnp.einsum("qhe,khe->hqk", d_mixed, values, preferred_element_type=jnp.float32)
    delta = jnp.sum(probs * d_probs, axis=2, keepdims=True)
    d_scores = (probs * (d_probs - delta)).astype(jnp.bfloat16)
    d_query = (
        jnp.einsum("hqk,khe->qhe", d_scores, keys, preferred_element_type=jnp.float32).reshape(
            rows, width
        )
        * scale
    )
    d_keys = jnp.einsum(
        "hqk,qhe->khe", d_scores, query, preferred_element_type=jnp.float32
    ).reshape(rows, width)
    d_values = d_values.reshape(rows, width)
    d_qkv = jnp.concatenate([d_query, d_keys, d_values], axis=1).astype(jnp.bfloat16)
    d_first = jnp.dot(d_qkv, bqkv.T, preferred_element_type=jnp.float32)
    input_grad = d_resid + norm_back(d_first, normed1, inverse1, vec[0:width])
    g_vec = jnp.concatenate(
        [
            jnp.sum(d_first * normed1, axis=0),
            jnp.sum(d_first, axis=0),
            jnp.sum(d_query, axis=0),
            jnp.sum(d_values, axis=0),
            jnp.sum(d_resid, axis=0),
            jnp.sum(d_second * normed2, axis=0),
            jnp.sum(d_second, axis=0),
            jnp.sum(d_upper, axis=0),
            jnp.sum(grad_top, axis=0),
        ]
    )
    pairs = [(first, d_qkv), (mixed, d_resid_low), (second, d_upper_low), (active, out_cotangent)]
    grad_qkv, grad_out, grad_up, grad_down, grad_vectors = reduce_flat(pairs, g_vec, device_total)
    return (block_output, input_grad, grad_qkv, grad_out, grad_up, grad_down, grad_vectors)


GROUP = 8
CHIPS = 4
ROWS = 16
LANES = 128
MESH = pl.DeviceIdType.MESH


def ceil_to(count, unit):
    return -(-count // unit) * unit


def gather_kernel(
    depth, s_in, t_in, u_in, d_in, c_in, s_all, t_all, u_all, d_all, c_all, *sems
):
    (
        local,
        z_send,
        z_recv,
        s_send,
        s_recv,
        half_send,
        half_recv,
        core_send,
        core_recv,
        t_send,
        t_recv,
        u_send,
        u_recv,
        c_send,
        c_recv,
    ) = sems
    me = lax.axis_index("dp")
    layer = me // GROUP
    chip = (me % GROUP) // 2
    core = me % 2
    east = chip % 2
    north = chip // 2
    chip_at = (
        chip,
        north * 2 + (1 - east),
        (1 - north) * 2 + east,
        (1 - north) * 2 + (1 - east),
    )
    mates = tuple(layer * GROUP + at * 2 + core for at in chip_at)
    twin = layer * GROUP + chip * 2 + (1 - core)
    above = me + GROUP
    below = me - GROUP
    has_above = layer < depth - 1
    has_below = layer > 0

    barrier = pltpu.get_barrier_semaphore()
    for device in mates[1:] + (twin,):
        pl.semaphore_signal(barrier, inc=1, device_id=(device,), device_id_type=MESH)

    @pl.when(has_above)
    def _():
        pl.semaphore_signal(barrier, inc=1, device_id=(above,), device_id_type=MESH)

    @pl.when(has_below)
    def _():
        pl.semaphore_signal(barrier, inc=1, device_id=(below,), device_id_type=MESH)

    ends = (layer + depth - 1) // depth + (2 * depth - 2 - layer) // depth
    pl.semaphore_wait(barrier, CHIPS + ends)

    def send(source, target, send_sem, recv_sem, device):
        return pltpu.make_async_remote_copy(
            src_ref=source,
            dst_ref=target,
            send_sem=send_sem,
            recv_sem=recv_sem,
            device_id=(device,),
            device_id_type=MESH,
        )

    def layer_of(slot):
        return lax.rem(layer + slot, depth)

    def s_at(slot):
        return s_in if slot == 0 else s_all.at[0, 0, slot]

    def t_at(slot):
        return t_in if slot == 0 else t_all.at[layer_of(slot), chip, core]

    def d_at(slot):
        return d_in if slot == 0 else d_all.at[layer_of(slot), core]

    def u_at(slot):
        return u_all.at[0, :, slot]

    def s_to(slot, source):
        return s_all.at[0, 0, slot]

    def t_to(slot, source):
        return t_all.at[layer_of(source), chip, core]

    def d_to(slot, source):
        return d_all.at[layer_of(source), core]

    def u_to(slot, source):
        return u_all.at[0, :, slot]

    places = {"t": (0, t_at, t_to), "s": (1, s_at, s_to), "d": (2, d_at, d_to), "u": (3, u_at, u_to)}

    def z_copy(name, slot, up):
        index, source, target = places[name]
        there = (slot - 1) % depth if up else (slot + 1) % depth
        return send(
            source(slot),
            target(there, slot),
            z_send.at[index, slot, 0 if up else 1],
            z_recv.at[index, there],
            above if up else below,
        )

    def z_arrival(name, slot):
        index, source, target = places[name]
        here = target(slot, slot)
        return send(here, here, z_send.at[index, slot, 0], z_recv.at[index, slot], above)

    def routes():
        found = [(0, True, has_above), (0, False, has_below)]
        for far in range(1, depth - 1):
            found.append((depth - far, True, (layer >= far) & has_above))
            found.append((far, False, (layer + far < depth) & has_below))
        return found

    def z_forward(name, step):
        for slot, up, allowed in routes()[2 * step : 2 * step + 2]:

            @pl.when(allowed)
            def _(slot=slot, up=up):
                z_copy(name, slot, up).start()

    def z_land(name, far, then=None):
        for slot, came in ((depth - far, layer >= far), (far, layer + far < depth)):

            @pl.when(came)
            def _(slot=slot):
                z_arrival(name, slot).wait_recv()
                if then is not None:
                    then(slot)

    def s_plane(slot, way):
        return send(
            s_at(slot), s_all.at[0, way, slot], s_send.at[way, slot], s_recv.at[way, slot], mates[way]
        )

    def s_half(slot, way):
        rows = s_in.shape[0] // 2
        part = pl.ds(0 if way == 1 else rows, rows)
        return send(
            s_all.at[0, way, slot, part],
            s_all.at[0, 3, slot, part],
            half_send.at[way, slot],
            half_recv.at[way, slot],
            mates[3 - way],
        )

    def s_core(slot, way):
        source = s_at(slot) if way == 0 else s_all.at[0, way, slot]
        return send(
            source, s_all.at[1, way, slot], core_send.at[way, slot], core_recv.at[way, slot], twin
        )

    def s_spread(slot):
        s_plane(slot, 1).start()
        s_plane(slot, 2).start()
        s_core(slot, 0).start()

    def s_pass(slot):
        for way in (1, 2):
            s_plane(slot, way).wait_recv()
            s_half(slot, way).start()
            s_core(slot, way).start()

    def s_close(slot):
        for way in (1, 2):
            s_half(slot, way).wait_recv()
        s_core(slot, 3).start()

    def by_distance(far, act):
        if far == 0:
            act(0)
            return
        for slot, came in ((depth - far, layer >= far), (far, layer + far < depth)):

            @pl.when(came)
            def _(slot=slot):
                act(slot)

    def d_core(slot):
        return send(
            d_at(slot), d_to(slot, slot), core_send.at[4, slot], core_recv.at[4, slot], twin
        )

    def u_core(slot):
        return send(
            u_at(slot), u_all.at[1, :, slot], core_send.at[5, slot], core_recv.at[5, slot], twin
        )

    def d_twin_arrival(slot):
        here = d_all.at[layer_of(slot), 1 - core]
        return send(here, here, core_send.at[4, slot], core_recv.at[4, slot], twin)

    t_mine = t_all.at[:, chip, core]

    def t_plane(way):
        return send(t_mine, t_mine, t_send.at[way], t_recv.at[way], mates[way])

    def t_plane_arrival(way):
        here = t_all.at[:, chip_at[way], core]
        return send(here, here, t_send.at[way], t_recv.at[way], mates[way])

    t_core_block = t_all.at[:, :, core]
    t_twin_block = t_all.at[:, :, 1 - core]
    t_core = send(t_core_block, t_core_block, t_send.at[0], t_recv.at[0], twin)
    t_core_arrival = send(t_twin_block, t_twin_block, t_send.at[0], t_recv.at[0], twin)

    def u_plane(way):
        return send(
            u_in.at[chip_at[way]], u_all.at[0, way, 0], u_send.at[way], u_recv.at[way], mates[way]
        )

    def c_plane(way):
        return send(c_in, c_all.at[way], c_send.at[way], c_recv.at[way], mates[way])

    stay = [
        pltpu.make_async_copy(t_in, t_all.at[layer, chip, core], local.at[0]),
        pltpu.make_async_copy(u_in.at[chip], u_all.at[0, 0, 0], local.at[1]),
        pltpu.make_async_copy(s_in, s_all.at[0, 0, 0], local.at[2]),
        pltpu.make_async_copy(d_in, d_all.at[layer, core], local.at[3]),
        pltpu.make_async_copy(c_in, c_all.at[0], local.at[4]),
    ]

    z_forward("t", 0)
    z_forward("s", 0)
    for copy in stay:
        copy.start()
    for way in (1, 2, 3):
        u_plane(way).start()
    s_spread(0)
    for far in range(1, depth):
        z_land("t", far)
        if far < depth - 1:
            z_forward("t", far)
        z_land("s", far)
        if far < depth - 1:
            z_forward("s", far)
        if far == 1:
            z_forward("d", 0)
        by_distance(far, s_spread)
        if far == depth - 1:
            stay[0].wait()
            for way in (1, 2, 3):
                t_plane(way).start()
        if far == min(2, depth - 1):
            for way in (1, 2, 3):
                u_plane(way).wait_recv()
            stay[1].wait()
            z_forward("u", 0)
            u_core(0).start()
            d_core(0).start()
        by_distance(far - 1, s_pass)
    for way in (1, 2, 3):
        c_plane(way).start()
    for far in range(1, depth):
        z_land("d", far)
        if far < depth - 1:
            z_forward("d", far)
        by_distance(far, lambda slot: d_core(slot).start())
        if far == 1:
            by_distance(depth - 1, s_pass)
            for way in (1, 2, 3):
                t_plane_arrival(way).wait_recv()
            t_core.start()
        z_land("u", far)
        if far < depth - 1:
            z_forward("u", far)
        by_distance(far, lambda slot: u_core(slot).start())
        if far == 1:
            for near in range(depth):
                by_distance(near, s_close)
    for slot in range(depth):
        for way in range(CHIPS):
            s_core(slot, way).wait()
        u_core(slot).wait()
        d_core(slot).wait_send()
        d_twin_arrival(slot).wait_recv()
        for way in (1, 2):
            s_plane(slot, way).wait_send()
            s_half(slot, way).wait_send()
    for way in (1, 2, 3):
        u_plane(way).wait_send()
        t_plane(way).wait_send()
        c_plane(way).wait()
    t_core.wait_send()
    t_core_arrival.wait_recv()
    for copy in stay[2:]:
        copy.wait()
    for slot, up, allowed in routes():

        @pl.when(allowed)
        def _(slot=slot, up=up):
            for name in places:
                z_copy(name, slot, up).wait_send()


def gather_all(s_own, t_own, u_own, d_own, c_own, depth):
    low = jnp.bfloat16
    return pl.pallas_call(
        functools.partial(gather_kernel, depth),
        out_shape=[
            jax.ShapeDtypeStruct((2, CHIPS, depth) + s_own.shape, low),
            jax.ShapeDtypeStruct((depth, CHIPS, 2) + t_own.shape, low),
            jax.ShapeDtypeStruct((2, CHIPS, depth) + u_own.shape[1:], low),
            jax.ShapeDtypeStruct((depth, 2) + d_own.shape, low),
            jax.ShapeDtypeStruct((CHIPS,) + c_own.shape, low),
        ],
        in_specs=[pl.BlockSpec(memory_space=pl.ANY)] * 5,
        out_specs=[pl.BlockSpec(memory_space=pl.ANY)] * 5,
        scratch_shapes=[
            pltpu.SemaphoreType.DMA((5,)),
            pltpu.SemaphoreType.DMA((4, depth, 2)),
            pltpu.SemaphoreType.DMA((4, depth)),
            pltpu.SemaphoreType.DMA((3, depth)),
            pltpu.SemaphoreType.DMA((3, depth)),
            pltpu.SemaphoreType.DMA((3, depth)),
            pltpu.SemaphoreType.DMA((3, depth)),
            pltpu.SemaphoreType.DMA((6, depth)),
            pltpu.SemaphoreType.DMA((6, depth)),
            pltpu.SemaphoreType.DMA((4,)),
            pltpu.SemaphoreType.DMA((4,)),
            pltpu.SemaphoreType.DMA((4,)),
            pltpu.SemaphoreType.DMA((4,)),
            pltpu.SemaphoreType.DMA((4,)),
            pltpu.SemaphoreType.DMA((4,)),
        ],
        compiler_params=pltpu.CompilerParams(collective_id=0, has_side_effects=True),
        name="gather_params",
    )(s_own, t_own, u_own, d_own, c_own)


def add_blocks(count, pick, other):
    @pl.loop(0, count)
    def _(at):
        here, term = pick(at), other(at)
        here[...] = (here[...].astype(jnp.float32) + term[...].astype(jnp.float32)).astype(here.dtype)


def scatter_kernel(depth, *refs):
    ins, outs, refs = refs[:7], refs[7:12], refs[12:]
    (
        acc_q,
        out_q,
        rc_q,
        p1_q,
        p2_q,
        z_q,
        acc_o,
        out_o,
        rc_o,
        p1_o,
        p2_o,
        z_o,
        acc_u,
        rc_u,
        z_u,
        fin_u,
        out_u,
        in_u,
        acc_d,
        rc_d,
        z_d,
        acc_t,
        rc_t,
        p_t,
        fin_t,
        z_t,
        local,
        c_send,
        c_recv,
        p_send,
        p_recv,
        t_send,
        t_recv,
        z_send,
        z_recv,
        a_send,
        a_recv,
    ) = refs
    q_left, q_right, o_left, o_right, t_in, u_in, d_in = ins
    q_out, o_out, t_out, u_out, d_out = outs
    me = lax.axis_index("dp")
    layer = me // GROUP
    chip = (me % GROUP) // 2
    core = me % 2
    east = chip % 2
    north = chip // 2
    chip_at = (
        chip,
        north * 2 + (1 - east),
        (1 - north) * 2 + east,
        (1 - north) * 2 + (1 - east),
    )
    mates = tuple(layer * GROUP + at * 2 + core for at in chip_at)
    twin = layer * GROUP + chip * 2 + (1 - core)
    above = me + GROUP
    below = me - GROUP

    barrier = pltpu.get_barrier_semaphore()
    for device in mates[1:] + (twin,):
        pl.semaphore_signal(barrier, inc=1, device_id=(device,), device_id_type=MESH)

    @pl.when(layer < depth - 1)
    def _():
        pl.semaphore_signal(barrier, inc=1, device_id=(above,), device_id_type=MESH)

    @pl.when(layer > 0)
    def _():
        pl.semaphore_signal(barrier, inc=1, device_id=(below,), device_id_type=MESH)

    ends = (layer + depth - 1) // depth + (2 * depth - 2 - layer) // depth
    pl.semaphore_wait(barrier, CHIPS + ends)

    def send(source, target, send_sem, recv_sem, device):
        return pltpu.make_async_remote_copy(
            src_ref=source,
            dst_ref=target,
            send_sem=send_sem,
            recv_sem=recv_sem,
            device_id=(device,),
            device_id_type=MESH,
        )

    def layer_of(slot):
        return lax.rem(layer + slot, depth)

    bulk = ((0, out_q, acc_q, rc_q, p1_q, p2_q), (1, out_o, acc_o, rc_o, p1_o, p2_o))
    half = p1_q.shape[3]

    def products(left, right, place, other):
        across = place.shape[2] * place.shape[3]
        for at in range(CHIPS):
            first = (other * CHIPS + at) * across
            block = contract_rows(left[:, first : first + across], right[...])
            place[at // 2, at % 2] = lower(block).reshape(place.shape[2:])

    stay = [
        pltpu.make_async_copy(u_in.at[0], acc_u, local.at[0]),
        pltpu.make_async_copy(d_in.at[:, core], acc_d, local.at[1]),
        pltpu.make_async_copy(t_in.at[:, :, core], acc_t, local.at[2]),
    ]
    u_core = send(u_in.at[1], rc_u, c_send.at[2, 0], c_recv.at[2, 0], twin)
    d_core = send(d_in.at[:, 1 - core], rc_d, c_send.at[3, 0], c_recv.at[3, 0], twin)
    t_core = send(t_in.at[:, :, 1 - core], rc_t, c_send.at[4, 0], c_recv.at[4, 0], twin)

    def b_core(item, slot):
        index, whole, acc, rc, p1, p2 = item
        return send(
            whole.at[:, :, slot],
            rc.at[:, :, slot],
            c_send.at[index, slot],
            c_recv.at[index, slot],
            twin,
        )

    def b_first(item, slot, side):
        index, whole, acc, rc, p1, p2 = item
        if side == 0:
            source = acc.at[1, :, slot, pl.ds(0, half)]
        else:
            source = acc.at[:, 1, slot, pl.ds(half, half)]
        at = (index * 2 + side) * 2
        return send(
            source, p1.at[side, :, slot], p_send.at[at, slot], p_recv.at[at, slot], mates[2 - side]
        )

    def b_second(item, slot, side):
        index, whole, acc, rc, p1, p2 = item
        if side == 0:
            source = acc.at[0, 1, slot, pl.ds(0, half)]
        else:
            source = acc.at[1, 0, slot, pl.ds(half, half)]
        at = (index * 2 + side) * 2 + 1
        return send(
            source, p2.at[side, slot], p_send.at[at, slot], p_recv.at[at, slot], mates[1 + side]
        )

    def open_slot(slot):
        for item in bulk:
            index, whole, acc, rc, p1, p2 = item
            b_core(item, slot).wait_recv()
            add_blocks(
                CHIPS,
                lambda at, acc=acc: acc.at[at // 2, at % 2, slot],
                lambda at, rc=rc: rc.at[at // 2, at % 2, slot],
            )
            b_first(item, slot, 0).start()
            b_first(item, slot, 1).start()

    def middle_slot(slot):
        for item in bulk:
            index, whole, acc, rc, p1, p2 = item
            b_first(item, slot, 0).wait_recv()
            add_blocks(
                2,
                lambda at, acc=acc: acc.at[0, at, slot, pl.ds(0, half)],
                lambda at, p1=p1: p1.at[0, at, slot],
            )
            b_second(item, slot, 0).start()
            b_first(item, slot, 1).wait_recv()
            add_blocks(
                2,
                lambda at, acc=acc: acc.at[at, 0, slot, pl.ds(half, half)],
                lambda at, p1=p1: p1.at[1, at, slot],
            )
            b_second(item, slot, 1).start()

    def close_slot(slot):
        for item in bulk:
            index, whole, acc, rc, p1, p2 = item
            for side in (0, 1):
                b_second(item, slot, side).wait_recv()
                add_blocks(
                    1,
                    lambda at, acc=acc, side=side: acc.at[0, 0, slot, pl.ds(side * half, half)],
                    lambda at, p2=p2, side=side: p2.at[side, slot],
                )

    chains = (
        (0, lambda slot: acc_q.at[0, 0, slot], z_q, q_out),
        (1, lambda slot: acc_o.at[0, 0, slot], z_o, o_out),
        (2, lambda slot: acc_u.at[:, slot], z_u, fin_u),
        (3, lambda slot: acc_d.at[layer_of(slot)], z_d, d_out),
        (4, lambda slot: fin_t.at[layer_of(slot)], z_t, t_out),
    )

    def z_up(chain, step):
        index, block, landing, final = chain
        return send(
            block(depth - step),
            landing.at[0, step],
            z_send.at[index, 0, step],
            z_recv.at[index, 0, step],
            above,
        )

    def z_down(chain, step):
        index, block, landing, final = chain
        return send(
            block(step),
            landing.at[1, step],
            z_send.at[index, 1, step],
            z_recv.at[index, 1, step],
            below,
        )

    def z_start(chain, step):
        @pl.when(layer < step)
        def _():
            z_up(chain, step).start()

        @pl.when(layer >= depth - step)
        def _():
            z_down(chain, step).start()

    def z_take(chain, step):
        index, block, landing, final = chain
        last = step == depth - 1
        if last:
            final[...] = block(0)[...].astype(jnp.float32)
        targets = (depth - step - 1, (step + 1) % depth)
        came = (
            (layer >= 1) & (layer <= step),
            (layer <= depth - 2) & (layer >= depth - step - 1),
        )
        for way, make in enumerate((z_up, z_down)):

            @pl.when(came[way])
            def _(way=way, make=make):
                make(chain, step).wait_recv()
                here = final if last else block(targets[way])
                total = here[...].astype(jnp.float32) + landing[way, step].astype(jnp.float32)
                here[...] = total.astype(here.dtype)

    def z_next(chain, step):
        z_take(chain, step)
        if step < depth - 1:
            z_start(chain, step + 1)

    def t_plane(way):
        return send(
            acc_t.at[:, chip_at[way]], p_t.at[way], t_send.at[way], t_recv.at[way], mates[way]
        )

    def u_turn(way):
        return send(out_u.at[way], in_u.at[way], a_send.at[way], a_recv.at[way], mates[way])

    chain_q, chain_o, chain_u, chain_d, chain_t = chains
    order = []
    for far in range(1, depth):
        for slot in (depth - far, far):
            if slot not in order:
                order.append(slot)
    order.append(0)
    closed = []
    opened = []

    def advance():
        while len(opened) < depth - 1:
            step = len(opened) + 1
            if step not in closed or depth - step not in closed:
                return
            for chain in (chain_q, chain_o):
                if step > 1:
                    z_take(chain, step - 1)
                z_start(chain, step)
            opened.append(step)

    u_core.start()
    d_core.start()
    for copy in stay:
        copy.start()
    products(o_left, o_right, out_o, 1)
    u_core.wait_recv()
    stay[0].wait()
    add_blocks(
        CHIPS * depth,
        lambda at: acc_u.at[at // depth, at % depth],
        lambda at: rc_u.at[at // depth, at % depth],
    )
    z_start(chain_u, 1)
    d_core.wait_recv()
    stay[1].wait()
    add_blocks(depth, lambda at: acc_d.at[at], lambda at: rc_d.at[at])
    z_start(chain_d, 1)
    products(q_left, q_right, out_q, 1)
    for slot in order:
        for item in bulk:
            b_core(item, slot).start()
    t_core.start()
    products(o_left, o_right, acc_o, 0)
    products(q_left, q_right, acc_q, 0)
    open_slot(order[0])
    open_slot(order[1])
    t_core.wait_recv()
    stay[2].wait()
    add_blocks(
        CHIPS * depth,
        lambda at: acc_t.at[at // CHIPS, at % CHIPS],
        lambda at: rc_t.at[at // CHIPS, at % CHIPS],
    )
    for way in (1, 2, 3):
        t_plane(way).start()
    z_steps = [(chain, step) for step in range(1, depth) for chain in (chain_u, chain_d)]
    taken = 0
    for at in range(depth):
        if taken < len(z_steps):
            z_next(*z_steps[taken])
            taken = taken + 1
        middle_slot(order[at])
        if at + 2 < depth:
            open_slot(order[at + 2])
        if at >= 1:
            close_slot(order[at - 1])
            closed.append(order[at - 1])
            advance()
    for way in (1, 2, 3):
        t_plane(way).wait_recv()

    @pl.loop(0, depth)
    def _(at):
        total = acc_t[at, chip].astype(jnp.float32)
        for way in (1, 2, 3):
            total = total + p_t[way, at].astype(jnp.float32)
        fin_t[at] = total.astype(jnp.bfloat16)

    z_start(chain_t, 1)
    for chain, step in z_steps[taken:]:
        if chain is chain_u:
            z_next(chain, step)
    for way in (1, 2, 3):
        out_u[way] = fin_u[way].astype(jnp.bfloat16)
        u_turn(way).start()
    close_slot(order[depth - 1])
    closed.append(order[depth - 1])
    advance()
    for chain, step in z_steps[taken:]:
        if chain is chain_d:
            z_next(chain, step)
    for step in range(1, depth):
        z_next(chain_t, step)
    for step in range(len(opened), depth):
        for chain in (chain_q, chain_o):
            z_next(chain, step)
    u_out[chip] = fin_u[0]
    for way in (1, 2, 3):
        u_turn(way).wait_recv()
        u_out[chip_at[way]] = in_u[way].astype(jnp.float32)

    for copy in (u_core, d_core, t_core):
        copy.wait_send()
    for slot in range(depth):
        for item in bulk:
            b_core(item, slot).wait_send()
            for side in (0, 1):
                b_first(item, slot, side).wait_send()
                b_second(item, slot, side).wait_send()
    for way in (1, 2, 3):
        t_plane(way).wait_send()
        u_turn(way).wait_send()
    for step in range(1, depth):

        @pl.when(layer < step)
        def _(step=step):
            for chain in chains:
                z_up(chain, step).wait_send()

        @pl.when(layer >= depth - step)
        def _(step=step):
            for chain in chains:
                z_down(chain, step).wait_send()


def scatter_sums(q_left, q_right, o_left, o_right, t_part, u_part, d_part, depth, main):
    low, full = jnp.bfloat16, jnp.float32
    half = main // 2

    def bulk_scratch(columns):
        return [
            pltpu.VMEM((2, 2, depth, main, columns), low),
            pltpu.VMEM((2, 2, depth, main, columns), low),
            pltpu.VMEM((2, 2, depth, main, columns), low),
            pltpu.VMEM((2, 2, depth, half, columns), low),
            pltpu.VMEM((2, depth, half, columns), low),
            pltpu.VMEM((2, depth, main, columns), low),
        ]

    q_columns, o_columns, u_columns = q_right.shape[1], o_right.shape[1], u_part.shape[1]
    down = d_part.shape[2:]
    small = t_part.shape[1:]
    dma = pltpu.SemaphoreType.DMA
    return pl.pallas_call(
        functools.partial(scatter_kernel, depth),
        out_shape=[
            jax.ShapeDtypeStruct((main, q_columns), full),
            jax.ShapeDtypeStruct((main, o_columns), full),
            jax.ShapeDtypeStruct(small, full),
            jax.ShapeDtypeStruct((CHIPS, main, u_columns), full),
            jax.ShapeDtypeStruct(down, full),
        ],
        in_specs=[pl.BlockSpec(memory_space=pltpu.VMEM)] * 4
        + [pl.BlockSpec(memory_space=pl.ANY)] * 3,
        out_specs=[pl.BlockSpec(memory_space=pltpu.VMEM)] * 5,
        scratch_shapes=bulk_scratch(q_columns)
        + bulk_scratch(o_columns)
        + [
            pltpu.VMEM((CHIPS, depth, main, u_columns), low),
            pltpu.VMEM((CHIPS, depth, main, u_columns), low),
            pltpu.VMEM((2, depth, CHIPS, main, u_columns), low),
            pltpu.VMEM((CHIPS, main, u_columns), full),
            pltpu.VMEM((CHIPS, main, u_columns), low),
            pltpu.VMEM((CHIPS, main, u_columns), low),
            pltpu.VMEM((depth,) + down, low),
            pltpu.VMEM((depth,) + down, low),
            pltpu.VMEM((2, depth) + down, low),
            pltpu.VMEM((depth, CHIPS) + small, low),
            pltpu.VMEM((depth, CHIPS) + small, low),
            pltpu.VMEM((CHIPS, depth) + small, low),
            pltpu.VMEM((depth,) + small, low),
            pltpu.VMEM((2, depth) + small, low),
            dma((3,)),
            dma((5, depth)),
            dma((5, depth)),
            dma((8, depth)),
            dma((8, depth)),
            dma((4,)),
            dma((4,)),
            dma((5, 2, depth)),
            dma((5, 2, depth)),
            dma((4,)),
            dma((4,)),
        ],
        compiler_params=pltpu.CompilerParams(
            collective_id=1, has_side_effects=True, vmem_limit_bytes=56 * 2**20
        ),
        name="scatter_sums",
    )(
        q_left,
        q_right,
        o_left,
        o_right,
        t_part.reshape((depth, CHIPS, 2) + small),
        u_part.reshape(2, CHIPS, depth, main, u_columns),
        d_part,
    )


def lower(value):
    return value.astype(jnp.bfloat16)


def wide(value):
    return value.astype(jnp.float32)


def contract_rows(left, right):
    return lax.dot_general(left, right, (((0,), (0,)), ((), ())), preferred_element_type=jnp.float32)


def contract_columns(left, right):
    return lax.dot_general(left, right, (((1,), (1,)), ((), ())), preferred_element_type=jnp.float32)


def multiply(left, right):
    return jnp.dot(left, right, preferred_element_type=jnp.float32)


def middle_kernel(*refs):
    second, onehot, bias, u_hbm, t_hbm, d_hbm, c_hbm = refs[:7]
    d_second, lifted, g_up, g_tail, g_down, g_bias = refs[7:13]
    (
        w_up,
        w_tail,
        w_down,
        cots,
        tokens,
        slopes,
        active,
        spread,
        steep,
        y_out,
        y_in,
        s_out,
        s_in,
        local,
        h_send,
        h_recv,
        y_send,
        y_recv,
        s_send,
        s_recv,
    ) = refs[13:]
    rows = second.shape[0]
    bulk = w_up.shape[0]
    me = lax.axis_index("dp")
    layer = me // GROUP
    chip = (me % GROUP) // 2
    core = me % 2
    east = chip % 2
    north = chip // 2
    chip_at = (
        chip,
        north * 2 + (1 - east),
        (1 - north) * 2 + east,
        (1 - north) * 2 + (1 - east),
    )
    mates = tuple(layer * GROUP + at * 2 + core for at in chip_at)
    barrier = pltpu.get_barrier_semaphore()
    for device in mates[1:]:
        pl.semaphore_signal(barrier, inc=1, device_id=(device,), device_id_type=MESH)
    loads = [
        pltpu.make_async_copy(d_hbm, w_down, local.at[0]),
        pltpu.make_async_copy(c_hbm, cots, local.at[1]),
        pltpu.make_async_copy(u_hbm, w_up, local.at[2]),
        pltpu.make_async_copy(t_hbm, w_tail, local.at[3]),
    ]
    for load in loads:
        load.start()
    pl.semaphore_wait(barrier, CHIPS - 1)

    def send(source, target, send_sem, recv_sem, way):
        return pltpu.make_async_remote_copy(
            src_ref=source,
            dst_ref=target,
            send_sem=send_sem.at[way],
            recv_sem=recv_sem.at[way],
            device_id=(mates[way],),
            device_id_type=MESH,
        )

    ways = (1, 2, 3)
    hidden = {way: send(second, tokens.at[way], h_send, h_recv, way) for way in ways}
    lifts = {way: send(y_out.at[way], y_in.at[way], y_send, y_recv, way) for way in ways}
    backs = {way: send(s_out.at[way], s_in.at[way], s_send, s_recv, way) for way in ways}
    for way in (1, 2, 3):
        hidden[way].start()
    tokens[0] = second[...]
    loads[0].wait()
    loads[1].wait()
    slopes[...] = contract_columns(cots[...], w_down[...])
    loads[2].wait()
    loads[3].wait()
    for way in range(CHIPS):
        if way > 0:
            hidden[way].wait_recv()
        span = pl.ds(way * rows, rows)
        mine = lower(multiply(tokens[way], onehot[...]))
        spread[span] = mine
        upper = multiply(mine[:, :bulk], w_up[...]) + multiply(mine[:, bulk:], w_tail[...])
        upper = upper + bias[...]
        phi = 0.5 * (1.0 + lax.erf(upper * ROOT_HALF))
        active[span] = lower(upper * phi)
        steep_rows = slopes[span] * (phi + upper * jnp.exp(-0.5 * upper * upper) * INV_ROOT_TAU)
        slopes[span] = steep_rows
        steep[span] = lower(steep_rows)
        back = jnp.concatenate(
            [contract_columns(steep[span], w_up[...]), contract_columns(steep[span], w_tail[...])],
            axis=1,
        )
        s_out[way] = lower(contract_columns(lower(back), onehot[...]))
        if way > 0:
            backs[way].start()
        y_out[way] = lower(multiply(active[span], w_down[...]))
        if way > 0:
            lifts[way].start()
    g_bias[...] = jnp.sum(slopes[...], axis=0, keepdims=True)
    g_up[...] = lower(contract_rows(spread[:, :bulk], steep[...]))
    part = steep.shape[1]
    g_tail[...] = jnp.zeros_like(g_tail)
    g_tail[:, pl.ds(pl.multiple_of(chip * part, LANES), part)] = lower(
        contract_rows(spread[:, bulk:], steep[...])
    )
    g_down[...] = lower(contract_rows(active[...], cots[...]))
    total = wide(s_out[0])
    for way in (1, 2, 3):
        backs[way].wait_recv()
        total = total + wide(s_in[way])
    d_second[...] = total
    total = wide(y_out[0])
    for way in (1, 2, 3):
        lifts[way].wait_recv()
        total = total + wide(y_in[way])
    lifted[...] = total
    for way in (1, 2, 3):
        hidden[way].wait_send()
        backs[way].wait_send()
        lifts[way].wait_send()


def middle(second, onehot, bias, w_up, w_tail, w_down, cots):
    rows, width = second.shape
    part = w_down.shape[0]
    bulk, left = w_up.shape[0], w_tail.shape[0]
    group = CHIPS * rows
    low, full = jnp.bfloat16, jnp.float32
    vmem = pl.BlockSpec(memory_space=pltpu.VMEM)
    dma = pltpu.SemaphoreType.DMA
    return pl.pallas_call(
        middle_kernel,
        out_shape=[
            jax.ShapeDtypeStruct((rows, width), full),
            jax.ShapeDtypeStruct((rows, width), full),
            jax.ShapeDtypeStruct((bulk, part), low),
            jax.ShapeDtypeStruct((left, CHIPS * part), low),
            jax.ShapeDtypeStruct((part, width), low),
            jax.ShapeDtypeStruct((1, part), full),
        ],
        in_specs=[vmem] * 3 + [pl.BlockSpec(memory_space=pl.ANY)] * 4,
        out_specs=[vmem] * 6,
        scratch_shapes=[
            pltpu.VMEM((bulk, part), low),
            pltpu.VMEM((left, part), low),
            pltpu.VMEM((part, width), low),
            pltpu.VMEM((group, width), low),
            pltpu.VMEM((CHIPS, rows, width), low),
            pltpu.VMEM((group, part), full),
            pltpu.VMEM((group, part), low),
            pltpu.VMEM((group, width), low),
            pltpu.VMEM((group, part), low),
            pltpu.VMEM((CHIPS, rows, width), low),
            pltpu.VMEM((CHIPS, rows, width), low),
            pltpu.VMEM((CHIPS, rows, width), low),
            pltpu.VMEM((CHIPS, rows, width), low),
            dma((4,)),
        ]
        + [dma((CHIPS,))] * 6,
        compiler_params=pltpu.CompilerParams(
            collective_id=2, has_side_effects=True, vmem_limit_bytes=50 * 2**20
        ),
        name="middle",
    )(second, onehot, bias, w_up, w_tail, w_down, cots)


def two_parts(value):
    high = lax.reduce_precision(value, 8, 7)
    return jnp.concatenate([lower(high), lower(value - high)], axis=0)


def body_group(block_input, out_cotangent, seq_lengths, w_qkv, w_out, w_up, w_down, vectors):
    rows, width = block_input.shape
    hidden = 4 * width
    scale = HEAD_DIM ** (-0.5)
    total = lax.axis_size("dp")
    depth = total // GROUP
    own = width // total
    main = own // (2 * ROWS) * (2 * ROWS)
    tail = own - main
    step = hidden // total
    wide_step = ceil_to(step, ROWS)
    part = total // CHIPS * wide_step
    count = vectors.shape[0]
    me = lax.axis_index("dp")
    layer = me // GROUP
    chip = (me // 2) % CHIPS
    core = me % 2
    mask = causal_mask(seq_lengths[0], rows)

    side = jnp.concatenate([w_qkv.reshape(own, 3 * width), w_out.reshape(own, width)], axis=1)
    upper_own = jnp.pad(
        w_up.reshape(own, depth, CHIPS, 2, step), ((0, 0),) * 4 + ((0, wide_step - step),)
    )
    upper_own = upper_own.transpose(2, 0, 1, 3, 4).reshape(CHIPS, own, part)
    down_own = jnp.pad(w_down.reshape(step, width), ((0, wide_step - step), (0, 0)))
    side_rows = tail * hidden // LANES
    up_rows = tail * CHIPS * part // LANES
    vec_rows = ceil_to(count, LANES) // LANES
    used = side_rows + up_rows + vec_rows
    tail_rows = ceil_to(used, ROWS)
    extra = jnp.concatenate(
        [
            side[main:].reshape(side_rows, LANES),
            upper_own[:, main:].reshape(up_rows, LANES),
            jnp.pad(vectors, (0, vec_rows * LANES - count)).reshape(vec_rows, LANES),
            jnp.zeros((tail_rows - used, LANES), jnp.bfloat16),
        ],
        axis=0,
    )
    s_all, t_all, u_all, d_all, c_all = gather_all(
        side[:main], extra, upper_own[:, :main], down_own, out_cotangent, depth
    )
    bulk = total * main
    w_side = s_all.reshape(bulk, hidden)
    w_upper = u_all.reshape(bulk, part)
    w_lower = d_all.reshape(part, width)
    cots = c_all.reshape(CHIPS * rows, width)
    t_all = t_all.reshape(total, tail_rows, LANES)
    side_tail = t_all[:, :side_rows].reshape(total * tail, hidden)
    up_tail = t_all[:, side_rows : side_rows + up_rows].reshape(total, CHIPS, tail, part)
    up_tail = lax.dynamic_index_in_dim(up_tail, chip, 1, keepdims=False)
    up_tail = up_tail.reshape(total * tail, part)
    vec = t_all[:, side_rows + up_rows : used].reshape(total, vec_rows * LANES)[:, :count]
    vec = wide(vec.reshape(-1))
    bias_up = vec[7 * width : 7 * width + hidden].reshape(depth, CHIPS, 2, step)
    bias_up = lax.dynamic_index_in_dim(bias_up, chip, 1, keepdims=False)
    bias_up = jnp.pad(bias_up, ((0, 0), (0, 0), (0, wide_step - step))).reshape(1, part)

    place = jnp.arange(width, dtype=jnp.int32)
    slot = place // main
    there = (layer + slot % depth) % depth * GROUP
    there = there + jnp.bitwise_xor(chip, slot // depth % CHIPS) * 2
    there = there + jnp.bitwise_xor(core, slot // (depth * CHIPS))
    late = place - bulk
    origin = jnp.where(
        place < bulk, there * own + place % main, late // tail * own + main + late % tail
    )
    onehot = lower(place[:, None] == origin[None, :])

    def permute(value):
        return lower(multiply(value, onehot))

    def restore(value):
        return lower(contract_columns(value, onehot))

    def restore_wide(value):
        both = contract_columns(two_parts(value), onehot)
        return both[:rows] + both[rows:]

    wq, wo = w_side[:, : 3 * width], w_side[:, 3 * width :]
    wq_tail, wo_tail = side_tail[:, : 3 * width], side_tail[:, 3 * width :]

    inputs = wide(block_input)
    normed1, inverse1, pre1 = layer_norm(inputs, vec[0:width], vec[width : 2 * width])
    first = permute(lower(pre1))
    qkv = multiply(first[:, :bulk], wq) + multiply(first[:, bulk:], wq_tail)
    query = lower((qkv[:, 0:width] + vec[2 * width : 3 * width]) * scale)
    query = query.reshape(rows, HEADS, HEAD_DIM)
    keys = lower(qkv[:, width : 2 * width]).reshape(rows, HEADS, HEAD_DIM)
    values = lower(qkv[:, 2 * width : 3 * width] + vec[3 * width : 4 * width])
    values = values.reshape(rows, HEADS, HEAD_DIM)
    scores = score_block(query, keys, mask)
    peak = jnp.max(scores, axis=2, keepdims=True)
    logsum = peak + jnp.log(jnp.sum(jnp.exp(scores - peak), axis=2, keepdims=True))
    probs_low = lower(jnp.exp(scores - logsum))
    mixed = jnp.einsum("hqk,khe->qhe", probs_low, values, preferred_element_type=jnp.float32)
    mixed = permute(lower(mixed).reshape(rows, width))
    resid = inputs + multiply(mixed[:, :bulk], wo) + multiply(mixed[:, bulk:], wo_tail)
    resid = resid + vec[4 * width : 5 * width]
    gain2 = vec[5 * width : 6 * width]
    normed2, inverse2, pre2 = layer_norm(resid, gain2, vec[6 * width : 7 * width])
    second = lower(pre2)
    d_second, lifted, g_up, g_up_tail, g_down, d_bias_up = middle(
        second, onehot, bias_up, w_upper, up_tail, w_lower, cots
    )
    block_output = lower(resid + lifted + vec[7 * width + hidden :])
    g_down = g_down.reshape(depth, 2, wide_step, width)
    turn = jnp.arange(CHIPS, dtype=jnp.int32)

    grad_top = wide(out_cotangent)
    d_resid = grad_top + norm_back(d_second, normed2, inverse2, gain2)
    d_resid_low = lower(d_resid)
    g_out_tail = contract_rows(mixed[:, bulk:], d_resid_low)
    d_mixed = jnp.concatenate(
        [contract_columns(d_resid_low, wo), contract_columns(d_resid_low, wo_tail)], axis=1
    )
    d_mixed = restore(lower(d_mixed)).reshape(rows, HEADS, HEAD_DIM)
    probs = jnp.exp(score_block(query, keys, mask) - logsum)
    probs_low = lower(probs)
    d_values = jnp.einsum("hqk,qhe->khe", probs_low, d_mixed, preferred_element_type=jnp.float32)
    d_probs = jnp.einsum("qhe,khe->hqk", d_mixed, values, preferred_element_type=jnp.float32)
    delta = jnp.sum(probs * d_probs, axis=2, keepdims=True)
    d_scores = lower(probs * (d_probs - delta))
    d_query = jnp.einsum("hqk,khe->qhe", d_scores, keys, preferred_element_type=jnp.float32)
    d_query = d_query.reshape(rows, width) * scale
    d_keys = jnp.einsum("hqk,qhe->khe", d_scores, query, preferred_element_type=jnp.float32)
    d_keys = d_keys.reshape(rows, width)
    d_values = d_values.reshape(rows, width)
    d_qkv = lower(jnp.concatenate([d_query, d_keys, d_values], axis=1))
    g_qkv_tail = contract_rows(first[:, bulk:], d_qkv)
    d_first = jnp.concatenate(
        [contract_columns(d_qkv, wq), contract_columns(d_qkv, wq_tail)], axis=1
    )
    d_first = restore_wide(d_first)
    input_grad = d_resid + norm_back(d_first, normed1, inverse1, vec[0:width])

    d_bias_up = d_bias_up.reshape(depth, 1, 2, wide_step)[..., :step]
    d_bias_up = jnp.where(turn[None, :, None, None] == chip, d_bias_up, 0.0)
    g_vec = jnp.concatenate(
        [
            jnp.sum(d_first * normed1, axis=0),
            jnp.sum(d_first, axis=0),
            jnp.sum(d_query, axis=0),
            jnp.sum(d_values, axis=0),
            jnp.sum(d_resid, axis=0),
            jnp.sum(d_second * normed2, axis=0),
            jnp.sum(d_second, axis=0),
            d_bias_up.reshape(hidden),
            jnp.sum(grad_top, axis=0),
        ]
    )
    g_tails = jnp.concatenate([lower(g_qkv_tail), lower(g_out_tail), g_up_tail], axis=1)
    g_tails = lax.optimization_barrier(g_tails)
    g_tails = g_tails.reshape(total, side_rows + up_rows, LANES)
    g_vec = jnp.pad(lower(g_vec).reshape(total, count), ((0, 0), (0, vec_rows * LANES - count)))
    g_extra = jnp.concatenate(
        [
            g_tails,
            g_vec.reshape(total, vec_rows, LANES),
            jnp.zeros((total, tail_rows - used, LANES), jnp.bfloat16),
        ],
        axis=1,
    )
    g_extra = lax.optimization_barrier(g_extra)
    g_qkv, g_out, g_extra, g_up, g_down = scatter_sums(
        first,
        d_qkv,
        mixed,
        d_resid_low,
        g_extra,
        g_up,
        g_down,
        depth,
        main,
    )
    g_tails = g_extra[: side_rows + up_rows].reshape(tail, hidden + CHIPS * part)
    g_side_tail = g_tails[:, :hidden]
    g_up_tail = g_tails[:, hidden:].reshape(tail, CHIPS, part).transpose(1, 0, 2)
    grad_vectors = g_extra[side_rows + up_rows : used].reshape(-1)[:count]
    grad_qkv = jnp.concatenate([g_qkv, g_side_tail[:, : 3 * width]], axis=0).reshape(-1)
    grad_out = jnp.concatenate([g_out, g_side_tail[:, 3 * width :]], axis=0).reshape(-1)
    grad_up = jnp.concatenate([g_up, g_up_tail], axis=1)
    grad_up = grad_up.reshape(CHIPS, own, depth, 2, wide_step)[..., :step]
    grad_up = grad_up.transpose(1, 2, 0, 3, 4).reshape(-1)
    grad_down = g_down[:step].reshape(-1)
    return (block_output, input_grad, grad_qkv, grad_out, grad_up, grad_down, grad_vectors)


def solution(mesh):
    in_specs = (
        P("dp", None),
        P("dp", None),
        P("dp", None),
        P("dp"),
        P("dp"),
        P("dp"),
        P("dp"),
        P("dp"),
    )
    out_specs = (P("dp", None), P("dp", None), P("dp"), P("dp"), P("dp"), P("dp"), P("dp"))
    total = mesh.shape["dp"]

    def body(*blocks):
        width = blocks[0].shape[1]
        own = width // total
        small = own % (2 * ROWS) * 4 * width
        tidy = total % (2 * GROUP) == 0 and width % total == 0 and own >= 2 * ROWS
        if tidy and small > 0 and small % LANES == 0:
            return body_group(*blocks)
        return body_flat(*blocks)

    return jax.shard_map(body, mesh=mesh, in_specs=in_specs, out_specs=out_specs, check_vma=False)
```

```python
import functools

import jax
import jax.numpy as jnp
from jax import lax
from jax.experimental import pallas as pl
from jax.experimental.pallas import tpu as pltpu
from jax.sharding import PartitionSpec as P

HEADS = 17
HEAD_DIM = 64


EPS = 1e-05
ROOT_HALF = 0.7071067811865476
INV_ROOT_TAU = 0.3989422804014327


def layer_norm(rows, gain, shift):
    mean = jnp.mean(rows, axis=1, keepdims=True)
    centered = rows - mean
    inverse = lax.rsqrt(jnp.mean(centered * centered, axis=1, keepdims=True) + EPS)
    normed = centered * inverse
    return (normed, inverse, normed * gain + shift)


def norm_back(grad_rows, normed, inverse, gain):
    scaled = grad_rows * gain
    inner = jnp.mean(scaled * normed, axis=1, keepdims=True)
    return inverse * (scaled - jnp.mean(scaled, axis=1, keepdims=True) - normed * inner)


def gelu_exact(value):
    return 0.5 * value * (1.0 + lax.erf(value * ROOT_HALF))


def gelu_slope(value):
    return (
        0.5 * (1.0 + lax.erf(value * ROOT_HALF))
        + value * jnp.exp(-0.5 * value * value) * INV_ROOT_TAU
    )


def causal_mask(lengths, rows):
    count = lengths.shape[0]
    order = jnp.arange(count, dtype=jnp.int32)
    ends = jnp.sum(jnp.where(order[:, None] <= order[None, :], lengths[:, None], 0), axis=0)
    position = jnp.arange(rows, dtype=jnp.int32)
    segment = jnp.sum((position[:, None] >= ends[None, :]).astype(jnp.int32), axis=1)
    return (segment[:, None] == segment[None, :]) & (position[None, :] <= position[:, None])


def score_block(query, keys, mask):
    scores = jnp.einsum("qhe,khe->hqk", query, keys, preferred_element_type=jnp.float32)
    return jnp.where(mask[None], scores, -1e30)


def shape_params(flat_parts, width):
    hidden = 4 * width
    return (
        flat_parts[0].reshape(width, 3 * width),
        flat_parts[1].reshape(width, width),
        flat_parts[2].reshape(width, hidden),
        flat_parts[3].reshape(hidden, width),
        flat_parts[4].astype(jnp.float32),
    )


def window_term(left_rows, right_rows, flat_start, flat_count):
    inner_len = left_rows.shape[1]
    columns = right_rows.shape[1]
    row_count = min(inner_len, flat_count // columns + 2)
    row_first = jnp.clip(flat_start // columns, 0, inner_len - row_count)
    product = lax.dot_general(
        left_rows, right_rows, (((0,), (0,)), ((), ())), preferred_element_type=jnp.float32
    ).reshape(-1)
    padded = jnp.concatenate([product, jnp.zeros((flat_count,), jnp.float32)])
    return lax.dynamic_slice_in_dim(padded, flat_start - row_first * columns, flat_count, 0)


def shard_terms(pairs, vector_grad, device_total):
    piece_lens = [
        left_rows.shape[1] * right_rows.shape[1] // device_total for left_rows, right_rows in pairs
    ]
    piece_lens = piece_lens + [vector_grad.shape[0] // device_total]
    shard_len = sum(piece_lens)

    def shard_term(start, count):
        dev_count = count // shard_len
        dev_first = start // shard_len
        pieces = []
        for (left_rows, right_rows), piece_len in zip(pairs, piece_lens):
            window = window_term(
                left_rows, right_rows, dev_first * piece_len, dev_count * piece_len
            )
            pieces.append(window.reshape(dev_count, piece_len))
        vec_len = piece_lens[-1]
        window = vector_grad
        pieces.append(window.reshape(dev_count, vec_len))
        return jnp.concatenate(pieces, axis=1).reshape(-1)

    return (shard_term, shard_len, piece_lens)


def split_shard(summed, piece_lens):
    outputs = []
    offset = 0
    for piece_len in piece_lens:
        outputs.append(summed[offset : offset + piece_len])
        offset = offset + piece_len
    return outputs


def fetch_flat(w_qkv, w_out, w_up, w_down, vectors, width):
    fetched = tuple(
        lax.all_gather(part, "dp", axis=0, tiled=True)
        for part in (w_qkv, w_out, w_up, w_down, vectors)
    )
    return shape_params(fetched, width)


def reduce_flat(pairs, g_vec, device_total):
    all_term, all_len, all_lens = shard_terms(pairs, g_vec, device_total)
    return split_shard(
        lax.psum_scatter(
            all_term(jnp.int32(0), all_len * device_total),
            "dp",
            scatter_dimension=0,
            tiled=True,
        ),
        all_lens,
    )


def body_flat(block_input, out_cotangent, seq_lengths, w_qkv, w_out, w_up, w_down, vectors):
    rows, width = block_input.shape
    hidden = 4 * width
    scale = HEAD_DIM ** (-0.5)
    device_total = lax.axis_size("dp")
    mask = causal_mask(seq_lengths[0], rows)
    wqkv, wo, wup, wdn, vec = fetch_flat(w_qkv, w_out, w_up, w_down, vectors, width)
    inputs = block_input.astype(jnp.float32)
    normed1, inverse1, pre1 = layer_norm(inputs, vec[0:width], vec[width : 2 * width])
    first = pre1.astype(jnp.bfloat16)
    qkv = jnp.dot(first, wqkv, preferred_element_type=jnp.float32)
    query = (
        ((qkv[:, 0:width] + vec[2 * width : 3 * width]) * scale)
        .astype(jnp.bfloat16)
        .reshape(rows, HEADS, HEAD_DIM)
    )
    keys = qkv[:, width : 2 * width].astype(jnp.bfloat16).reshape(rows, HEADS, HEAD_DIM)
    values = (
        (qkv[:, 2 * width : 3 * width] + vec[3 * width : 4 * width])
        .astype(jnp.bfloat16)
        .reshape(rows, HEADS, HEAD_DIM)
    )
    scores = score_block(query, keys, mask)
    peak = jnp.max(scores, axis=2, keepdims=True)
    logsum = peak + jnp.log(jnp.sum(jnp.exp(scores - peak), axis=2, keepdims=True))
    probs_low = jnp.exp(scores - logsum).astype(jnp.bfloat16)
    mixed = jnp.einsum("hqk,khe->qhe", probs_low, values, preferred_element_type=jnp.float32)
    mixed = mixed.astype(jnp.bfloat16).reshape(rows, width)
    resid = (
        inputs + jnp.dot(mixed, wo, preferred_element_type=jnp.float32) + vec[4 * width : 5 * width]
    )
    normed2, inverse2, pre2 = layer_norm(
        resid, vec[5 * width : 6 * width], vec[6 * width : 7 * width]
    )
    second = pre2.astype(jnp.bfloat16)
    upper = (
        jnp.dot(second, wup, preferred_element_type=jnp.float32)
        + vec[7 * width : 7 * width + hidden]
    )
    active = gelu_exact(upper).astype(jnp.bfloat16)
    output = (
        resid + jnp.dot(active, wdn, preferred_element_type=jnp.float32) + vec[7 * width + hidden :]
    )
    block_output = output.astype(jnp.bfloat16)
    back_w = (wqkv, wo, wup, wdn)
    bqkv, bwo, bwup, bwdn = back_w
    grad_top = out_cotangent.astype(jnp.float32)
    d_upper = jnp.dot(out_cotangent, bwdn.T, preferred_element_type=jnp.float32) * gelu_slope(upper)
    d_upper_low = d_upper.astype(jnp.bfloat16)
    d_second = jnp.dot(d_upper_low, bwup.T, preferred_element_type=jnp.float32)
    d_resid = grad_top + norm_back(d_second, normed2, inverse2, vec[5 * width : 6 * width])
    d_resid_low = d_resid.astype(jnp.bfloat16)
    d_mixed = jnp.dot(d_resid_low, bwo.T, preferred_element_type=jnp.float32).astype(jnp.bfloat16)
    d_mixed = d_mixed.reshape(rows, HEADS, HEAD_DIM)
    probs = jnp.exp(score_block(query, keys, mask) - logsum)
    probs_low = probs.astype(jnp.bfloat16)
    d_values = jnp.einsum("hqk,qhe->khe", probs_low, d_mixed, preferred_element_type=jnp.float32)
    d_probs = jnp.einsum("qhe,khe->hqk", d_mixed, values, preferred_element_type=jnp.float32)
    delta = jnp.sum(probs * d_probs, axis=2, keepdims=True)
    d_scores = (probs * (d_probs - delta)).astype(jnp.bfloat16)
    d_query = (
        jnp.einsum("hqk,khe->qhe", d_scores, keys, preferred_element_type=jnp.float32).reshape(
            rows, width
        )
        * scale
    )
    d_keys = jnp.einsum(
        "hqk,qhe->khe", d_scores, query, preferred_element_type=jnp.float32
    ).reshape(rows, width)
    d_values = d_values.reshape(rows, width)
    d_qkv = jnp.concatenate([d_query, d_keys, d_values], axis=1).astype(jnp.bfloat16)
    d_first = jnp.dot(d_qkv, bqkv.T, preferred_element_type=jnp.float32)
    input_grad = d_resid + norm_back(d_first, normed1, inverse1, vec[0:width])
    g_vec = jnp.concatenate(
        [
            jnp.sum(d_first * normed1, axis=0),
            jnp.sum(d_first, axis=0),
            jnp.sum(d_query, axis=0),
            jnp.sum(d_values, axis=0),
            jnp.sum(d_resid, axis=0),
            jnp.sum(d_second * normed2, axis=0),
            jnp.sum(d_second, axis=0),
            jnp.sum(d_upper, axis=0),
            jnp.sum(grad_top, axis=0),
        ]
    )
    pairs = [(first, d_qkv), (mixed, d_resid_low), (second, d_upper_low), (active, out_cotangent)]
    grad_qkv, grad_out, grad_up, grad_down, grad_vectors = reduce_flat(pairs, g_vec, device_total)
    return (block_output, input_grad, grad_qkv, grad_out, grad_up, grad_down, grad_vectors)


GROUP = 8
CHIPS = 4
ROWS = 16
LANES = 128
MESH = pl.DeviceIdType.MESH


def ceil_to(count, unit):
    return -(-count // unit) * unit


def gather_kernel(
    depth, s_in, t_in, u_in, d_in, c_in, s_all, t_all, u_all, d_all, c_all, *sems
):
    (
        local,
        z_send,
        z_recv,
        s_send,
        s_recv,
        half_send,
        half_recv,
        core_send,
        core_recv,
        t_send,
        t_recv,
        u_send,
        u_recv,
        c_send,
        c_recv,
    ) = sems
    me = lax.axis_index("dp")
    layer = me // GROUP
    chip = (me % GROUP) // 2
    core = me % 2
    east = chip % 2
    north = chip // 2
    chip_at = (
        chip,
        north * 2 + (1 - east),
        (1 - north) * 2 + east,
        (1 - north) * 2 + (1 - east),
    )
    mates = tuple(layer * GROUP + at * 2 + core for at in chip_at)
    twin = layer * GROUP + chip * 2 + (1 - core)
    above = me + GROUP
    below = me - GROUP
    has_above = layer < depth - 1
    has_below = layer > 0

    barrier = pltpu.get_barrier_semaphore()
    for device in mates[1:] + (twin,):
        pl.semaphore_signal(barrier, inc=1, device_id=(device,), device_id_type=MESH)

    @pl.when(has_above)
    def _():
        pl.semaphore_signal(barrier, inc=1, device_id=(above,), device_id_type=MESH)

    @pl.when(has_below)
    def _():
        pl.semaphore_signal(barrier, inc=1, device_id=(below,), device_id_type=MESH)

    ends = (layer + depth - 1) // depth + (2 * depth - 2 - layer) // depth
    pl.semaphore_wait(barrier, CHIPS + ends)

    def send(source, target, send_sem, recv_sem, device):
        return pltpu.make_async_remote_copy(
            src_ref=source,
            dst_ref=target,
            send_sem=send_sem,
            recv_sem=recv_sem,
            device_id=(device,),
            device_id_type=MESH,
        )

    def layer_of(slot):
        return lax.rem(layer + slot, depth)

    def s_at(slot):
        return s_in if slot == 0 else s_all.at[0, 0, slot]

    def t_at(slot):
        return t_in if slot == 0 else t_all.at[layer_of(slot), chip, core]

    def d_at(slot):
        return d_in if slot == 0 else d_all.at[layer_of(slot), core]

    def u_at(slot):
        return u_all.at[0, :, slot]

    def s_to(slot, source):
        return s_all.at[0, 0, slot]

    def t_to(slot, source):
        return t_all.at[layer_of(source), chip, core]

    def d_to(slot, source):
        return d_all.at[layer_of(source), core]

    def u_to(slot, source):
        return u_all.at[0, :, slot]

    places = {"t": (0, t_at, t_to), "s": (1, s_at, s_to), "d": (2, d_at, d_to), "u": (3, u_at, u_to)}

    def z_copy(name, slot, up):
        index, source, target = places[name]
        there = (slot - 1) % depth if up else (slot + 1) % depth
        return send(
            source(slot),
            target(there, slot),
            z_send.at[index, slot, 0 if up else 1],
            z_recv.at[index, there],
            above if up else below,
        )

    def z_arrival(name, slot):
        index, source, target = places[name]
        here = target(slot, slot)
        return send(here, here, z_send.at[index, slot, 0], z_recv.at[index, slot], above)

    def routes():
        found = [(0, True, has_above), (0, False, has_below)]
        for far in range(1, depth - 1):
            found.append((depth - far, True, (layer >= far) & has_above))
            found.append((far, False, (layer + far < depth) & has_below))
        return found

    def z_forward(name, step):
        for slot, up, allowed in routes()[2 * step : 2 * step + 2]:

            @pl.when(allowed)
            def _(slot=slot, up=up):
                z_copy(name, slot, up).start()

    def z_land(name, far, then=None):
        for slot, came in ((depth - far, layer >= far), (far, layer + far < depth)):

            @pl.when(came)
            def _(slot=slot):
                z_arrival(name, slot).wait_recv()
                if then is not None:
                    then(slot)

    def s_plane(slot, way):
        return send(
            s_at(slot), s_all.at[0, way, slot], s_send.at[way, slot], s_recv.at[way, slot], mates[way]
        )

    def s_half(slot, way):
        rows = s_in.shape[0] // 2
        part = pl.ds(0 if way == 1 else rows, rows)
        return send(
            s_all.at[0, way, slot, part],
            s_all.at[0, 3, slot, part],
            half_send.at[way, slot],
            half_recv.at[way, slot],
            mates[3 - way],
        )

    def s_core(slot, way):
        source = s_at(slot) if way == 0 else s_all.at[0, way, slot]
        return send(
            source, s_all.at[1, way, slot], core_send.at[way, slot], core_recv.at[way, slot], twin
        )

    def s_spread(slot):
        s_plane(slot, 1).start()
        s_plane(slot, 2).start()
        s_core(slot, 0).start()

    def s_pass(slot):
        for way in (1, 2):
            s_plane(slot, way).wait_recv()
            s_half(slot, way).start()
            s_core(slot, way).start()

    def s_close(slot):
        for way in (1, 2):
            s_half(slot, way).wait_recv()
        s_core(slot, 3).start()

    def by_distance(far, act):
        if far == 0:
            act(0)
            return
        for slot, came in ((depth - far, layer >= far), (far, layer + far < depth)):

            @pl.when(came)
            def _(slot=slot):
                act(slot)

    def d_core(slot):
        return send(
            d_at(slot), d_to(slot, slot), core_send.at[4, slot], core_recv.at[4, slot], twin
        )

    def u_core(slot):
        return send(
            u_at(slot), u_all.at[1, :, slot], core_send.at[5, slot], core_recv.at[5, slot], twin
        )

    def d_twin_arrival(slot):
        here = d_all.at[layer_of(slot), 1 - core]
        return send(here, here, core_send.at[4, slot], core_recv.at[4, slot], twin)

    t_mine = t_all.at[:, chip, core]

    def t_plane(way):
        return send(t_mine, t_mine, t_send.at[way], t_recv.at[way], mates[way])

    def t_plane_arrival(way):
        here = t_all.at[:, chip_at[way], core]
        return send(here, here, t_send.at[way], t_recv.at[way], mates[way])

    t_core_block = t_all.at[:, :, core]
    t_twin_block = t_all.at[:, :, 1 - core]
    t_core = send(t_core_block, t_core_block, t_send.at[0], t_recv.at[0], twin)
    t_core_arrival = send(t_twin_block, t_twin_block, t_send.at[0], t_recv.at[0], twin)

    def u_plane(way):
        return send(
            u_in.at[chip_at[way]], u_all.at[0, way, 0], u_send.at[way], u_recv.at[way], mates[way]
        )

    def c_plane(way):
        return send(c_in, c_all.at[way], c_send.at[way], c_recv.at[way], mates[way])

    stay = [
        pltpu.make_async_copy(t_in, t_all.at[layer, chip, core], local.at[0]),
        pltpu.make_async_copy(u_in.at[chip], u_all.at[0, 0, 0], local.at[1]),
        pltpu.make_async_copy(s_in, s_all.at[0, 0, 0], local.at[2]),
        pltpu.make_async_copy(d_in, d_all.at[layer, core], local.at[3]),
        pltpu.make_async_copy(c_in, c_all.at[0], local.at[4]),
    ]

    z_forward("t", 0)
    z_forward("s", 0)
    for copy in stay:
        copy.start()
    for way in (1, 2, 3):
        u_plane(way).start()
    s_spread(0)
    for far in range(1, depth):
        z_land("t", far)
        if far < depth - 1:
            z_forward("t", far)
        z_land("s", far)
        if far < depth - 1:
            z_forward("s", far)
        if far == 1:
            z_forward("d", 0)
        by_distance(far, s_spread)
        if far == depth - 1:
            stay[0].wait()
            for way in (1, 2, 3):
                t_plane(way).start()
        if far == min(2, depth - 1):
            for way in (1, 2, 3):
                u_plane(way).wait_recv()
            stay[1].wait()
            z_forward("u", 0)
            u_core(0).start()
            d_core(0).start()
        by_distance(far - 1, s_pass)
    for way in (1, 2, 3):
        c_plane(way).start()
    for far in range(1, depth):
        z_land("d", far)
        if far < depth - 1:
            z_forward("d", far)
        by_distance(far, lambda slot: d_core(slot).start())
        if far == 1:
            by_distance(depth - 1, s_pass)
            for way in (1, 2, 3):
                t_plane_arrival(way).wait_recv()
            t_core.start()
        z_land("u", far)
        if far < depth - 1:
            z_forward("u", far)
        by_distance(far, lambda slot: u_core(slot).start())
        if far == 1:
            for near in range(depth):
                by_distance(near, s_close)
    for slot in range(depth):
        for way in range(CHIPS):
            s_core(slot, way).wait()
        u_core(slot).wait()
        d_core(slot).wait_send()
        d_twin_arrival(slot).wait_recv()
        for way in (1, 2):
            s_plane(slot, way).wait_send()
            s_half(slot, way).wait_send()
    for way in (1, 2, 3):
        u_plane(way).wait_send()
        t_plane(way).wait_send()
        c_plane(way).wait()
    t_core.wait_send()
    t_core_arrival.wait_recv()
    for copy in stay[2:]:
        copy.wait()
    for slot, up, allowed in routes():

        @pl.when(allowed)
        def _(slot=slot, up=up):
            for name in places:
                z_copy(name, slot, up).wait_send()


def gather_all(s_own, t_own, u_own, d_own, c_own, depth):
    low = jnp.bfloat16
    return pl.pallas_call(
        functools.partial(gather_kernel, depth),
        out_shape=[
            jax.ShapeDtypeStruct((2, CHIPS, depth) + s_own.shape, low),
            jax.ShapeDtypeStruct((depth, CHIPS, 2) + t_own.shape, low),
            jax.ShapeDtypeStruct((2, CHIPS, depth) + u_own.shape[1:], low),
            jax.ShapeDtypeStruct((depth, 2) + d_own.shape, low),
            jax.ShapeDtypeStruct((CHIPS,) + c_own.shape, low),
        ],
        in_specs=[pl.BlockSpec(memory_space=pl.ANY)] * 5,
        out_specs=[pl.BlockSpec(memory_space=pl.ANY)] * 5,
        scratch_shapes=[
            pltpu.SemaphoreType.DMA((5,)),
            pltpu.SemaphoreType.DMA((4, depth, 2)),
            pltpu.SemaphoreType.DMA((4, depth)),
            pltpu.SemaphoreType.DMA((3, depth)),
            pltpu.SemaphoreType.DMA((3, depth)),
            pltpu.SemaphoreType.DMA((3, depth)),
            pltpu.SemaphoreType.DMA((3, depth)),
            pltpu.SemaphoreType.DMA((6, depth)),
            pltpu.SemaphoreType.DMA((6, depth)),
            pltpu.SemaphoreType.DMA((4,)),
            pltpu.SemaphoreType.DMA((4,)),
            pltpu.SemaphoreType.DMA((4,)),
            pltpu.SemaphoreType.DMA((4,)),
            pltpu.SemaphoreType.DMA((4,)),
            pltpu.SemaphoreType.DMA((4,)),
        ],
        compiler_params=pltpu.CompilerParams(collective_id=0, has_side_effects=True),
        name="gather_params",
    )(s_own, t_own, u_own, d_own, c_own)


def add_blocks(count, pick, other):
    @pl.loop(0, count)
    def _(at):
        here, term = pick(at), other(at)
        here[...] = (here[...].astype(jnp.float32) + term[...].astype(jnp.float32)).astype(here.dtype)


def scatter_kernel(depth, *refs):
    ins, outs, refs = refs[:7], refs[7:12], refs[12:]
    (
        acc_q,
        out_q,
        rc_q,
        p1_q,
        p2_q,
        z_q,
        acc_o,
        out_o,
        rc_o,
        p1_o,
        p2_o,
        z_o,
        acc_u,
        rc_u,
        z_u,
        fin_u,
        out_u,
        in_u,
        acc_d,
        rc_d,
        z_d,
        acc_t,
        rc_t,
        p_t,
        fin_t,
        z_t,
        local,
        c_send,
        c_recv,
        p_send,
        p_recv,
        t_send,
        t_recv,
        z_send,
        z_recv,
        a_send,
        a_recv,
    ) = refs
    q_left, q_right, o_left, o_right, t_in, u_in, d_in = ins
    q_out, o_out, t_out, u_out, d_out = outs
    me = lax.axis_index("dp")
    layer = me // GROUP
    chip = (me % GROUP) // 2
    core = me % 2
    east = chip % 2
    north = chip // 2
    chip_at = (
        chip,
        north * 2 + (1 - east),
        (1 - north) * 2 + east,
        (1 - north) * 2 + (1 - east),
    )
    mates = tuple(layer * GROUP + at * 2 + core for at in chip_at)
    twin = layer * GROUP + chip * 2 + (1 - core)
    above = me + GROUP
    below = me - GROUP

    barrier = pltpu.get_barrier_semaphore()
    for device in mates[1:] + (twin,):
        pl.semaphore_signal(barrier, inc=1, device_id=(device,), device_id_type=MESH)

    @pl.when(layer < depth - 1)
    def _():
        pl.semaphore_signal(barrier, inc=1, device_id=(above,), device_id_type=MESH)

    @pl.when(layer > 0)
    def _():
        pl.semaphore_signal(barrier, inc=1, device_id=(below,), device_id_type=MESH)

    ends = (layer + depth - 1) // depth + (2 * depth - 2 - layer) // depth
    pl.semaphore_wait(barrier, CHIPS + ends)

    def send(source, target, send_sem, recv_sem, device):
        return pltpu.make_async_remote_copy(
            src_ref=source,
            dst_ref=target,
            send_sem=send_sem,
            recv_sem=recv_sem,
            device_id=(device,),
            device_id_type=MESH,
        )

    def layer_of(slot):
        return lax.rem(layer + slot, depth)

    bulk = ((0, out_q, acc_q, rc_q, p1_q, p2_q), (1, out_o, acc_o, rc_o, p1_o, p2_o))
    half = p1_q.shape[3]

    def products(left, right, place, other):
        across = place.shape[2] * place.shape[3]
        for at in range(CHIPS):
            first = (other * CHIPS + at) * across
            block = contract_rows(left[:, first : first + across], right[...])
            place[at // 2, at % 2] = lower(block).reshape(place.shape[2:])

    stay = [
        pltpu.make_async_copy(u_in.at[0], acc_u, local.at[0]),
        pltpu.make_async_copy(d_in.at[:, core], acc_d, local.at[1]),
        pltpu.make_async_copy(t_in.at[:, :, core], acc_t, local.at[2]),
    ]
    u_core = send(u_in.at[1], rc_u, c_send.at[2, 0], c_recv.at[2, 0], twin)
    d_core = send(d_in.at[:, 1 - core], rc_d, c_send.at[3, 0], c_recv.at[3, 0], twin)
    t_core = send(t_in.at[:, :, 1 - core], rc_t, c_send.at[4, 0], c_recv.at[4, 0], twin)

    def b_core(item, slot):
        index, whole, acc, rc, p1, p2 = item
        return send(
            whole.at[:, :, slot],
            rc.at[:, :, slot],
            c_send.at[index, slot],
            c_recv.at[index, slot],
            twin,
        )

    def b_first(item, slot, side):
        index, whole, acc, rc, p1, p2 = item
        if side == 0:
            source = acc.at[1, :, slot, pl.ds(0, half)]
        else:
            source = acc.at[:, 1, slot, pl.ds(half, half)]
        at = (index * 2 + side) * 2
        return send(
            source, p1.at[side, :, slot], p_send.at[at, slot], p_recv.at[at, slot], mates[2 - side]
        )

    def b_second(item, slot, side):
        index, whole, acc, rc, p1, p2 = item
        if side == 0:
            source = acc.at[0, 1, slot, pl.ds(0, half)]
        else:
            source = acc.at[1, 0, slot, pl.ds(half, half)]
        at = (index * 2 + side) * 2 + 1
        return send(
            source, p2.at[side, slot], p_send.at[at, slot], p_recv.at[at, slot], mates[1 + side]
        )

    def open_slot(slot):
        for item in bulk:
            index, whole, acc, rc, p1, p2 = item
            b_core(item, slot).wait_recv()
            add_blocks(
                CHIPS,
                lambda at, acc=acc: acc.at[at // 2, at % 2, slot],
                lambda at, rc=rc: rc.at[at // 2, at % 2, slot],
            )
            b_first(item, slot, 0).start()
            b_first(item, slot, 1).start()

    def middle_slot(slot):
        for item in bulk:
            index, whole, acc, rc, p1, p2 = item
            b_first(item, slot, 0).wait_recv()
            add_blocks(
                2,
                lambda at, acc=acc: acc.at[0, at, slot, pl.ds(0, half)],
                lambda at, p1=p1: p1.at[0, at, slot],
            )
            b_second(item, slot, 0).start()
            b_first(item, slot, 1).wait_recv()
            add_blocks(
                2,
                lambda at, acc=acc: acc.at[at, 0, slot, pl.ds(half, half)],
                lambda at, p1=p1: p1.at[1, at, slot],
            )
            b_second(item, slot, 1).start()

    def close_slot(slot):
        for item in bulk:
            index, whole, acc, rc, p1, p2 = item
            for side in (0, 1):
                b_second(item, slot, side).wait_recv()
                add_blocks(
                    1,
                    lambda at, acc=acc, side=side: acc.at[0, 0, slot, pl.ds(side * half, half)],
                    lambda at, p2=p2, side=side: p2.at[side, slot],
                )

    chains = (
        (0, lambda slot: acc_q.at[0, 0, slot], z_q, q_out),
        (1, lambda slot: acc_o.at[0, 0, slot], z_o, o_out),
        (2, lambda slot: acc_u.at[:, slot], z_u, fin_u),
        (3, lambda slot: acc_d.at[layer_of(slot)], z_d, d_out),
        (4, lambda slot: fin_t.at[layer_of(slot)], z_t, t_out),
    )

    def z_up(chain, step):
        index, block, landing, final = chain
        return send(
            block(depth - step),
            landing.at[0, step],
            z_send.at[index, 0, step],
            z_recv.at[index, 0, step],
            above,
        )

    def z_down(chain, step):
        index, block, landing, final = chain
        return send(
            block(step),
            landing.at[1, step],
            z_send.at[index, 1, step],
            z_recv.at[index, 1, step],
            below,
        )

    def z_start(chain, step):
        @pl.when(layer < step)
        def _():
            z_up(chain, step).start()

        @pl.when(layer >= depth - step)
        def _():
            z_down(chain, step).start()

    def z_take(chain, step):
        index, block, landing, final = chain
        last = step == depth - 1
        if last:
            final[...] = block(0)[...].astype(jnp.float32)
        targets = (depth - step - 1, (step + 1) % depth)
        came = (
            (layer >= 1) & (layer <= step),
            (layer <= depth - 2) & (layer >= depth - step - 1),
        )
        for way, make in enumerate((z_up, z_down)):

            @pl.when(came[way])
            def _(way=way, make=make):
                make(chain, step).wait_recv()
                here = final if last else block(targets[way])
                total = here[...].astype(jnp.float32) + landing[way, step].astype(jnp.float32)
                here[...] = total.astype(here.dtype)

    def z_next(chain, step):
        z_take(chain, step)
        if step < depth - 1:
            z_start(chain, step + 1)

    def t_plane(way):
        return send(
            acc_t.at[:, chip_at[way]], p_t.at[way], t_send.at[way], t_recv.at[way], mates[way]
        )

    def u_turn(way):
        return send(out_u.at[way], in_u.at[way], a_send.at[way], a_recv.at[way], mates[way])

    chain_q, chain_o, chain_u, chain_d, chain_t = chains
    order = []
    for far in range(1, depth):
        for slot in (depth - far, far):
            if slot not in order:
                order.append(slot)
    order.append(0)
    closed = []
    opened = []

    def advance():
        while len(opened) < depth - 1:
            step = len(opened) + 1
            if step not in closed or depth - step not in closed:
                return
            for chain in (chain_q, chain_o):
                if step > 1:
                    z_take(chain, step - 1)
                z_start(chain, step)
            opened.append(step)

    u_core.start()
    d_core.start()
    for copy in stay:
        copy.start()
    products(o_left, o_right, out_o, 1)
    u_core.wait_recv()
    stay[0].wait()
    add_blocks(
        CHIPS * depth,
        lambda at: acc_u.at[at // depth, at % depth],
        lambda at: rc_u.at[at // depth, at % depth],
    )
    z_start(chain_u, 1)
    d_core.wait_recv()
    stay[1].wait()
    add_blocks(depth, lambda at: acc_d.at[at], lambda at: rc_d.at[at])
    z_start(chain_d, 1)
    products(q_left, q_right, out_q, 1)
    for slot in order:
        for item in bulk:
            b_core(item, slot).start()
    t_core.start()
    products(o_left, o_right, acc_o, 0)
    products(q_left, q_right, acc_q, 0)
    open_slot(order[0])
    open_slot(order[1])
    t_core.wait_recv()
    stay[2].wait()
    add_blocks(
        CHIPS * depth,
        lambda at: acc_t.at[at // CHIPS, at % CHIPS],
        lambda at: rc_t.at[at // CHIPS, at % CHIPS],
    )
    for way in (1, 2, 3):
        t_plane(way).start()
    z_steps = [(chain, step) for step in range(1, depth) for chain in (chain_u, chain_d)]
    taken = 0
    for at in range(depth):
        if taken < len(z_steps):
            z_next(*z_steps[taken])
            taken = taken + 1
        middle_slot(order[at])
        if at + 2 < depth:
            open_slot(order[at + 2])
        if at >= 1:
            close_slot(order[at - 1])
            closed.append(order[at - 1])
            advance()
    for way in (1, 2, 3):
        t_plane(way).wait_recv()

    @pl.loop(0, depth)
    def _(at):
        total = acc_t[at, chip].astype(jnp.float32)
        for way in (1, 2, 3):
            total = total + p_t[way, at].astype(jnp.float32)
        fin_t[at] = total.astype(jnp.bfloat16)

    z_start(chain_t, 1)
    for chain, step in z_steps[taken:]:
        if chain is chain_u:
            z_next(chain, step)
    for way in (1, 2, 3):
        out_u[way] = fin_u[way].astype(jnp.bfloat16)
        u_turn(way).start()
    if depth > 2:
        z_next(chain_t, 1)
    close_slot(order[depth - 1])
    closed.append(order[depth - 1])
    advance()
    for step in range(2, depth - 1):
        z_next(chain_t, step)
    for chain, step in z_steps[taken:]:
        if chain is chain_d:
            z_next(chain, step)
    z_next(chain_t, depth - 1)
    for step in range(len(opened), depth):
        for chain in (chain_q, chain_o):
            z_next(chain, step)
    u_out[chip] = fin_u[0]
    for way in (1, 2, 3):
        u_turn(way).wait_recv()
        u_out[chip_at[way]] = in_u[way].astype(jnp.float32)

    for copy in (u_core, d_core, t_core):
        copy.wait_send()
    for slot in range(depth):
        for item in bulk:
            b_core(item, slot).wait_send()
            for side in (0, 1):
                b_first(item, slot, side).wait_send()
                b_second(item, slot, side).wait_send()
    for way in (1, 2, 3):
        t_plane(way).wait_send()
        u_turn(way).wait_send()
    for step in range(1, depth):

        @pl.when(layer < step)
        def _(step=step):
            for chain in chains:
                z_up(chain, step).wait_send()

        @pl.when(layer >= depth - step)
        def _(step=step):
            for chain in chains:
                z_down(chain, step).wait_send()


def scatter_sums(q_left, q_right, o_left, o_right, t_part, u_part, d_part, depth, main):
    low, full = jnp.bfloat16, jnp.float32
    half = main // 2

    def bulk_scratch(columns):
        return [
            pltpu.VMEM((2, 2, depth, main, columns), low),
            pltpu.VMEM((2, 2, depth, main, columns), low),
            pltpu.VMEM((2, 2, depth, main, columns), low),
            pltpu.VMEM((2, 2, depth, half, columns), low),
            pltpu.VMEM((2, depth, half, columns), low),
            pltpu.VMEM((2, depth, main, columns), low),
        ]

    q_columns, o_columns, u_columns = q_right.shape[1], o_right.shape[1], u_part.shape[1]
    down = d_part.shape[2:]
    small = t_part.shape[1:]
    dma = pltpu.SemaphoreType.DMA
    return pl.pallas_call(
        functools.partial(scatter_kernel, depth),
        out_shape=[
            jax.ShapeDtypeStruct((main, q_columns), full),
            jax.ShapeDtypeStruct((main, o_columns), full),
            jax.ShapeDtypeStruct(small, full),
            jax.ShapeDtypeStruct((CHIPS, main, u_columns), full),
            jax.ShapeDtypeStruct(down, full),
        ],
        in_specs=[pl.BlockSpec(memory_space=pltpu.VMEM)] * 4
        + [pl.BlockSpec(memory_space=pl.ANY)] * 3,
        out_specs=[pl.BlockSpec(memory_space=pltpu.VMEM)] * 5,
        scratch_shapes=bulk_scratch(q_columns)
        + bulk_scratch(o_columns)
        + [
            pltpu.VMEM((CHIPS, depth, main, u_columns), low),
            pltpu.VMEM((CHIPS, depth, main, u_columns), low),
            pltpu.VMEM((2, depth, CHIPS, main, u_columns), low),
            pltpu.VMEM((CHIPS, main, u_columns), full),
            pltpu.VMEM((CHIPS, main, u_columns), low),
            pltpu.VMEM((CHIPS, main, u_columns), low),
            pltpu.VMEM((depth,) + down, low),
            pltpu.VMEM((depth,) + down, low),
            pltpu.VMEM((2, depth) + down, low),
            pltpu.VMEM((depth, CHIPS) + small, low),
            pltpu.VMEM((depth, CHIPS) + small, low),
            pltpu.VMEM((CHIPS, depth) + small, low),
            pltpu.VMEM((depth,) + small, low),
            pltpu.VMEM((2, depth) + small, low),
            dma((3,)),
            dma((5, depth)),
            dma((5, depth)),
            dma((8, depth)),
            dma((8, depth)),
            dma((4,)),
            dma((4,)),
            dma((5, 2, depth)),
            dma((5, 2, depth)),
            dma((4,)),
            dma((4,)),
        ],
        compiler_params=pltpu.CompilerParams(
            collective_id=1, has_side_effects=True, vmem_limit_bytes=56 * 2**20
        ),
        name="scatter_sums",
    )(
        q_left,
        q_right,
        o_left,
        o_right,
        t_part.reshape((depth, CHIPS, 2) + small),
        u_part.reshape(2, CHIPS, depth, main, u_columns),
        d_part,
    )


def lower(value):
    return value.astype(jnp.bfloat16)


def wide(value):
    return value.astype(jnp.float32)


def contract_rows(left, right):
    return lax.dot_general(left, right, (((0,), (0,)), ((), ())), preferred_element_type=jnp.float32)


def contract_columns(left, right):
    return lax.dot_general(left, right, (((1,), (1,)), ((), ())), preferred_element_type=jnp.float32)


def multiply(left, right):
    return jnp.dot(left, right, preferred_element_type=jnp.float32)


def middle_kernel(*refs):
    second, onehot, bias, u_hbm, t_hbm, d_hbm, c_hbm = refs[:7]
    d_second, lifted, g_up, g_tail, g_down, g_bias = refs[7:13]
    (
        w_up,
        w_tail,
        w_down,
        cots,
        tokens,
        slopes,
        active,
        spread,
        steep,
        y_out,
        y_in,
        s_out,
        s_in,
        local,
        h_send,
        h_recv,
        y_send,
        y_recv,
        s_send,
        s_recv,
    ) = refs[13:]
    rows = second.shape[0]
    bulk = w_up.shape[0]
    me = lax.axis_index("dp")
    layer = me // GROUP
    chip = (me % GROUP) // 2
    core = me % 2
    east = chip % 2
    north = chip // 2
    chip_at = (
        chip,
        north * 2 + (1 - east),
        (1 - north) * 2 + east,
        (1 - north) * 2 + (1 - east),
    )
    mates = tuple(layer * GROUP + at * 2 + core for at in chip_at)
    barrier = pltpu.get_barrier_semaphore()
    for device in mates[1:]:
        pl.semaphore_signal(barrier, inc=1, device_id=(device,), device_id_type=MESH)
    loads = [
        pltpu.make_async_copy(d_hbm, w_down, local.at[0]),
        pltpu.make_async_copy(c_hbm, cots, local.at[1]),
        pltpu.make_async_copy(u_hbm, w_up, local.at[2]),
        pltpu.make_async_copy(t_hbm, w_tail, local.at[3]),
    ]
    for load in loads:
        load.start()
    pl.semaphore_wait(barrier, CHIPS - 1)

    def send(source, target, send_sem, recv_sem, way):
        return pltpu.make_async_remote_copy(
            src_ref=source,
            dst_ref=target,
            send_sem=send_sem.at[way],
            recv_sem=recv_sem.at[way],
            device_id=(mates[way],),
            device_id_type=MESH,
        )

    ways = (1, 2, 3)
    hidden = {way: send(second, tokens.at[way], h_send, h_recv, way) for way in ways}
    lifts = {way: send(y_out.at[way], y_in.at[way], y_send, y_recv, way) for way in ways}
    backs = {way: send(s_out.at[way], s_in.at[way], s_send, s_recv, way) for way in ways}
    for way in (1, 2, 3):
        hidden[way].start()
    tokens[0] = second[...]
    loads[0].wait()
    loads[1].wait()
    slopes[...] = contract_columns(cots[...], w_down[...])
    loads[2].wait()
    loads[3].wait()
    for way in range(CHIPS):
        if way > 0:
            hidden[way].wait_recv()
        span = pl.ds(way * rows, rows)
        mine = lower(multiply(tokens[way], onehot[...]))
        spread[span] = mine
        upper = multiply(mine[:, :bulk], w_up[...]) + multiply(mine[:, bulk:], w_tail[...])
        upper = upper + bias[...]
        phi = 0.5 * (1.0 + lax.erf(upper * ROOT_HALF))
        active[span] = lower(upper * phi)
        steep_rows = slopes[span] * (phi + upper * jnp.exp(-0.5 * upper * upper) * INV_ROOT_TAU)
        slopes[span] = steep_rows
        steep[span] = lower(steep_rows)
        back = jnp.concatenate(
            [contract_columns(steep[span], w_up[...]), contract_columns(steep[span], w_tail[...])],
            axis=1,
        )
        s_out[way] = lower(contract_columns(lower(back), onehot[...]))
        if way > 0:
            backs[way].start()
        y_out[way] = lower(multiply(active[span], w_down[...]))
        if way > 0:
            lifts[way].start()
    g_bias[...] = jnp.sum(slopes[...], axis=0, keepdims=True)
    g_up[...] = lower(contract_rows(spread[:, :bulk], steep[...]))
    part = steep.shape[1]
    g_tail[...] = jnp.zeros_like(g_tail)
    g_tail[:, pl.ds(pl.multiple_of(chip * part, LANES), part)] = lower(
        contract_rows(spread[:, bulk:], steep[...])
    )
    g_down[...] = lower(contract_rows(active[...], cots[...]))
    total = wide(s_out[0])
    for way in (1, 2, 3):
        backs[way].wait_recv()
        total = total + wide(s_in[way])
    d_second[...] = total
    total = wide(y_out[0])
    for way in (1, 2, 3):
        lifts[way].wait_recv()
        total = total + wide(y_in[way])
    lifted[...] = total
    for way in (1, 2, 3):
        hidden[way].wait_send()
        backs[way].wait_send()
        lifts[way].wait_send()


def middle(second, onehot, bias, w_up, w_tail, w_down, cots):
    rows, width = second.shape
    part = w_down.shape[0]
    bulk, left = w_up.shape[0], w_tail.shape[0]
    group = CHIPS * rows
    low, full = jnp.bfloat16, jnp.float32
    vmem = pl.BlockSpec(memory_space=pltpu.VMEM)
    dma = pltpu.SemaphoreType.DMA
    return pl.pallas_call(
        middle_kernel,
        out_shape=[
            jax.ShapeDtypeStruct((rows, width), full),
            jax.ShapeDtypeStruct((rows, width), full),
            jax.ShapeDtypeStruct((bulk, part), low),
            jax.ShapeDtypeStruct((left, CHIPS * part), low),
            jax.ShapeDtypeStruct((part, width), low),
            jax.ShapeDtypeStruct((1, part), full),
        ],
        in_specs=[vmem] * 3 + [pl.BlockSpec(memory_space=pl.ANY)] * 4,
        out_specs=[vmem] * 6,
        scratch_shapes=[
            pltpu.VMEM((bulk, part), low),
            pltpu.VMEM((left, part), low),
            pltpu.VMEM((part, width), low),
            pltpu.VMEM((group, width), low),
            pltpu.VMEM((CHIPS, rows, width), low),
            pltpu.VMEM((group, part), full),
            pltpu.VMEM((group, part), low),
            pltpu.VMEM((group, width), low),
            pltpu.VMEM((group, part), low),
            pltpu.VMEM((CHIPS, rows, width), low),
            pltpu.VMEM((CHIPS, rows, width), low),
            pltpu.VMEM((CHIPS, rows, width), low),
            pltpu.VMEM((CHIPS, rows, width), low),
            dma((4,)),
        ]
        + [dma((CHIPS,))] * 6,
        compiler_params=pltpu.CompilerParams(
            collective_id=2, has_side_effects=True, vmem_limit_bytes=50 * 2**20
        ),
        name="middle",
    )(second, onehot, bias, w_up, w_tail, w_down, cots)


def two_parts(value):
    high = lax.reduce_precision(value, 8, 7)
    return jnp.concatenate([lower(high), lower(value - high)], axis=0)


def body_group(block_input, out_cotangent, seq_lengths, w_qkv, w_out, w_up, w_down, vectors):
    rows, width = block_input.shape
    hidden = 4 * width
    scale = HEAD_DIM ** (-0.5)
    total = lax.axis_size("dp")
    depth = total // GROUP
    own = width // total
    main = own // (2 * ROWS) * (2 * ROWS)
    tail = own - main
    step = hidden // total
    wide_step = ceil_to(step, ROWS)
    part = total // CHIPS * wide_step
    count = vectors.shape[0]
    me = lax.axis_index("dp")
    layer = me // GROUP
    chip = (me // 2) % CHIPS
    core = me % 2
    mask = causal_mask(seq_lengths[0], rows)

    side = jnp.concatenate([w_qkv.reshape(own, 3 * width), w_out.reshape(own, width)], axis=1)
    upper_own = jnp.pad(
        w_up.reshape(own, depth, CHIPS, 2, step), ((0, 0),) * 4 + ((0, wide_step - step),)
    )
    upper_own = upper_own.transpose(2, 0, 1, 3, 4).reshape(CHIPS, own, part)
    down_own = jnp.pad(w_down.reshape(step, width), ((0, wide_step - step), (0, 0)))
    side_rows = tail * hidden // LANES
    up_rows = tail * CHIPS * part // LANES
    vec_rows = ceil_to(count, LANES) // LANES
    used = side_rows + up_rows + vec_rows
    tail_rows = ceil_to(used, ROWS)
    extra = jnp.concatenate(
        [
            side[main:].reshape(side_rows, LANES),
            upper_own[:, main:].reshape(up_rows, LANES),
            jnp.pad(vectors, (0, vec_rows * LANES - count)).reshape(vec_rows, LANES),
            jnp.zeros((tail_rows - used, LANES), jnp.bfloat16),
        ],
        axis=0,
    )
    s_all, t_all, u_all, d_all, c_all = gather_all(
        side[:main], extra, upper_own[:, :main], down_own, out_cotangent, depth
    )
    bulk = total * main
    w_side = s_all.reshape(bulk, hidden)
    w_upper = u_all.reshape(bulk, part)
    w_lower = d_all.reshape(part, width)
    cots = c_all.reshape(CHIPS * rows, width)
    t_all = t_all.reshape(total, tail_rows, LANES)
    side_tail = t_all[:, :side_rows].reshape(total * tail, hidden)
    up_each = up_rows // CHIPS
    up_tail = lax.dynamic_slice_in_dim(t_all, side_rows + chip * up_each, up_each, 1)
    up_tail = up_tail.reshape(total * tail, part)
    vec = t_all[:, side_rows + up_rows : used].reshape(total, vec_rows * LANES)[:, :count]
    vec = wide(vec.reshape(-1))
    bias_up = vec[7 * width : 7 * width + hidden].reshape(depth, CHIPS, 2, step)
    bias_up = lax.dynamic_index_in_dim(bias_up, chip, 1, keepdims=False)
    bias_up = jnp.pad(bias_up, ((0, 0), (0, 0), (0, wide_step - step))).reshape(1, part)

    place = jnp.arange(width, dtype=jnp.int32)
    slot = place // main
    there = (layer + slot % depth) % depth * GROUP
    there = there + jnp.bitwise_xor(chip, slot // depth % CHIPS) * 2
    there = there + jnp.bitwise_xor(core, slot // (depth * CHIPS))
    late = place - bulk
    origin = jnp.where(
        place < bulk, there * own + place % main, late // tail * own + main + late % tail
    )
    onehot = lower(place[:, None] == origin[None, :])

    def permute(value):
        return lower(multiply(value, onehot))

    def restore(value):
        return lower(contract_columns(value, onehot))

    def restore_wide(value):
        both = contract_columns(two_parts(value), onehot)
        return both[:rows] + both[rows:]

    wq, wo = w_side[:, : 3 * width], w_side[:, 3 * width :]
    wq_tail, wo_tail = side_tail[:, : 3 * width], side_tail[:, 3 * width :]

    inputs = wide(block_input)
    normed1, inverse1, pre1 = layer_norm(inputs, vec[0:width], vec[width : 2 * width])
    first = permute(lower(pre1))
    qkv = multiply(first[:, :bulk], wq) + multiply(first[:, bulk:], wq_tail)
    query = lower((qkv[:, 0:width] + vec[2 * width : 3 * width]) * scale)
    query = query.reshape(rows, HEADS, HEAD_DIM)
    keys = lower(qkv[:, width : 2 * width]).reshape(rows, HEADS, HEAD_DIM)
    values = lower(qkv[:, 2 * width : 3 * width] + vec[3 * width : 4 * width])
    values = values.reshape(rows, HEADS, HEAD_DIM)
    scores = score_block(query, keys, mask)
    peak = jnp.max(scores, axis=2, keepdims=True)
    logsum = peak + jnp.log(jnp.sum(jnp.exp(scores - peak), axis=2, keepdims=True))
    probs_low = lower(jnp.exp(scores - logsum))
    mixed = jnp.einsum("hqk,khe->qhe", probs_low, values, preferred_element_type=jnp.float32)
    mixed = permute(lower(mixed).reshape(rows, width))
    resid = inputs + multiply(mixed[:, :bulk], wo) + multiply(mixed[:, bulk:], wo_tail)
    resid = resid + vec[4 * width : 5 * width]
    gain2 = vec[5 * width : 6 * width]
    normed2, inverse2, pre2 = layer_norm(resid, gain2, vec[6 * width : 7 * width])
    second = lower(pre2)
    d_second, lifted, g_up, g_up_tail, g_down, d_bias_up = middle(
        second, onehot, bias_up, w_upper, up_tail, w_lower, cots
    )
    block_output = lower(resid + lifted + vec[7 * width + hidden :])
    g_down = g_down.reshape(depth, 2, wide_step, width)
    turn = jnp.arange(CHIPS, dtype=jnp.int32)

    grad_top = wide(out_cotangent)
    d_resid = grad_top + norm_back(d_second, normed2, inverse2, gain2)
    d_resid_low = lower(d_resid)
    g_out_tail = contract_rows(mixed[:, bulk:], d_resid_low)
    d_mixed = jnp.concatenate(
        [contract_columns(d_resid_low, wo), contract_columns(d_resid_low, wo_tail)], axis=1
    )
    d_mixed = restore(lower(d_mixed)).reshape(rows, HEADS, HEAD_DIM)
    probs = jnp.exp(score_block(query, keys, mask) - logsum)
    probs_low = lower(probs)
    d_values = jnp.einsum("hqk,qhe->khe", probs_low, d_mixed, preferred_element_type=jnp.float32)
    d_probs = jnp.einsum("qhe,khe->hqk", d_mixed, values, preferred_element_type=jnp.float32)
    delta = jnp.sum(probs * d_probs, axis=2, keepdims=True)
    d_scores = lower(probs * (d_probs - delta))
    d_query = jnp.einsum("hqk,khe->qhe", d_scores, keys, preferred_element_type=jnp.float32)
    d_query = d_query.reshape(rows, width) * scale
    d_keys = jnp.einsum("hqk,qhe->khe", d_scores, query, preferred_element_type=jnp.float32)
    d_keys = d_keys.reshape(rows, width)
    d_values = d_values.reshape(rows, width)
    d_qkv = lower(jnp.concatenate([d_query, d_keys, d_values], axis=1))
    g_qkv_tail = contract_rows(first[:, bulk:], d_qkv)
    d_first = jnp.concatenate(
        [contract_columns(d_qkv, wq), contract_columns(d_qkv, wq_tail)], axis=1
    )
    d_first = restore_wide(d_first)
    input_grad = d_resid + norm_back(d_first, normed1, inverse1, vec[0:width])

    d_bias_up = d_bias_up.reshape(depth, 1, 2, wide_step)[..., :step]
    d_bias_up = jnp.where(turn[None, :, None, None] == chip, d_bias_up, 0.0)
    g_vec = jnp.concatenate(
        [
            jnp.sum(d_first * normed1, axis=0),
            jnp.sum(d_first, axis=0),
            jnp.sum(d_query, axis=0),
            jnp.sum(d_values, axis=0),
            jnp.sum(d_resid, axis=0),
            jnp.sum(d_second * normed2, axis=0),
            jnp.sum(d_second, axis=0),
            d_bias_up.reshape(hidden),
            jnp.sum(grad_top, axis=0),
        ]
    )
    g_tails = jnp.concatenate([lower(g_qkv_tail), lower(g_out_tail), g_up_tail], axis=1)
    g_tails = lax.optimization_barrier(g_tails)
    g_tails = g_tails.reshape(total, side_rows + up_rows, LANES)
    g_vec = jnp.pad(lower(g_vec).reshape(total, count), ((0, 0), (0, vec_rows * LANES - count)))
    g_extra = jnp.concatenate(
        [
            g_tails,
            g_vec.reshape(total, vec_rows, LANES),
            jnp.zeros((total, tail_rows - used, LANES), jnp.bfloat16),
        ],
        axis=1,
    )
    g_extra = lax.optimization_barrier(g_extra)
    g_qkv, g_out, g_extra, g_up, g_down = scatter_sums(
        first,
        d_qkv,
        mixed,
        d_resid_low,
        g_extra,
        g_up,
        g_down,
        depth,
        main,
    )
    g_tails = g_extra[: side_rows + up_rows].reshape(tail, hidden + CHIPS * part)
    g_side_tail = g_tails[:, :hidden]
    g_up_tail = g_tails[:, hidden:].reshape(tail, CHIPS, part).transpose(1, 0, 2)
    grad_vectors = g_extra[side_rows + up_rows : used].reshape(-1)[:count]
    grad_qkv = jnp.concatenate([g_qkv, g_side_tail[:, : 3 * width]], axis=0).reshape(-1)
    grad_out = jnp.concatenate([g_out, g_side_tail[:, 3 * width :]], axis=0).reshape(-1)
    grad_up = jnp.concatenate([g_up, g_up_tail], axis=1)
    grad_up = grad_up.reshape(CHIPS, own, depth, 2, wide_step)[..., :step]
    grad_up = grad_up.transpose(1, 2, 0, 3, 4).reshape(-1)
    grad_down = g_down[:step].reshape(-1)
    return (block_output, input_grad, grad_qkv, grad_out, grad_up, grad_down, grad_vectors)


def solution(mesh):
    in_specs = (
        P("dp", None),
        P("dp", None),
        P("dp", None),
        P("dp"),
        P("dp"),
        P("dp"),
        P("dp"),
        P("dp"),
    )
    out_specs = (P("dp", None), P("dp", None), P("dp"), P("dp"), P("dp"), P("dp"), P("dp"))
    total = mesh.shape["dp"]

    def body(*blocks):
        width = blocks[0].shape[1]
        own = width // total
        small = own % (2 * ROWS) * 4 * width
        tidy = total % (2 * GROUP) == 0 and width % total == 0 and own >= 2 * ROWS
        if tidy and small > 0 and small % LANES == 0:
            return body_group(*blocks)
        return body_flat(*blocks)

    return jax.shard_map(body, mesh=mesh, in_specs=in_specs, out_specs=out_specs, check_vma=False)
```

```python
import functools

import jax
import jax.numpy as jnp
from jax import lax
from jax.experimental import pallas as pl
from jax.experimental.pallas import tpu as pltpu
from jax.sharding import PartitionSpec as P

HEADS = 17
HEAD_DIM = 64


EPS = 1e-05
ROOT_HALF = 0.7071067811865476
INV_ROOT_TAU = 0.3989422804014327


def layer_norm(rows, gain, shift):
    mean = jnp.mean(rows, axis=1, keepdims=True)
    centered = rows - mean
    inverse = lax.rsqrt(jnp.mean(centered * centered, axis=1, keepdims=True) + EPS)
    normed = centered * inverse
    return (normed, inverse, normed * gain + shift)


def norm_back(grad_rows, normed, inverse, gain):
    scaled = grad_rows * gain
    inner = jnp.mean(scaled * normed, axis=1, keepdims=True)
    return inverse * (scaled - jnp.mean(scaled, axis=1, keepdims=True) - normed * inner)


def gelu_exact(value):
    return 0.5 * value * (1.0 + lax.erf(value * ROOT_HALF))


def gelu_slope(value):
    return (
        0.5 * (1.0 + lax.erf(value * ROOT_HALF))
        + value * jnp.exp(-0.5 * value * value) * INV_ROOT_TAU
    )


def causal_mask(lengths, rows):
    count = lengths.shape[0]
    order = jnp.arange(count, dtype=jnp.int32)
    ends = jnp.sum(jnp.where(order[:, None] <= order[None, :], lengths[:, None], 0), axis=0)
    position = jnp.arange(rows, dtype=jnp.int32)
    segment = jnp.sum((position[:, None] >= ends[None, :]).astype(jnp.int32), axis=1)
    return (segment[:, None] == segment[None, :]) & (position[None, :] <= position[:, None])


def score_block(query, keys, mask):
    scores = jnp.einsum("qhe,khe->hqk", query, keys, preferred_element_type=jnp.float32)
    return jnp.where(mask[None], scores, -1e30)


def shape_params(flat_parts, width):
    hidden = 4 * width
    return (
        flat_parts[0].reshape(width, 3 * width),
        flat_parts[1].reshape(width, width),
        flat_parts[2].reshape(width, hidden),
        flat_parts[3].reshape(hidden, width),
        flat_parts[4].astype(jnp.float32),
    )


def window_term(left_rows, right_rows, flat_start, flat_count):
    inner_len = left_rows.shape[1]
    columns = right_rows.shape[1]
    row_count = min(inner_len, flat_count // columns + 2)
    row_first = jnp.clip(flat_start // columns, 0, inner_len - row_count)
    product = lax.dot_general(
        left_rows, right_rows, (((0,), (0,)), ((), ())), preferred_element_type=jnp.float32
    ).reshape(-1)
    padded = jnp.concatenate([product, jnp.zeros((flat_count,), jnp.float32)])
    return lax.dynamic_slice_in_dim(padded, flat_start - row_first * columns, flat_count, 0)


def shard_terms(pairs, vector_grad, device_total):
    piece_lens = [
        left_rows.shape[1] * right_rows.shape[1] // device_total for left_rows, right_rows in pairs
    ]
    piece_lens = piece_lens + [vector_grad.shape[0] // device_total]
    shard_len = sum(piece_lens)

    def shard_term(start, count):
        dev_count = count // shard_len
        dev_first = start // shard_len
        pieces = []
        for (left_rows, right_rows), piece_len in zip(pairs, piece_lens):
            window = window_term(
                left_rows, right_rows, dev_first * piece_len, dev_count * piece_len
            )
            pieces.append(window.reshape(dev_count, piece_len))
        vec_len = piece_lens[-1]
        window = vector_grad
        pieces.append(window.reshape(dev_count, vec_len))
        return jnp.concatenate(pieces, axis=1).reshape(-1)

    return (shard_term, shard_len, piece_lens)


def split_shard(summed, piece_lens):
    outputs = []
    offset = 0
    for piece_len in piece_lens:
        outputs.append(summed[offset : offset + piece_len])
        offset = offset + piece_len
    return outputs


def fetch_flat(w_qkv, w_out, w_up, w_down, vectors, width):
    fetched = tuple(
        lax.all_gather(part, "dp", axis=0, tiled=True)
        for part in (w_qkv, w_out, w_up, w_down, vectors)
    )
    return shape_params(fetched, width)


def reduce_flat(pairs, g_vec, device_total):
    all_term, all_len, all_lens = shard_terms(pairs, g_vec, device_total)
    return split_shard(
        lax.psum_scatter(
            all_term(jnp.int32(0), all_len * device_total),
            "dp",
            scatter_dimension=0,
            tiled=True,
        ),
        all_lens,
    )


def body_flat(block_input, out_cotangent, seq_lengths, w_qkv, w_out, w_up, w_down, vectors):
    rows, width = block_input.shape
    hidden = 4 * width
    scale = HEAD_DIM ** (-0.5)
    device_total = lax.axis_size("dp")
    mask = causal_mask(seq_lengths[0], rows)
    wqkv, wo, wup, wdn, vec = fetch_flat(w_qkv, w_out, w_up, w_down, vectors, width)
    inputs = block_input.astype(jnp.float32)
    normed1, inverse1, pre1 = layer_norm(inputs, vec[0:width], vec[width : 2 * width])
    first = pre1.astype(jnp.bfloat16)
    qkv = jnp.dot(first, wqkv, preferred_element_type=jnp.float32)
    query = (
        ((qkv[:, 0:width] + vec[2 * width : 3 * width]) * scale)
        .astype(jnp.bfloat16)
        .reshape(rows, HEADS, HEAD_DIM)
    )
    keys = qkv[:, width : 2 * width].astype(jnp.bfloat16).reshape(rows, HEADS, HEAD_DIM)
    values = (
        (qkv[:, 2 * width : 3 * width] + vec[3 * width : 4 * width])
        .astype(jnp.bfloat16)
        .reshape(rows, HEADS, HEAD_DIM)
    )
    scores = score_block(query, keys, mask)
    peak = jnp.max(scores, axis=2, keepdims=True)
    logsum = peak + jnp.log(jnp.sum(jnp.exp(scores - peak), axis=2, keepdims=True))
    probs_low = jnp.exp(scores - logsum).astype(jnp.bfloat16)
    mixed = jnp.einsum("hqk,khe->qhe", probs_low, values, preferred_element_type=jnp.float32)
    mixed = mixed.astype(jnp.bfloat16).reshape(rows, width)
    resid = (
        inputs + jnp.dot(mixed, wo, preferred_element_type=jnp.float32) + vec[4 * width : 5 * width]
    )
    normed2, inverse2, pre2 = layer_norm(
        resid, vec[5 * width : 6 * width], vec[6 * width : 7 * width]
    )
    second = pre2.astype(jnp.bfloat16)
    upper = (
        jnp.dot(second, wup, preferred_element_type=jnp.float32)
        + vec[7 * width : 7 * width + hidden]
    )
    active = gelu_exact(upper).astype(jnp.bfloat16)
    output = (
        resid + jnp.dot(active, wdn, preferred_element_type=jnp.float32) + vec[7 * width + hidden :]
    )
    block_output = output.astype(jnp.bfloat16)
    back_w = (wqkv, wo, wup, wdn)
    bqkv, bwo, bwup, bwdn = back_w
    grad_top = out_cotangent.astype(jnp.float32)
    d_upper = jnp.dot(out_cotangent, bwdn.T, preferred_element_type=jnp.float32) * gelu_slope(upper)
    d_upper_low = d_upper.astype(jnp.bfloat16)
    d_second = jnp.dot(d_upper_low, bwup.T, preferred_element_type=jnp.float32)
    d_resid = grad_top + norm_back(d_second, normed2, inverse2, vec[5 * width : 6 * width])
    d_resid_low = d_resid.astype(jnp.bfloat16)
    d_mixed = jnp.dot(d_resid_low, bwo.T, preferred_element_type=jnp.float32).astype(jnp.bfloat16)
    d_mixed = d_mixed.reshape(rows, HEADS, HEAD_DIM)
    probs = jnp.exp(score_block(query, keys, mask) - logsum)
    probs_low = probs.astype(jnp.bfloat16)
    d_values = jnp.einsum("hqk,qhe->khe", probs_low, d_mixed, preferred_element_type=jnp.float32)
    d_probs = jnp.einsum("qhe,khe->hqk", d_mixed, values, preferred_element_type=jnp.float32)
    delta = jnp.sum(probs * d_probs, axis=2, keepdims=True)
    d_scores = (probs * (d_probs - delta)).astype(jnp.bfloat16)
    d_query = (
        jnp.einsum("hqk,khe->qhe", d_scores, keys, preferred_element_type=jnp.float32).reshape(
            rows, width
        )
        * scale
    )
    d_keys = jnp.einsum(
        "hqk,qhe->khe", d_scores, query, preferred_element_type=jnp.float32
    ).reshape(rows, width)
    d_values = d_values.reshape(rows, width)
    d_qkv = jnp.concatenate([d_query, d_keys, d_values], axis=1).astype(jnp.bfloat16)
    d_first = jnp.dot(d_qkv, bqkv.T, preferred_element_type=jnp.float32)
    input_grad = d_resid + norm_back(d_first, normed1, inverse1, vec[0:width])
    g_vec = jnp.concatenate(
        [
            jnp.sum(d_first * normed1, axis=0),
            jnp.sum(d_first, axis=0),
            jnp.sum(d_query, axis=0),
            jnp.sum(d_values, axis=0),
            jnp.sum(d_resid, axis=0),
            jnp.sum(d_second * normed2, axis=0),
            jnp.sum(d_second, axis=0),
            jnp.sum(d_upper, axis=0),
            jnp.sum(grad_top, axis=0),
        ]
    )
    pairs = [(first, d_qkv), (mixed, d_resid_low), (second, d_upper_low), (active, out_cotangent)]
    grad_qkv, grad_out, grad_up, grad_down, grad_vectors = reduce_flat(pairs, g_vec, device_total)
    return (block_output, input_grad, grad_qkv, grad_out, grad_up, grad_down, grad_vectors)


GROUP = 8
CHIPS = 4
ROWS = 16
LANES = 128
MESH = pl.DeviceIdType.MESH


def ceil_to(count, unit):
    return -(-count // unit) * unit


def gather_kernel(
    depth, s_in, t_in, u_in, d_in, c_in, s_all, t_all, u_all, d_all, c_all, *sems
):
    (
        local,
        z_send,
        z_recv,
        s_send,
        s_recv,
        half_send,
        half_recv,
        core_send,
        core_recv,
        t_send,
        t_recv,
        u_send,
        u_recv,
        c_send,
        c_recv,
    ) = sems
    me = lax.axis_index("dp")
    layer = me // GROUP
    chip = (me % GROUP) // 2
    core = me % 2
    east = chip % 2
    north = chip // 2
    chip_at = (
        chip,
        north * 2 + (1 - east),
        (1 - north) * 2 + east,
        (1 - north) * 2 + (1 - east),
    )
    mates = tuple(layer * GROUP + at * 2 + core for at in chip_at)
    twin = layer * GROUP + chip * 2 + (1 - core)
    above = me + GROUP
    below = me - GROUP
    has_above = layer < depth - 1
    has_below = layer > 0

    barrier = pltpu.get_barrier_semaphore()
    for device in mates[1:] + (twin,):
        pl.semaphore_signal(barrier, inc=1, device_id=(device,), device_id_type=MESH)

    @pl.when(has_above)
    def _():
        pl.semaphore_signal(barrier, inc=1, device_id=(above,), device_id_type=MESH)

    @pl.when(has_below)
    def _():
        pl.semaphore_signal(barrier, inc=1, device_id=(below,), device_id_type=MESH)

    ends = (layer + depth - 1) // depth + (2 * depth - 2 - layer) // depth
    pl.semaphore_wait(barrier, CHIPS + ends)

    def send(source, target, send_sem, recv_sem, device):
        return pltpu.make_async_remote_copy(
            src_ref=source,
            dst_ref=target,
            send_sem=send_sem,
            recv_sem=recv_sem,
            device_id=(device,),
            device_id_type=MESH,
        )

    def layer_of(slot):
        return lax.rem(layer + slot, depth)

    def s_at(slot):
        return s_in if slot == 0 else s_all.at[0, 0, slot]

    def t_at(slot):
        return t_in if slot == 0 else t_all.at[layer_of(slot), chip, core]

    def d_at(slot):
        return d_in if slot == 0 else d_all.at[layer_of(slot), core]

    def u_at(slot):
        return u_all.at[0, :, slot]

    def s_to(slot, source):
        return s_all.at[0, 0, slot]

    def t_to(slot, source):
        return t_all.at[layer_of(source), chip, core]

    def d_to(slot, source):
        return d_all.at[layer_of(source), core]

    def u_to(slot, source):
        return u_all.at[0, :, slot]

    places = {"t": (0, t_at, t_to), "s": (1, s_at, s_to), "d": (2, d_at, d_to), "u": (3, u_at, u_to)}

    def z_copy(name, slot, up):
        index, source, target = places[name]
        there = (slot - 1) % depth if up else (slot + 1) % depth
        return send(
            source(slot),
            target(there, slot),
            z_send.at[index, slot, 0 if up else 1],
            z_recv.at[index, there],
            above if up else below,
        )

    def z_arrival(name, slot):
        index, source, target = places[name]
        here = target(slot, slot)
        return send(here, here, z_send.at[index, slot, 0], z_recv.at[index, slot], above)

    def routes():
        found = [(0, True, has_above), (0, False, has_below)]
        for far in range(1, depth - 1):
            found.append((depth - far, True, (layer >= far) & has_above))
            found.append((far, False, (layer + far < depth) & has_below))
        return found

    def z_forward(name, step):
        for slot, up, allowed in routes()[2 * step : 2 * step + 2]:

            @pl.when(allowed)
            def _(slot=slot, up=up):
                z_copy(name, slot, up).start()

    def z_land(name, far, then=None):
        for slot, came in ((depth - far, layer >= far), (far, layer + far < depth)):

            @pl.when(came)
            def _(slot=slot):
                z_arrival(name, slot).wait_recv()
                if then is not None:
                    then(slot)

    def s_plane(slot, way):
        return send(
            s_at(slot), s_all.at[0, way, slot], s_send.at[way, slot], s_recv.at[way, slot], mates[way]
        )

    def s_half(slot, way):
        rows = s_in.shape[0] // 2
        part = pl.ds(0 if way == 1 else rows, rows)
        return send(
            s_all.at[0, way, slot, part],
            s_all.at[0, 3, slot, part],
            half_send.at[way, slot],
            half_recv.at[way, slot],
            mates[3 - way],
        )

    def s_core(slot, way):
        source = s_at(slot) if way == 0 else s_all.at[0, way, slot]
        return send(
            source, s_all.at[1, way, slot], core_send.at[way, slot], core_recv.at[way, slot], twin
        )

    def s_spread(slot):
        s_plane(slot, 1).start()
        s_plane(slot, 2).start()
        s_core(slot, 0).start()

    def s_pass(slot):
        for way in (1, 2):
            s_plane(slot, way).wait_recv()
            s_half(slot, way).start()
            s_core(slot, way).start()

    def s_close(slot):
        for way in (1, 2):
            s_half(slot, way).wait_recv()
        s_core(slot, 3).start()

    def by_distance(far, act):
        if far == 0:
            act(0)
            return
        for slot, came in ((depth - far, layer >= far), (far, layer + far < depth)):

            @pl.when(came)
            def _(slot=slot):
                act(slot)

    def d_core(slot):
        return send(
            d_at(slot), d_to(slot, slot), core_send.at[4, slot], core_recv.at[4, slot], twin
        )

    def u_core(slot):
        return send(
            u_at(slot), u_all.at[1, :, slot], core_send.at[5, slot], core_recv.at[5, slot], twin
        )

    def d_twin_arrival(slot):
        here = d_all.at[layer_of(slot), 1 - core]
        return send(here, here, core_send.at[4, slot], core_recv.at[4, slot], twin)

    t_mine = t_all.at[:, chip, core]

    def t_plane(way):
        return send(t_mine, t_mine, t_send.at[way], t_recv.at[way], mates[way])

    def t_plane_arrival(way):
        here = t_all.at[:, chip_at[way], core]
        return send(here, here, t_send.at[way], t_recv.at[way], mates[way])

    t_core_block = t_all.at[:, :, core]
    t_twin_block = t_all.at[:, :, 1 - core]
    t_core = send(t_core_block, t_core_block, t_send.at[0], t_recv.at[0], twin)
    t_core_arrival = send(t_twin_block, t_twin_block, t_send.at[0], t_recv.at[0], twin)

    def u_plane(way):
        return send(
            u_in.at[chip_at[way]], u_all.at[0, way, 0], u_send.at[way], u_recv.at[way], mates[way]
        )

    def c_plane(way):
        return send(c_in, c_all.at[way], c_send.at[way], c_recv.at[way], mates[way])

    stay = [
        pltpu.make_async_copy(t_in, t_all.at[layer, chip, core], local.at[0]),
        pltpu.make_async_copy(u_in.at[chip], u_all.at[0, 0, 0], local.at[1]),
        pltpu.make_async_copy(s_in, s_all.at[0, 0, 0], local.at[2]),
        pltpu.make_async_copy(d_in, d_all.at[layer, core], local.at[3]),
        pltpu.make_async_copy(c_in, c_all.at[0], local.at[4]),
    ]

    z_forward("t", 0)
    z_forward("s", 0)
    for copy in stay:
        copy.start()
    for way in (1, 2, 3):
        u_plane(way).start()
    s_spread(0)
    for far in range(1, depth):
        z_land("t", far)
        if far < depth - 1:
            z_forward("t", far)
        z_land("s", far)
        if far < depth - 1:
            z_forward("s", far)
        if far == 1:
            z_forward("d", 0)
        by_distance(far, s_spread)
        if far == depth - 1:
            stay[0].wait()
            for way in (1, 2, 3):
                t_plane(way).start()
        if far == min(2, depth - 1):
            for way in (1, 2, 3):
                u_plane(way).wait_recv()
            stay[1].wait()
            z_forward("u", 0)
            u_core(0).start()
            d_core(0).start()
        by_distance(far - 1, s_pass)
    for way in (1, 2, 3):
        c_plane(way).start()
    for far in range(1, depth):
        z_land("d", far)
        if far < depth - 1:
            z_forward("d", far)
        by_distance(far, lambda slot: d_core(slot).start())
        if far == 1:
            by_distance(depth - 1, s_pass)
            for way in (1, 2, 3):
                t_plane_arrival(way).wait_recv()
            t_core.start()
        z_land("u", far)
        if far < depth - 1:
            z_forward("u", far)
        by_distance(far, lambda slot: u_core(slot).start())
        if far == min(2, depth - 1):
            for near in range(depth):
                by_distance(near, s_close)
    for slot in range(depth):
        for way in range(CHIPS):
            s_core(slot, way).wait()
        u_core(slot).wait()
        d_core(slot).wait_send()
        d_twin_arrival(slot).wait_recv()
        for way in (1, 2):
            s_plane(slot, way).wait_send()
            s_half(slot, way).wait_send()
    for way in (1, 2, 3):
        u_plane(way).wait_send()
        t_plane(way).wait_send()
        c_plane(way).wait()
    t_core.wait_send()
    t_core_arrival.wait_recv()
    for copy in stay[2:]:
        copy.wait()
    for slot, up, allowed in routes():

        @pl.when(allowed)
        def _(slot=slot, up=up):
            for name in places:
                z_copy(name, slot, up).wait_send()


def gather_all(s_own, t_own, u_own, d_own, c_own, depth):
    low = jnp.bfloat16
    return pl.pallas_call(
        functools.partial(gather_kernel, depth),
        out_shape=[
            jax.ShapeDtypeStruct((2, CHIPS, depth) + s_own.shape, low),
            jax.ShapeDtypeStruct((depth, CHIPS, 2) + t_own.shape, low),
            jax.ShapeDtypeStruct((2, CHIPS, depth) + u_own.shape[1:], low),
            jax.ShapeDtypeStruct((depth, 2) + d_own.shape, low),
            jax.ShapeDtypeStruct((CHIPS,) + c_own.shape, low),
        ],
        in_specs=[pl.BlockSpec(memory_space=pl.ANY)] * 5,
        out_specs=[pl.BlockSpec(memory_space=pl.ANY)] * 5,
        scratch_shapes=[
            pltpu.SemaphoreType.DMA((5,)),
            pltpu.SemaphoreType.DMA((4, depth, 2)),
            pltpu.SemaphoreType.DMA((4, depth)),
            pltpu.SemaphoreType.DMA((3, depth)),
            pltpu.SemaphoreType.DMA((3, depth)),
            pltpu.SemaphoreType.DMA((3, depth)),
            pltpu.SemaphoreType.DMA((3, depth)),
            pltpu.SemaphoreType.DMA((6, depth)),
            pltpu.SemaphoreType.DMA((6, depth)),
            pltpu.SemaphoreType.DMA((4,)),
            pltpu.SemaphoreType.DMA((4,)),
            pltpu.SemaphoreType.DMA((4,)),
            pltpu.SemaphoreType.DMA((4,)),
            pltpu.SemaphoreType.DMA((4,)),
            pltpu.SemaphoreType.DMA((4,)),
        ],
        compiler_params=pltpu.CompilerParams(collective_id=0, has_side_effects=True),
        name="gather_params",
    )(s_own, t_own, u_own, d_own, c_own)


def add_blocks(count, pick, other):
    @pl.loop(0, count)
    def _(at):
        here, term = pick(at), other(at)
        here[...] = (here[...].astype(jnp.float32) + term[...].astype(jnp.float32)).astype(here.dtype)


def scatter_kernel(depth, *refs):
    ins, outs, refs = refs[:7], refs[7:12], refs[12:]
    (
        acc_q,
        out_q,
        rc_q,
        p1_q,
        p2_q,
        z_q,
        acc_o,
        out_o,
        rc_o,
        p1_o,
        p2_o,
        z_o,
        acc_u,
        rc_u,
        z_u,
        fin_u,
        out_u,
        in_u,
        acc_d,
        rc_d,
        z_d,
        acc_t,
        rc_t,
        p_t,
        fin_t,
        z_t,
        local,
        c_send,
        c_recv,
        p_send,
        p_recv,
        t_send,
        t_recv,
        z_send,
        z_recv,
        a_send,
        a_recv,
    ) = refs
    q_left, q_right, o_left, o_right, t_in, u_in, d_in = ins
    q_out, o_out, t_out, u_out, d_out = outs
    me = lax.axis_index("dp")
    layer = me // GROUP
    chip = (me % GROUP) // 2
    core = me % 2
    east = chip % 2
    north = chip // 2
    chip_at = (
        chip,
        north * 2 + (1 - east),
        (1 - north) * 2 + east,
        (1 - north) * 2 + (1 - east),
    )
    mates = tuple(layer * GROUP + at * 2 + core for at in chip_at)
    twin = layer * GROUP + chip * 2 + (1 - core)
    above = me + GROUP
    below = me - GROUP

    barrier = pltpu.get_barrier_semaphore()
    for device in mates[1:] + (twin,):
        pl.semaphore_signal(barrier, inc=1, device_id=(device,), device_id_type=MESH)

    @pl.when(layer < depth - 1)
    def _():
        pl.semaphore_signal(barrier, inc=1, device_id=(above,), device_id_type=MESH)

    @pl.when(layer > 0)
    def _():
        pl.semaphore_signal(barrier, inc=1, device_id=(below,), device_id_type=MESH)

    ends = (layer + depth - 1) // depth + (2 * depth - 2 - layer) // depth
    pl.semaphore_wait(barrier, CHIPS + ends)

    def send(source, target, send_sem, recv_sem, device):
        return pltpu.make_async_remote_copy(
            src_ref=source,
            dst_ref=target,
            send_sem=send_sem,
            recv_sem=recv_sem,
            device_id=(device,),
            device_id_type=MESH,
        )

    def layer_of(slot):
        return lax.rem(layer + slot, depth)

    bulk = ((0, out_q, acc_q, rc_q, p1_q, p2_q), (1, out_o, acc_o, rc_o, p1_o, p2_o))
    half = p1_q.shape[3]

    def products(left, right, place, other):
        across = place.shape[2] * place.shape[3]
        for at in range(CHIPS):
            first = (other * CHIPS + at) * across
            block = contract_rows(left[:, first : first + across], right[...])
            place[at // 2, at % 2] = lower(block).reshape(place.shape[2:])

    stay = [
        pltpu.make_async_copy(u_in.at[0], acc_u, local.at[0]),
        pltpu.make_async_copy(d_in.at[:, core], acc_d, local.at[1]),
        pltpu.make_async_copy(t_in.at[:, :, core], acc_t, local.at[2]),
    ]
    u_core = send(u_in.at[1], rc_u, c_send.at[2, 0], c_recv.at[2, 0], twin)
    d_core = send(d_in.at[:, 1 - core], rc_d, c_send.at[3, 0], c_recv.at[3, 0], twin)
    t_core = send(t_in.at[:, :, 1 - core], rc_t, c_send.at[4, 0], c_recv.at[4, 0], twin)

    def b_core(item, slot):
        index, whole, acc, rc, p1, p2 = item
        return send(
            whole.at[:, :, slot],
            rc.at[:, :, slot],
            c_send.at[index, slot],
            c_recv.at[index, slot],
            twin,
        )

    def b_first(item, slot, side):
        index, whole, acc, rc, p1, p2 = item
        if side == 0:
            source = acc.at[1, :, slot, pl.ds(0, half)]
        else:
            source = acc.at[:, 1, slot, pl.ds(half, half)]
        at = (index * 2 + side) * 2
        return send(
            source, p1.at[side, :, slot], p_send.at[at, slot], p_recv.at[at, slot], mates[2 - side]
        )

    def b_second(item, slot, side):
        index, whole, acc, rc, p1, p2 = item
        if side == 0:
            source = acc.at[0, 1, slot, pl.ds(0, half)]
        else:
            source = acc.at[1, 0, slot, pl.ds(half, half)]
        at = (index * 2 + side) * 2 + 1
        return send(
            source, p2.at[side, slot], p_send.at[at, slot], p_recv.at[at, slot], mates[1 + side]
        )

    def open_slot(slot):
        for item in bulk:
            index, whole, acc, rc, p1, p2 = item
            b_core(item, slot).wait_recv()
            add_blocks(
                CHIPS,
                lambda at, acc=acc: acc.at[at // 2, at % 2, slot],
                lambda at, rc=rc: rc.at[at // 2, at % 2, slot],
            )
            b_first(item, slot, 0).start()
            b_first(item, slot, 1).start()

    def middle_slot(slot):
        for item in bulk:
            index, whole, acc, rc, p1, p2 = item
            b_first(item, slot, 0).wait_recv()
            add_blocks(
                2,
                lambda at, acc=acc: acc.at[0, at, slot, pl.ds(0, half)],
                lambda at, p1=p1: p1.at[0, at, slot],
            )
            b_second(item, slot, 0).start()
            b_first(item, slot, 1).wait_recv()
            add_blocks(
                2,
                lambda at, acc=acc: acc.at[at, 0, slot, pl.ds(half, half)],
                lambda at, p1=p1: p1.at[1, at, slot],
            )
            b_second(item, slot, 1).start()

    def close_slot(slot):
        for item in bulk:
            index, whole, acc, rc, p1, p2 = item
            for side in (0, 1):
                b_second(item, slot, side).wait_recv()
                add_blocks(
                    1,
                    lambda at, acc=acc, side=side: acc.at[0, 0, slot, pl.ds(side * half, half)],
                    lambda at, p2=p2, side=side: p2.at[side, slot],
                )

    chains = (
        (0, lambda slot: acc_q.at[0, 0, slot], z_q, q_out),
        (1, lambda slot: acc_o.at[0, 0, slot], z_o, o_out),
        (2, lambda slot: acc_u.at[:, slot], z_u, fin_u),
        (3, lambda slot: acc_d.at[layer_of(slot)], z_d, d_out),
        (4, lambda slot: fin_t.at[layer_of(slot)], z_t, t_out),
    )

    def z_up(chain, step):
        index, block, landing, final = chain
        return send(
            block(depth - step),
            landing.at[0, step],
            z_send.at[index, 0, step],
            z_recv.at[index, 0, step],
            above,
        )

    def z_down(chain, step):
        index, block, landing, final = chain
        return send(
            block(step),
            landing.at[1, step],
            z_send.at[index, 1, step],
            z_recv.at[index, 1, step],
            below,
        )

    def z_start(chain, step):
        @pl.when(layer < step)
        def _():
            z_up(chain, step).start()

        @pl.when(layer >= depth - step)
        def _():
            z_down(chain, step).start()

    def z_take(chain, step):
        index, block, landing, final = chain
        last = step == depth - 1
        if last:
            final[...] = block(0)[...].astype(jnp.float32)
        targets = (depth - step - 1, (step + 1) % depth)
        came = (
            (layer >= 1) & (layer <= step),
            (layer <= depth - 2) & (layer >= depth - step - 1),
        )
        for way, make in enumerate((z_up, z_down)):

            @pl.when(came[way])
            def _(way=way, make=make):
                make(chain, step).wait_recv()
                here = final if last else block(targets[way])
                total = here[...].astype(jnp.float32) + landing[way, step].astype(jnp.float32)
                here[...] = total.astype(here.dtype)

    def z_next(chain, step):
        z_take(chain, step)
        if step < depth - 1:
            z_start(chain, step + 1)

    def t_plane(way):
        return send(
            acc_t.at[:, chip_at[way]], p_t.at[way], t_send.at[way], t_recv.at[way], mates[way]
        )

    def u_turn(way):
        return send(out_u.at[way], in_u.at[way], a_send.at[way], a_recv.at[way], mates[way])

    chain_q, chain_o, chain_u, chain_d, chain_t = chains
    order = []
    for far in range(1, depth):
        for slot in (depth - far, far):
            if slot not in order:
                order.append(slot)
    order.append(0)
    closed = []
    opened = []

    def advance():
        while len(opened) < depth - 1:
            step = len(opened) + 1
            if step not in closed or depth - step not in closed:
                return
            for chain in (chain_q, chain_o):
                if step > 1:
                    z_take(chain, step - 1)
                z_start(chain, step)
            opened.append(step)

    u_core.start()
    d_core.start()
    for copy in stay:
        copy.start()
    products(o_left, o_right, out_o, 1)
    u_core.wait_recv()
    stay[0].wait()
    add_blocks(
        CHIPS * depth,
        lambda at: acc_u.at[at // depth, at % depth],
        lambda at: rc_u.at[at // depth, at % depth],
    )
    z_start(chain_u, 1)
    d_core.wait_recv()
    stay[1].wait()
    add_blocks(depth, lambda at: acc_d.at[at], lambda at: rc_d.at[at])
    z_start(chain_d, 1)
    products(q_left, q_right, out_q, 1)
    for slot in order:
        for item in bulk:
            b_core(item, slot).start()
    t_core.start()
    products(o_left, o_right, acc_o, 0)
    products(q_left, q_right, acc_q, 0)
    open_slot(order[0])
    open_slot(order[1])
    t_core.wait_recv()
    stay[2].wait()
    add_blocks(
        CHIPS * depth,
        lambda at: acc_t.at[at // CHIPS, at % CHIPS],
        lambda at: rc_t.at[at // CHIPS, at % CHIPS],
    )
    for way in (1, 2, 3):
        t_plane(way).start()
    z_steps = [(chain, step) for step in range(1, depth) for chain in (chain_u, chain_d)]
    taken = 0
    for at in range(depth):
        if taken < len(z_steps):
            z_next(*z_steps[taken])
            taken = taken + 1
        middle_slot(order[at])
        if at + 2 < depth:
            open_slot(order[at + 2])
        if at >= 1:
            close_slot(order[at - 1])
            closed.append(order[at - 1])
            advance()
    for way in (1, 2, 3):
        t_plane(way).wait_recv()

    @pl.loop(0, depth)
    def _(at):
        total = acc_t[at, chip].astype(jnp.float32)
        for way in (1, 2, 3):
            total = total + p_t[way, at].astype(jnp.float32)
        fin_t[at] = total.astype(jnp.bfloat16)

    z_start(chain_t, 1)
    for chain, step in z_steps[taken:]:
        if chain is chain_u:
            z_next(chain, step)
    for way in (1, 2, 3):
        out_u[way] = fin_u[way].astype(jnp.bfloat16)
        u_turn(way).start()
    if depth > 2:
        z_next(chain_t, 1)
    close_slot(order[depth - 1])
    closed.append(order[depth - 1])
    advance()
    for step in range(2, depth - 1):
        z_next(chain_t, step)
    for chain, step in z_steps[taken:]:
        if chain is chain_d:
            z_next(chain, step)
    z_next(chain_t, depth - 1)
    for step in range(len(opened), depth):
        for chain in (chain_q, chain_o):
            z_next(chain, step)
    u_out[chip] = fin_u[0]
    for way in (1, 2, 3):
        u_turn(way).wait_recv()
        u_out[chip_at[way]] = in_u[way].astype(jnp.float32)

    for copy in (u_core, d_core, t_core):
        copy.wait_send()
    for slot in range(depth):
        for item in bulk:
            b_core(item, slot).wait_send()
            for side in (0, 1):
                b_first(item, slot, side).wait_send()
                b_second(item, slot, side).wait_send()
    for way in (1, 2, 3):
        t_plane(way).wait_send()
        u_turn(way).wait_send()
    for step in range(1, depth):

        @pl.when(layer < step)
        def _(step=step):
            for chain in chains:
                z_up(chain, step).wait_send()

        @pl.when(layer >= depth - step)
        def _(step=step):
            for chain in chains:
                z_down(chain, step).wait_send()


def scatter_sums(q_left, q_right, o_left, o_right, t_part, u_part, d_part, depth, main):
    low, full = jnp.bfloat16, jnp.float32
    half = main // 2

    def bulk_scratch(columns):
        return [
            pltpu.VMEM((2, 2, depth, main, columns), low),
            pltpu.VMEM((2, 2, depth, main, columns), low),
            pltpu.VMEM((2, 2, depth, main, columns), low),
            pltpu.VMEM((2, 2, depth, half, columns), low),
            pltpu.VMEM((2, depth, half, columns), low),
            pltpu.VMEM((2, depth, main, columns), low),
        ]

    q_columns, o_columns, u_columns = q_right.shape[1], o_right.shape[1], u_part.shape[1]
    down = d_part.shape[2:]
    small = t_part.shape[1:]
    dma = pltpu.SemaphoreType.DMA
    return pl.pallas_call(
        functools.partial(scatter_kernel, depth),
        out_shape=[
            jax.ShapeDtypeStruct((main, q_columns), full),
            jax.ShapeDtypeStruct((main, o_columns), full),
            jax.ShapeDtypeStruct(small, full),
            jax.ShapeDtypeStruct((CHIPS, main, u_columns), full),
            jax.ShapeDtypeStruct(down, full),
        ],
        in_specs=[pl.BlockSpec(memory_space=pltpu.VMEM)] * 4
        + [pl.BlockSpec(memory_space=pl.ANY)] * 3,
        out_specs=[pl.BlockSpec(memory_space=pltpu.VMEM)] * 5,
        scratch_shapes=bulk_scratch(q_columns)
        + bulk_scratch(o_columns)
        + [
            pltpu.VMEM((CHIPS, depth, main, u_columns), low),
            pltpu.VMEM((CHIPS, depth, main, u_columns), low),
            pltpu.VMEM((2, depth, CHIPS, main, u_columns), low),
            pltpu.VMEM((CHIPS, main, u_columns), full),
            pltpu.VMEM((CHIPS, main, u_columns), low),
            pltpu.VMEM((CHIPS, main, u_columns), low),
            pltpu.VMEM((depth,) + down, low),
            pltpu.VMEM((depth,) + down, low),
            pltpu.VMEM((2, depth) + down, low),
            pltpu.VMEM((depth, CHIPS) + small, low),
            pltpu.VMEM((depth, CHIPS) + small, low),
            pltpu.VMEM((CHIPS, depth) + small, low),
            pltpu.VMEM((depth,) + small, low),
            pltpu.VMEM((2, depth) + small, low),
            dma((3,)),
            dma((5, depth)),
            dma((5, depth)),
            dma((8, depth)),
            dma((8, depth)),
            dma((4,)),
            dma((4,)),
            dma((5, 2, depth)),
            dma((5, 2, depth)),
            dma((4,)),
            dma((4,)),
        ],
        compiler_params=pltpu.CompilerParams(
            collective_id=1, has_side_effects=True, vmem_limit_bytes=56 * 2**20
        ),
        name="scatter_sums",
    )(
        q_left,
        q_right,
        o_left,
        o_right,
        t_part.reshape((depth, CHIPS, 2) + small),
        u_part.reshape(2, CHIPS, depth, main, u_columns),
        d_part,
    )


def lower(value):
    return value.astype(jnp.bfloat16)


def wide(value):
    return value.astype(jnp.float32)


def contract_rows(left, right):
    return lax.dot_general(left, right, (((0,), (0,)), ((), ())), preferred_element_type=jnp.float32)


def contract_columns(left, right):
    return lax.dot_general(left, right, (((1,), (1,)), ((), ())), preferred_element_type=jnp.float32)


def multiply(left, right):
    return jnp.dot(left, right, preferred_element_type=jnp.float32)


def middle_kernel(*refs):
    second, onehot, bias, u_hbm, t_hbm, d_hbm, c_hbm = refs[:7]
    d_second, lifted, g_up, g_tail, g_down, g_bias = refs[7:13]
    (
        w_up,
        w_tail,
        w_down,
        cots,
        tokens,
        slopes,
        active,
        spread,
        steep,
        y_out,
        y_in,
        s_out,
        s_in,
        local,
        h_send,
        h_recv,
        y_send,
        y_recv,
        s_send,
        s_recv,
    ) = refs[13:]
    rows = second.shape[0]
    bulk = w_up.shape[0]
    me = lax.axis_index("dp")
    layer = me // GROUP
    chip = (me % GROUP) // 2
    core = me % 2
    east = chip % 2
    north = chip // 2
    chip_at = (
        chip,
        north * 2 + (1 - east),
        (1 - north) * 2 + east,
        (1 - north) * 2 + (1 - east),
    )
    mates = tuple(layer * GROUP + at * 2 + core for at in chip_at)
    barrier = pltpu.get_barrier_semaphore()
    for device in mates[1:]:
        pl.semaphore_signal(barrier, inc=1, device_id=(device,), device_id_type=MESH)
    loads = [
        pltpu.make_async_copy(d_hbm, w_down, local.at[0]),
        pltpu.make_async_copy(c_hbm, cots, local.at[1]),
        pltpu.make_async_copy(u_hbm, w_up, local.at[2]),
        pltpu.make_async_copy(t_hbm, w_tail, local.at[3]),
    ]
    for load in loads:
        load.start()
    pl.semaphore_wait(barrier, CHIPS - 1)

    def send(source, target, send_sem, recv_sem, way):
        return pltpu.make_async_remote_copy(
            src_ref=source,
            dst_ref=target,
            send_sem=send_sem.at[way],
            recv_sem=recv_sem.at[way],
            device_id=(mates[way],),
            device_id_type=MESH,
        )

    ways = (1, 2, 3)
    hidden = {way: send(second, tokens.at[way], h_send, h_recv, way) for way in ways}
    lifts = {way: send(y_out.at[way], y_in.at[way], y_send, y_recv, way) for way in ways}
    backs = {way: send(s_out.at[way], s_in.at[way], s_send, s_recv, way) for way in ways}
    for way in (1, 2, 3):
        hidden[way].start()
    tokens[0] = second[...]
    loads[0].wait()
    loads[1].wait()
    slopes[...] = contract_columns(cots[...], w_down[...])
    loads[2].wait()
    loads[3].wait()
    for way in range(CHIPS):
        if way > 0:
            hidden[way].wait_recv()
        span = pl.ds(way * rows, rows)
        mine = lower(multiply(tokens[way], onehot[...]))
        spread[span] = mine
        upper = multiply(mine[:, :bulk], w_up[...]) + multiply(mine[:, bulk:], w_tail[...])
        upper = upper + bias[...]
        phi = 0.5 * (1.0 + lax.erf(upper * ROOT_HALF))
        active[span] = lower(upper * phi)
        steep_rows = slopes[span] * (phi + upper * jnp.exp(-0.5 * upper * upper) * INV_ROOT_TAU)
        slopes[span] = steep_rows
        steep[span] = lower(steep_rows)
        back = jnp.concatenate(
            [contract_columns(steep[span], w_up[...]), contract_columns(steep[span], w_tail[...])],
            axis=1,
        )
        s_out[way] = lower(contract_columns(lower(back), onehot[...]))
        if way > 0:
            backs[way].start()
        y_out[way] = lower(multiply(active[span], w_down[...]))
        if way > 0:
            lifts[way].start()
    g_bias[...] = jnp.sum(slopes[...], axis=0, keepdims=True)
    g_up[...] = lower(contract_rows(spread[:, :bulk], steep[...]))
    part = steep.shape[1]
    g_tail[...] = jnp.zeros_like(g_tail)
    g_tail[:, pl.ds(pl.multiple_of(chip * part, LANES), part)] = lower(
        contract_rows(spread[:, bulk:], steep[...])
    )
    g_down[...] = lower(contract_rows(active[...], cots[...]))
    total = wide(s_out[0])
    for way in (1, 2, 3):
        backs[way].wait_recv()
        total = total + wide(s_in[way])
    d_second[...] = total
    total = wide(y_out[0])
    for way in (1, 2, 3):
        lifts[way].wait_recv()
        total = total + wide(y_in[way])
    lifted[...] = total
    for way in (1, 2, 3):
        hidden[way].wait_send()
        backs[way].wait_send()
        lifts[way].wait_send()


def middle(second, onehot, bias, w_up, w_tail, w_down, cots):
    rows, width = second.shape
    part = w_down.shape[0]
    bulk, left = w_up.shape[0], w_tail.shape[0]
    group = CHIPS * rows
    low, full = jnp.bfloat16, jnp.float32
    vmem = pl.BlockSpec(memory_space=pltpu.VMEM)
    dma = pltpu.SemaphoreType.DMA
    return pl.pallas_call(
        middle_kernel,
        out_shape=[
            jax.ShapeDtypeStruct((rows, width), full),
            jax.ShapeDtypeStruct((rows, width), full),
            jax.ShapeDtypeStruct((bulk, part), low),
            jax.ShapeDtypeStruct((left, CHIPS * part), low),
            jax.ShapeDtypeStruct((part, width), low),
            jax.ShapeDtypeStruct((1, part), full),
        ],
        in_specs=[vmem] * 3 + [pl.BlockSpec(memory_space=pl.ANY)] * 4,
        out_specs=[vmem] * 6,
        scratch_shapes=[
            pltpu.VMEM((bulk, part), low),
            pltpu.VMEM((left, part), low),
            pltpu.VMEM((part, width), low),
            pltpu.VMEM((group, width), low),
            pltpu.VMEM((CHIPS, rows, width), low),
            pltpu.VMEM((group, part), full),
            pltpu.VMEM((group, part), low),
            pltpu.VMEM((group, width), low),
            pltpu.VMEM((group, part), low),
            pltpu.VMEM((CHIPS, rows, width), low),
            pltpu.VMEM((CHIPS, rows, width), low),
            pltpu.VMEM((CHIPS, rows, width), low),
            pltpu.VMEM((CHIPS, rows, width), low),
            dma((4,)),
        ]
        + [dma((CHIPS,))] * 6,
        compiler_params=pltpu.CompilerParams(
            collective_id=2, has_side_effects=True, vmem_limit_bytes=50 * 2**20
        ),
        name="middle",
    )(second, onehot, bias, w_up, w_tail, w_down, cots)


def two_parts(value):
    high = lax.reduce_precision(value, 8, 7)
    return jnp.concatenate([lower(high), lower(value - high)], axis=0)


def body_group(block_input, out_cotangent, seq_lengths, w_qkv, w_out, w_up, w_down, vectors):
    rows, width = block_input.shape
    hidden = 4 * width
    scale = HEAD_DIM ** (-0.5)
    total = lax.axis_size("dp")
    depth = total // GROUP
    own = width // total
    main = own // (2 * ROWS) * (2 * ROWS)
    tail = own - main
    step = hidden // total
    wide_step = ceil_to(step, ROWS)
    part = total // CHIPS * wide_step
    count = vectors.shape[0]
    me = lax.axis_index("dp")
    layer = me // GROUP
    chip = (me // 2) % CHIPS
    core = me % 2
    mask = causal_mask(seq_lengths[0], rows)

    side = jnp.concatenate([w_qkv.reshape(own, 3 * width), w_out.reshape(own, width)], axis=1)
    upper_own = jnp.pad(
        w_up.reshape(own, depth, CHIPS, 2, step), ((0, 0),) * 4 + ((0, wide_step - step),)
    )
    upper_own = upper_own.transpose(2, 0, 1, 3, 4).reshape(CHIPS, own, part)
    down_own = jnp.pad(w_down.reshape(step, width), ((0, wide_step - step), (0, 0)))
    side_rows = tail * hidden // LANES
    up_rows = tail * CHIPS * part // LANES
    vec_rows = ceil_to(count, LANES) // LANES
    used = side_rows + up_rows + vec_rows
    tail_rows = ceil_to(used, ROWS)
    extra = jnp.concatenate(
        [
            side[main:].reshape(side_rows, LANES),
            upper_own[:, main:].reshape(up_rows, LANES),
            jnp.pad(vectors, (0, vec_rows * LANES - count)).reshape(vec_rows, LANES),
            jnp.zeros((tail_rows - used, LANES), jnp.bfloat16),
        ],
        axis=0,
    )
    s_all, t_all, u_all, d_all, c_all = gather_all(
        side[:main], extra, upper_own[:, :main], down_own, out_cotangent, depth
    )
    bulk = total * main
    w_side = s_all.reshape(bulk, hidden)
    w_upper = u_all.reshape(bulk, part)
    w_lower = d_all.reshape(part, width)
    cots = c_all.reshape(CHIPS * rows, width)
    t_all = t_all.reshape(total, tail_rows, LANES)
    side_tail = t_all[:, :side_rows].reshape(total * tail, hidden)
    up_each = up_rows // CHIPS
    up_tail = lax.dynamic_slice_in_dim(t_all, side_rows + chip * up_each, up_each, 1)
    up_tail = up_tail.reshape(total * tail, part)
    vec = t_all[:, side_rows + up_rows : used].reshape(total, vec_rows * LANES)[:, :count]
    vec = wide(vec.reshape(-1))
    bias_up = vec[7 * width : 7 * width + hidden].reshape(depth, CHIPS, 2, step)
    bias_up = lax.dynamic_index_in_dim(bias_up, chip, 1, keepdims=False)
    bias_up = jnp.pad(bias_up, ((0, 0), (0, 0), (0, wide_step - step))).reshape(1, part)

    place = jnp.arange(width, dtype=jnp.int32)
    slot = place // main
    there = (layer + slot % depth) % depth * GROUP
    there = there + jnp.bitwise_xor(chip, slot // depth % CHIPS) * 2
    there = there + jnp.bitwise_xor(core, slot // (depth * CHIPS))
    late = place - bulk
    origin = jnp.where(
        place < bulk, there * own + place % main, late // tail * own + main + late % tail
    )
    onehot = lower(place[:, None] == origin[None, :])

    def permute(value):
        return lower(multiply(value, onehot))

    def restore(value):
        return lower(contract_columns(value, onehot))

    def restore_wide(value):
        both = contract_columns(two_parts(value), onehot)
        return both[:rows] + both[rows:]

    wq, wo = w_side[:, : 3 * width], w_side[:, 3 * width :]
    wq_tail, wo_tail = side_tail[:, : 3 * width], side_tail[:, 3 * width :]

    inputs = wide(block_input)
    normed1, inverse1, pre1 = layer_norm(inputs, vec[0:width], vec[width : 2 * width])
    first = permute(lower(pre1))
    qkv = multiply(first[:, :bulk], wq) + multiply(first[:, bulk:], wq_tail)
    query = lower((qkv[:, 0:width] + vec[2 * width : 3 * width]) * scale)
    query = query.reshape(rows, HEADS, HEAD_DIM)
    keys = lower(qkv[:, width : 2 * width]).reshape(rows, HEADS, HEAD_DIM)
    values = lower(qkv[:, 2 * width : 3 * width] + vec[3 * width : 4 * width])
    values = values.reshape(rows, HEADS, HEAD_DIM)
    scores = score_block(query, keys, mask)
    peak = jnp.max(scores, axis=2, keepdims=True)
    logsum = peak + jnp.log(jnp.sum(jnp.exp(scores - peak), axis=2, keepdims=True))
    probs_low = lower(jnp.exp(scores - logsum))
    mixed = jnp.einsum("hqk,khe->qhe", probs_low, values, preferred_element_type=jnp.float32)
    mixed = permute(lower(mixed).reshape(rows, width))
    resid = inputs + multiply(mixed[:, :bulk], wo) + multiply(mixed[:, bulk:], wo_tail)
    resid = resid + vec[4 * width : 5 * width]
    gain2 = vec[5 * width : 6 * width]
    normed2, inverse2, pre2 = layer_norm(resid, gain2, vec[6 * width : 7 * width])
    second = lower(pre2)
    d_second, lifted, g_up, g_up_tail, g_down, d_bias_up = middle(
        second, onehot, bias_up, w_upper, up_tail, w_lower, cots
    )
    block_output = lower(resid + lifted + vec[7 * width + hidden :])
    g_down = g_down.reshape(depth, 2, wide_step, width)
    turn = jnp.arange(CHIPS, dtype=jnp.int32)

    grad_top = wide(out_cotangent)
    d_resid = grad_top + norm_back(d_second, normed2, inverse2, gain2)
    d_resid_low = lower(d_resid)
    g_out_tail = contract_rows(mixed[:, bulk:], d_resid_low)
    d_mixed = jnp.concatenate(
        [contract_columns(d_resid_low, wo), contract_columns(d_resid_low, wo_tail)], axis=1
    )
    d_mixed = restore(lower(d_mixed)).reshape(rows, HEADS, HEAD_DIM)
    probs = jnp.exp(score_block(query, keys, mask) - logsum)
    probs_low = lower(probs)
    d_values = jnp.einsum("hqk,qhe->khe", probs_low, d_mixed, preferred_element_type=jnp.float32)
    d_probs = jnp.einsum("qhe,khe->hqk", d_mixed, values, preferred_element_type=jnp.float32)
    delta = jnp.sum(probs * d_probs, axis=2, keepdims=True)
    d_scores = lower(probs * (d_probs - delta))
    d_query = jnp.einsum("hqk,khe->qhe", d_scores, keys, preferred_element_type=jnp.float32)
    d_query = d_query.reshape(rows, width) * scale
    d_keys = jnp.einsum("hqk,qhe->khe", d_scores, query, preferred_element_type=jnp.float32)
    d_keys = d_keys.reshape(rows, width)
    d_values = d_values.reshape(rows, width)
    d_qkv = lower(jnp.concatenate([d_query, d_keys, d_values], axis=1))
    g_qkv_tail = contract_rows(first[:, bulk:], d_qkv)
    d_first = jnp.concatenate(
        [contract_columns(d_qkv, wq), contract_columns(d_qkv, wq_tail)], axis=1
    )
    d_first = restore_wide(d_first)
    input_grad = d_resid + norm_back(d_first, normed1, inverse1, vec[0:width])

    d_bias_up = d_bias_up.reshape(depth, 1, 2, wide_step)[..., :step]
    d_bias_up = jnp.where(turn[None, :, None, None] == chip, d_bias_up, 0.0)
    g_vec = jnp.concatenate(
        [
            jnp.sum(d_first * normed1, axis=0),
            jnp.sum(d_first, axis=0),
            jnp.sum(d_query, axis=0),
            jnp.sum(d_values, axis=0),
            jnp.sum(d_resid, axis=0),
            jnp.sum(d_second * normed2, axis=0),
            jnp.sum(d_second, axis=0),
            d_bias_up.reshape(hidden),
            jnp.sum(grad_top, axis=0),
        ]
    )
    g_tails = jnp.concatenate([lower(g_qkv_tail), lower(g_out_tail), g_up_tail], axis=1)
    g_tails = lax.optimization_barrier(g_tails)
    g_tails = g_tails.reshape(total, side_rows + up_rows, LANES)
    g_vec = jnp.pad(lower(g_vec).reshape(total, count), ((0, 0), (0, vec_rows * LANES - count)))
    g_extra = jnp.concatenate(
        [
            g_tails,
            g_vec.reshape(total, vec_rows, LANES),
            jnp.zeros((total, tail_rows - used, LANES), jnp.bfloat16),
        ],
        axis=1,
    )
    g_extra = lax.optimization_barrier(g_extra)
    g_qkv, g_out, g_extra, g_up, g_down = scatter_sums(
        first,
        d_qkv,
        mixed,
        d_resid_low,
        g_extra,
        g_up,
        g_down,
        depth,
        main,
    )
    g_tails = g_extra[: side_rows + up_rows].reshape(tail, hidden + CHIPS * part)
    g_side_tail = g_tails[:, :hidden]
    g_up_tail = g_tails[:, hidden:].reshape(tail, CHIPS, part).transpose(1, 0, 2)
    grad_vectors = g_extra[side_rows + up_rows : used].reshape(-1)[:count]
    grad_qkv = jnp.concatenate([g_qkv, g_side_tail[:, : 3 * width]], axis=0).reshape(-1)
    grad_out = jnp.concatenate([g_out, g_side_tail[:, 3 * width :]], axis=0).reshape(-1)
    grad_up = jnp.concatenate([g_up, g_up_tail], axis=1)
    grad_up = grad_up.reshape(CHIPS, own, depth, 2, wide_step)[..., :step]
    grad_up = grad_up.transpose(1, 2, 0, 3, 4).reshape(-1)
    grad_down = g_down[:step].reshape(-1)
    return (block_output, input_grad, grad_qkv, grad_out, grad_up, grad_down, grad_vectors)


def solution(mesh):
    in_specs = (
        P("dp", None),
        P("dp", None),
        P("dp", None),
        P("dp"),
        P("dp"),
        P("dp"),
        P("dp"),
        P("dp"),
    )
    out_specs = (P("dp", None), P("dp", None), P("dp"), P("dp"), P("dp"), P("dp"), P("dp"))
    total = mesh.shape["dp"]

    def body(*blocks):
        width = blocks[0].shape[1]
        own = width // total
        small = own % (2 * ROWS) * 4 * width
        tidy = total % (2 * GROUP) == 0 and width % total == 0 and own >= 2 * ROWS
        if tidy and small > 0 and small % LANES == 0:
            return body_group(*blocks)
        return body_flat(*blocks)

    return jax.shard_map(body, mesh=mesh, in_specs=in_specs, out_specs=out_specs, check_vma=False)
```
